256 devices in a mesh: sx: 8 (over y, core), sy: 4 (over z_hi), row: 8 (over x, z_lo).
Axes of the slice: x: 4, y: 4, z: 8 (z_hi: 4, z_lo: 2; z = z_hi * 2 + z_lo), core: 2. Of those that a mesh axis runs over, the one named last changes fastest.
Arguments:
- thermal_state: float32 [256, 512, 512], P('row', 'sx', 'sy'), may hold values from -6 to 6
- substance_label: int32 [256, 512, 512], P('row', 'sx', 'sy'), may hold values from 0 to 2
- thermal_coefficients: float32 [3], replicated, may hold values from 0.04 to 0.16
- optical_thickness: float32 [3], replicated, may hold values from 1 to 6
- substance_colours: float32 [3, 3], replicated, may hold values from 0.1 to 1
Outputs:
- advanced_thermal_state: float32 [256, 512, 512], P('row', 'sx', 'sy')
- output_picture: float32 [4, 512, 512], P(None, ('sx', 'row'), 'sy')
The draws below stay inside these ranges and needn't reach their ends.
All inputs are finite; a program needn't handle non-finite values.
Results may differ from the reference program's by a relative error of at most 0.00002.
Values sent between devices are 32-bit elements; how exact they have to be, the bound alone decides.
A program may use at most 64 MiB of HBM per device.

```python
import math
import jax
import jax.numpy as jnp
from jax import lax

CELLS_WIDE = 512
CELLS_TALL = 512
CELLS_DEEP = 256


def plant(values, own_key, smallest, high):
    shape = values.shape
    spot = [jax.random.randint(jax.random.fold_in(own_key, axis), (), 0, shape[axis]) for axis in range(len(shape))]
    values = values.at[tuple(spot)].set(smallest)
    longest = shape.index(max(shape))
    spot[longest] = (spot[longest] + 1) % shape[longest]
    return values.at[tuple(spot)].set(high)


def level_of(stream_key, shape, pieces, least, largest):
    loudness = 1.0
    for dim, parts in pieces:
        steps = jax.random.uniform(jax.random.fold_in(jax.random.fold_in(stream_key, 6), dim), (parts,), jnp.float32, least / len(pieces), largest / len(pieces))
        loudness = loudness * jnp.repeat(jnp.exp(steps), shape[dim] // parts).reshape((-1,) + (1,) * (len(shape) - 1 - dim))
    return loudness


def scatter_about(rng, extent, scale, bound, pieces=(), dtype=jnp.bfloat16):
    loudness = level_of(rng, extent, pieces, -0.22, 0.18) if pieces else 1.0
    entries = jax.random.normal(rng, extent, jnp.float32) * scale * loudness
    return jnp.minimum(jnp.maximum(entries, -bound), bound).astype(dtype)


def setup_inputs(seed: int = 0) -> dict:
    keys = jax.random.split(jax.random.key(seed), 6)
    return {
        "thermal_state": scatter_about(keys[0], (CELLS_DEEP, CELLS_WIDE, CELLS_TALL), 1.0, 6.0, ((0, 8), (1, 8), (2, 4)), jnp.float32),
        "substance_label": plant(jax.random.randint(keys[1], (CELLS_DEEP, CELLS_WIDE, CELLS_TALL), 0, 3), jax.random.fold_in(keys[1], 1), 0, 2).astype(jnp.int32),
        "thermal_coefficients": jnp.clip(jnp.exp(jax.random.uniform(keys[2], (3,), jnp.float32, math.log(0.04), math.log(0.16))), 0.04, 0.16),
        "optical_thickness": jnp.clip(jnp.exp(jax.random.uniform(keys[3], (3,), jnp.float32, math.log(1.0), math.log(6.0))), 1.0, 6.0),
        "substance_colours": jnp.clip(jax.random.uniform(keys[4], (3, 3), jnp.float32, 0.1, 1.0), 0.1, 1.0),
    }


def spread_warmth(present_warmth, coupling_operator):
    summed = jnp.zeros_like(present_warmth)
    for axis_at in (0, 2):
        pad_width = [(0, 0), (0, 0), (0, 0)]
        pad_width[axis_at] = (1, 1)
        padded_heat = jnp.pad(present_warmth, pad_width)
        padded_conduct = jnp.pad(coupling_operator, pad_width)
        length = present_warmth.shape[axis_at]
        for start_at in (0, 2):
            neighbour = lax.slice_in_dim(padded_heat, start_at, start_at + length, axis=axis_at)
            neighbour_conduct = lax.slice_in_dim(padded_conduct, start_at, start_at + length, axis=axis_at)
            summed = summed + 0.5 * (coupling_operator + neighbour_conduct) * (neighbour - present_warmth)
    for offset_by in (1, -1):
        neighbour = jnp.roll(present_warmth, offset_by, axis=1)
        neighbour_conduct = jnp.roll(coupling_operator, offset_by, axis=1)
        summed = summed + 0.5 * (coupling_operator + neighbour_conduct) * (neighbour - present_warmth)
    return present_warmth + summed


def reference(thermal_state, substance_label, thermal_coefficients, optical_thickness, substance_colours):
    coupling_operator = thermal_coefficients[substance_label]
    warmed_plate = spread_warmth(thermal_state, coupling_operator)
    advanced_thermal_state = spread_warmth(warmed_plate, coupling_operator)
    glowing = jax.nn.sigmoid(advanced_thermal_state)
    opacity = optical_thickness[substance_label] * glowing / CELLS_DEEP
    through = jnp.cumprod(1.0 - opacity, axis=0)
    before = jnp.concatenate([jnp.ones_like(through[:1]), through[:-1]], axis=0)
    weight = before * opacity
    colours = [jnp.sum(weight * substance_colours[substance_label, channel], axis=0) for channel in range(3)]
    output_picture = jnp.stack(colours + [1.0 - through[-1]])
    return advanced_thermal_state, output_picture
```

```python
import functools

import jax
import jax.numpy as jnp
from jax import lax
from jax.experimental import pallas as pl
from jax.experimental.pallas import tpu as pltpu
from jax.sharding import PartitionSpec as P

MESH = pl.DeviceIdType.MESH
SUB, LANES = 8, 128


def kernel(
    sizes,
    t_hbm, lab_hbm, coef_hbm, thick_hbm, tint_hbm,
    out_hbm, pic_ref,
    u, d, h, f, lab, xs, xr, xs2, xr2, ys, yr, ys2, yr2, mid, ib, rb,
    coef, thick, tint, lsem, ssem, rsem, asem, bsem,
):
    n_sx, n_sy, n_row = sizes
    depth, wide = lab.shape[0], lab.shape[1]
    blocks = wide // SUB
    per_group = LANES // depth
    groups = blocks // per_group
    chunks = depth // SUB
    last = depth
    me, my_sx, my_sy = lax.axis_index("row"), lax.axis_index("sx"), lax.axis_index("sy")
    has_prev, has_next = me > 0, me < n_row - 1
    has_left, has_right = my_sy > 0, my_sy < n_sy - 1

    load_t = pltpu.make_async_copy(t_hbm, u.at[pl.ds(1, depth)], lsem.at[0])
    load_l = pltpu.make_async_copy(lab_hbm, lab, lsem.at[1])
    load_c = pltpu.make_async_copy(coef_hbm, coef, lsem.at[2])
    load_k = pltpu.make_async_copy(thick_hbm, thick, lsem.at[3])
    load_p = pltpu.make_async_copy(tint_hbm, tint, lsem.at[4])
    load_c.start()
    load_l.start()
    load_t.start()
    load_k.start()
    load_p.start()

    barrier = pltpu.get_barrier_semaphore()
    for o in range(1, n_row):
        pl.semaphore_signal(barrier, inc=1, device_id={"row": lax.rem(me + o, n_row)}, device_id_type=MESH)
    sx_next = lax.rem(my_sx + 1, n_sx)
    sx_prev = lax.rem(my_sx + n_sx - 1, n_sx)
    pl.semaphore_signal(barrier, inc=1, device_id={"sx": sx_next}, device_id_type=MESH)
    pl.semaphore_signal(barrier, inc=1, device_id={"sx": sx_prev}, device_id_type=MESH)

    @pl.when(has_left)
    def _():
        pl.semaphore_signal(barrier, inc=1, device_id={"sy": my_sy - 1}, device_id_type=MESH)

    @pl.when(has_right)
    def _():
        pl.semaphore_signal(barrier, inc=1, device_id={"sy": my_sy + 1}, device_id_type=MESH)

    lane = lax.broadcasted_iota(jnp.int32, (SUB, LANES), 1)
    sub = lax.broadcasted_iota(jnp.int32, (SUB, LANES), 0)
    lane_after = lax.rem(lane + 1, LANES)
    at_ends = (lane == 0) | (lane == LANES - 1)
    is_even = lax.rem(lane, 2) == 0
    zero = jnp.zeros((SUB, LANES), jnp.float32)

    @pl.when(jnp.logical_not(has_prev))
    def _():
        for a in (u, d, h):
            a[0] = jnp.zeros((wide, LANES), jnp.float32)

    @pl.when(jnp.logical_not(has_next))
    def _():
        for a in (u, d, h):
            a[depth + 1] = jnp.zeros((wide, LANES), jnp.float32)

    @pl.when(jnp.logical_not(has_left))
    def _():
        yr[0] = jnp.zeros(yr.shape[1:], jnp.float32)
        yr2[0] = jnp.zeros(yr2.shape[1:], jnp.float32)

    @pl.when(jnp.logical_not(has_right))
    def _():
        yr[1] = jnp.zeros(yr.shape[1:], jnp.float32)
        yr2[1] = jnp.zeros(yr2.shape[1:], jnp.float32)

    def rows(xb):
        return pl.ds(SUB * xb, SUB)

    def spot(z0, xb):
        return depth * (xb % per_group) + z0

    load_c.wait()
    c0, c1, c2 = 0.5 * coef[0], 0.5 * coef[1], 0.5 * coef[2]
    load_l.wait()
    load_t.wait()

    def put(acc, v, m, xb):
        left, right = acc
        r = pltpu.roll(v, m, 1)
        g = xb // per_group
        left[g] = jnp.where(lane == m, r, left[g])
        right[g] = jnp.where(lane_after == m, r, right[g])

    def pack_first(z0, carry):
        lu, ru, ld, rd = [list(c) for c in carry]
        for xb in range(blocks):
            v = u[z0 + 1, rows(xb), :]
            lb = lab[z0, rows(xb), :]
            dv = jnp.where(lb == 0, c0, jnp.where(lb == 1, c1, c2))
            d[z0 + 1, rows(xb), :] = dv
            m = spot(z0, xb)
            put((lu, ru), v, m, xb)
            put((ld, rd), dv, m, xb)
        return tuple(tuple(c) for c in (lu, ru, ld, rd))

    empty = (zero,) * groups
    lu, ru, ld, rd = lax.fori_loop(0, depth, pack_first, (empty,) * 4)
    for g in range(groups):
        at = pl.ds(SUB * g, SUB)
        ys[0, 0, at, :] = lu[g]
        ys[0, 1, at, :] = ld[g]
        ys[1, 0, at, :] = pltpu.roll(ru[g], 1, 1)
        ys[1, 1, at, :] = pltpu.roll(rd[g], 1, 1)

    def edge(ref, first, k, side):
        row = (wide - 1) * side
        flat = ref.reshape(ref.shape[0] * wide, LANES)
        return flat, pl.ds((first + SUB * k) * wide + row, SUB, stride=wide)

    for side in (0, 1):
        for k in range(chunks):
            for i, a in enumerate((u, d)):
                flat, at = edge(a, 1, k, side)
                xs[side, i, pl.ds(SUB * k, SUB), :] = flat[at, :]

    def remote(src, dst, s, where):
        return pltpu.make_async_remote_copy(
            src_ref=src, dst_ref=dst, send_sem=ssem.at[s], recv_sem=rsem.at[s],
            device_id=where, device_id_type=MESH,
        )

    to_next, to_prev = {"row": me + 1}, {"row": me - 1}
    to_right, to_left = {"sy": my_sy + 1}, {"sy": my_sy - 1}
    to_up, to_down = {"sx": sx_next}, {"sx": sx_prev}
    z_first = [
        (remote(u.at[last], u.at[0], 0, to_next), has_next, has_prev),
        (remote(d.at[last], d.at[0], 1, to_next), has_next, has_prev),
        (remote(u.at[1], u.at[depth + 1], 2, to_prev), has_prev, has_next),
        (remote(d.at[1], d.at[depth + 1], 3, to_prev), has_prev, has_next),
    ]
    y_first = [
        (remote(ys.at[1], yr.at[0], 4, to_right), has_right, has_left),
        (remote(ys.at[0], yr.at[1], 5, to_left), has_left, has_right),
    ]
    x_first = [
        (remote(xs.at[1], xr.at[0], 6, to_up), None, None),
        (remote(xs.at[0], xr.at[1], 7, to_down), None, None),
    ]
    z_second = [
        (remote(h.at[last], h.at[0], 8, to_next), has_next, has_prev),
        (remote(h.at[1], h.at[depth + 1], 9, to_prev), has_prev, has_next),
    ]
    y_second = [
        (remote(ys2.at[1], yr2.at[0], 10, to_right), has_right, has_left),
        (remote(ys2.at[0], yr2.at[1], 11, to_left), has_left, has_right),
    ]
    x_second = [
        (remote(xs2.at[1], xr2.at[0], 12, to_up), None, None),
        (remote(xs2.at[0], xr2.at[1], 13, to_down), None, None),
    ]

    def only(cond, act):
        if cond is None:
            act()
        else:
            pl.when(cond)(act)

    def start(copies):
        for copy, sends, _ in copies:
            only(sends, copy.start)

    def arrive(copies):
        for copy, _, receives in copies:
            only(receives, copy.wait_recv)

    def left_here(copies):
        for copy, sends, _ in copies:
            only(sends, copy.wait_send)

    waits = n_row + 1 + has_left.astype(jnp.int32) + has_right.astype(jnp.int32)
    pl.semaphore_wait(barrier, waits)
    start(y_first)
    start(z_first)
    start(x_first)

    def flux(da, db, ub, ua):
        return (da + db) * (ub - ua)

    def inner(src, dst, shift):
        def plane(z, uc, dc, fz, un, dn):
            nf = []
            for xb in range(blocks):
                a, k = uc[xb], dc[xb]
                if xb < blocks - 1:
                    at = pl.ds(SUB * xb + 1, SUB)
                    fx = flux(k, d[z, at, :], src[z, at, :], a)
                else:
                    fx = flux(k, pltpu.roll(k, SUB - 1, 0), pltpu.roll(a, SUB - 1, 0), a)
                    fx = jnp.where(sub == SUB - 1, 0.0, fx)
                if xb > 0:
                    at = pl.ds(SUB * xb - 1, SUB)
                    gx = flux(k, d[z, at, :], src[z, at, :], a)
                else:
                    gx = flux(k, pltpu.roll(k, 1, 0), pltpu.roll(a, 1, 0), a)
                    gx = jnp.where(sub == 0, 0.0, gx)
                fy = flux(k, pltpu.roll(k, LANES - 1, 1), pltpu.roll(a, LANES - 1, 1), a)
                fy = jnp.where(lane == LANES - 1, 0.0, fy)
                total = (fx + gx) + (fy - pltpu.roll(fy, 1, 1))
                if un is not None:
                    nz = flux(k, dn[xb], un[xb], a)
                    total = total + (nz - fz[xb])
                    nf.append(nz)
                else:
                    total = total - fz[xb]
                dst[z + shift, rows(xb), :] = a + total
            return tuple(nf)

        def load(ref, z):
            return tuple(ref[z, rows(xb), :] for xb in range(blocks))

        def step(z, carry):
            uc, dc, fz = carry
            un, dn = load(src, z + 1), load(d, z + 1)
            return un, dn, plane(z, uc, dc, fz, un, dn)

        first = (load(src, 1), load(d, 1), (zero,) * blocks)
        uc, dc, fz = lax.fori_loop(1, last, step, first)
        plane(last, uc, dc, fz, None, None)

    def x_faces(dst, first, own, came):
        for side in (0, 1):
            for k in range(chunks):
                at = pl.ds(SUB * k, SUB)
                flat, where = edge(dst, first, k, side)
                flat[where, :] = flat[where, :] + flux(
                    xs[side, 1, at, :], xr[side, 1, at, :], came(side, at), own(side, at)
                )

    def y_faces(own, came):
        even, odd = [], []
        for g in range(groups):
            at = pl.ds(SUB * g, SUB)
            a = flux(ys[0, 1, at, :], yr[0, 1, at, :], came(0, at), own(0, at))
            b = flux(ys[1, 1, at, :], yr[1, 1, at, :], came(1, at), own(1, at))
            b = pltpu.roll(b, LANES - 1, 1)
            even.append(jnp.where(is_even, a, b))
            odd.append(jnp.where(is_even, b, a))
        return even, odd

    def from_sides(packed, z0, parity, xb):
        m = spot(z0, xb)
        r = pltpu.roll(packed[parity][xb // per_group], lax.rem(LANES - m, LANES), 1)
        return jnp.where(at_ends, r, 0.0)

    inner(u, h, 0)

    arrive(x_first)
    x_faces(h, 1, lambda s, at: xs[s, 0, at, :], lambda s, at: xr[s, 0, at, :])
    arrive(y_first)
    packed = y_faces(lambda s, at: ys[s, 0, at, :], lambda s, at: yr[s, 0, at, :])
    arrive(z_first)
    for z, ghost in ((1, 0), (last, depth + 1)):
        for xb in range(blocks):
            at = rows(xb)
            fz = flux(d[z, at, :], d[ghost, at, :], u[ghost, at, :], u[z, at, :])
            h[z, at, :] = h[z, at, :] + fz + from_sides(packed, z - 1, (z - 1) % 2, xb)
    start(z_second)

    def pack_plane(z0, parity, carry, corrected):
        lh, rh = [list(c) for c in carry]
        for xb in range(blocks):
            v = h[z0 + 1, rows(xb), :]
            if not corrected:
                v = v + from_sides(packed, z0, parity, xb)
                h[z0 + 1, rows(xb), :] = v
            put((lh, rh), v, spot(z0, xb), xb)
        return tuple(lh), tuple(rh)

    def pack_pair(j, carry):
        carry = pack_plane(2 * j + 1, 1, carry, False)
        return pack_plane(2 * j + 2, 0, carry, False)

    carry = pack_plane(0, 0, (empty, empty), True)
    carry = lax.fori_loop(0, depth // 2 - 1, pack_pair, carry)
    lh, rh = pack_plane(depth - 1, 1, carry, True)
    for g in range(groups):
        at = pl.ds(SUB * g, SUB)
        ys2[0, at, :] = lh[g]
        ys2[1, at, :] = pltpu.roll(rh[g], 1, 1)
    start(y_second)
    for side in (0, 1):
        for k in range(chunks):
            flat, at = edge(h, 1, k, side)
            xs2[side, pl.ds(SUB * k, SUB), :] = flat[at, :]
    start(x_second)

    inner(h, f, -1)

    load_k.wait()
    scale = 0.5 / (depth * n_row)
    k0, k1, k2 = thick[0] * scale, thick[1] * scale, thick[2] * scale

    def opaque(v, lb):
        first, second = lb == 0, lb == 1
        half = jnp.where(first, k0, jnp.where(second, k1, k2))
        return half + half * jnp.tanh(0.5 * v), first, second

    arrive(x_second)
    x_faces(f, 0, lambda s, at: xs2[s, at, :], lambda s, at: xr2[s, at, :])
    arrive(y_second)
    packed2 = y_faces(lambda s, at: ys2[s, at, :], lambda s, at: yr2[s, at, :])

    def march(z0, parity, carry):
        through, w0, w1, w2 = [list(c) for c in carry]
        for xb in range(blocks):
            v = f[z0, rows(xb), :] + from_sides(packed2, z0, parity, xb)
            f[z0, rows(xb), :] = v
            a, first, second = opaque(v, lab[z0, rows(xb), :])
            w = through[xb] * a
            through[xb] = through[xb] - w
            w0[xb] = w0[xb] + jnp.where(first, w, 0.0)
            w1[xb] = w1[xb] + jnp.where(second, w, 0.0)
            w2[xb] = w2[xb] + jnp.where(first | second, 0.0, w)
        return tuple(tuple(c) for c in (through, w0, w1, w2))

    def march_pair(j, carry):
        return march(2 * j + 2, 0, march(2 * j + 1, 1, carry))

    one = jnp.ones((SUB, LANES), jnp.float32)
    state = ((one,) * blocks,) + ((zero,) * blocks,) * 3
    state = lax.fori_loop(0, depth // 2 - 1, march_pair, state)
    for i in range(4):
        for xb in range(blocks):
            mid[i, rows(xb), :] = state[i][xb]
    store_mid = pltpu.make_async_copy(f.at[pl.ds(1, depth - 2)], out_hbm.at[pl.ds(1, depth - 2)], lsem.at[0])
    store_mid.start()
    load_p.wait()

    arrive(z_second)
    for z0, ghost, parity in ((0, 0, 0), (depth - 1, depth + 1, 1)):
        for xb in range(blocks):
            at = rows(xb)
            fz = flux(d[z0 + 1, at, :], d[ghost, at, :], h[ghost, at, :], h[z0 + 1, at, :])
            f[z0, at, :] = f[z0, at, :] + fz + from_sides(packed2, z0, parity, xb)
    store_a = pltpu.make_async_copy(f.at[0], out_hbm.at[0], lsem.at[1])
    store_b = pltpu.make_async_copy(f.at[depth - 1], out_hbm.at[depth - 1], lsem.at[2])
    store_a.start()
    store_b.start()

    def finish(dest, ref, slot):
        at = pl.ds(pl.multiple_of(dest * SUB, SUB), SUB)
        a, fa, fb = opaque(f[0, at, :], lab[0, at, :])
        b, ga, gb = opaque(f[depth - 1, at, :], lab[depth - 1, at, :])
        clear = 1.0 - a
        through = clear * mid[0, at, :]
        w = through * b
        w0 = jnp.where(fa, a, 0.0) + clear * mid[1, at, :] + jnp.where(ga, w, 0.0)
        w1 = jnp.where(fb, a, 0.0) + clear * mid[2, at, :] + jnp.where(gb, w, 0.0)
        w2 = jnp.where(fa | fb, 0.0, a) + clear * mid[3, at, :] + jnp.where(ga | gb, 0.0, w)
        for c in range(3):
            ref[slot, c] = w0 * tint[0, c] + w1 * tint[1, c] + w2 * tint[2, c]
        ref[slot, 3] = through - w

    def hand(o):
        dest = lax.rem(me + o, n_row)
        return pltpu.make_async_remote_copy(
            src_ref=ib.at[dest], dst_ref=rb.at[me], send_sem=asem.at[o], recv_sem=bsem.at[me],
            device_id={"row": dest}, device_id_type=MESH,
        )

    for o in range(1, n_row):
        finish(lax.rem(me + o, n_row), ib, lax.rem(me + o, n_row))
        hand(o).start()
    finish(me, rb, me)

    for s in range(n_row):
        @pl.when(me != s)
        def _():
            pltpu.make_async_remote_copy(
                src_ref=ib.at[s], dst_ref=rb.at[s], send_sem=asem.at[0], recv_sem=bsem.at[s],
                device_id={"row": s}, device_id_type=MESH,
            ).wait_recv()

    through = one
    colour = [zero] * 3
    for s in range(n_row):
        for c in range(3):
            colour[c] = colour[c] + through * rb[s, c]
        through = through * rb[s, 3]
    for c in range(3):
        pic_ref[c] = colour[c]
    pic_ref[3] = 1.0 - through

    for o in range(1, n_row):
        hand(o).wait_send()
    for copies in (z_first, y_first, x_first, z_second, y_second, x_second):
        left_here(copies)
    store_mid.wait()
    store_a.wait()
    store_b.wait()


def solution(mesh):
    sizes = (mesh.shape["sx"], mesh.shape["sy"], mesh.shape["row"])
    n_row = sizes[2]

    def per_device(thermal_state, substance_label, thermal_coefficients, optical_thickness, substance_colours):
        depth, wide, tall = thermal_state.shape
        f32 = jnp.float32
        sides = (2, SUB * (depth * wide // (SUB * LANES)), LANES)
        both = (2, 2) + sides[1:]
        anywhere = pl.BlockSpec(memory_space=pl.ANY)
        return pl.pallas_call(
            functools.partial(kernel, sizes),
            out_shape=(
                jax.ShapeDtypeStruct((depth, wide, tall), f32),
                jax.ShapeDtypeStruct((4, wide // n_row, tall), f32),
            ),
            in_specs=[anywhere] * 5,
            out_specs=(anywhere, pl.BlockSpec(memory_space=pltpu.VMEM)),
            scratch_shapes=[
                pltpu.VMEM((depth + 2, wide, tall), f32),
                pltpu.VMEM((depth + 2, wide, tall), f32),
                pltpu.VMEM((depth + 2, wide, tall), f32),
                pltpu.VMEM((depth, wide, tall), f32),
                pltpu.VMEM((depth, wide, tall), jnp.int32),
                pltpu.VMEM((2, 2, depth, tall), f32),
                pltpu.VMEM((2, 2, depth, tall), f32),
                pltpu.VMEM((2, depth, tall), f32),
                pltpu.VMEM((2, depth, tall), f32),
                pltpu.VMEM(both, f32),
                pltpu.VMEM(both, f32),
                pltpu.VMEM(sides, f32),
                pltpu.VMEM(sides, f32),
                pltpu.VMEM((4, wide, tall), f32),
                pltpu.VMEM((n_row, 4, wide // n_row, tall), f32),
                pltpu.VMEM((n_row, 4, wide // n_row, tall), f32),
                pltpu.SMEM((3,), f32),
                pltpu.SMEM((3,), f32),
                pltpu.SMEM((3, 3), f32),
                pltpu.SemaphoreType.DMA((5,)),
                pltpu.SemaphoreType.DMA((14,)),
                pltpu.SemaphoreType.DMA((14,)),
                pltpu.SemaphoreType.DMA((n_row,)),
                pltpu.SemaphoreType.DMA((n_row,)),
            ],
            compiler_params=pltpu.CompilerParams(collective_id=0, has_side_effects=True),
        )(thermal_state, substance_label, thermal_coefficients, optical_thickness, substance_colours)

    placed = (P("row", "sx", "sy"), P("row", "sx", "sy"), P(), P(), P())
    return jax.shard_map(
        per_device,
        mesh=mesh,
        in_specs=placed,
        out_specs=(P("row", "sx", "sy"), P(None, ("sx", "row"), "sy")),
        check_vma=False,
    )
```

```python
import functools

import jax
import jax.numpy as jnp
from jax import lax
from jax.experimental import pallas as pl
from jax.experimental.pallas import tpu as pltpu
from jax.sharding import PartitionSpec as P

MESH = pl.DeviceIdType.MESH
SUB, LANES = 8, 128
UNROLL, MARCH = 8, 10
VMEM_LIMIT = 16 << 20


def kernel(
    sizes,
    t_hbm, lab_hbm, coef_hbm, thick_hbm, tint_hbm,
    f, pic_ref,
    u, d, h, lab, xs, xr, xs2, xr2, fx, ys, yr, ys2, yr2, mid, ib, rb,
    coef, thick, tint, lsem, csem, ssem, rsem, asem, bsem,
):
    n_sx, n_sy, n_row = sizes
    depth, wide = lab.shape[0], lab.shape[1]
    blocks = wide // SUB
    per_group = LANES // depth
    groups = blocks // per_group
    chunks = depth // SUB
    last = depth
    me, my_sx, my_sy = lax.axis_index("row"), lax.axis_index("sx"), lax.axis_index("sy")
    has_prev, has_next = me > 0, me < n_row - 1
    has_left, has_right = my_sy > 0, my_sy < n_sy - 1

    def load(j):
        at = pl.ds(SUB * j, SUB)
        return (
            pltpu.make_async_copy(lab_hbm.at[at], lab.at[at], lsem.at[0, j]),
            pltpu.make_async_copy(t_hbm.at[at], u.at[pl.ds(SUB * j + 1, SUB)], lsem.at[1, j]),
        )

    load_c = pltpu.make_async_copy(coef_hbm, coef, csem.at[0])
    load_k = pltpu.make_async_copy(thick_hbm, thick, csem.at[1])
    load_p = pltpu.make_async_copy(tint_hbm, tint, csem.at[2])
    load_c.start()
    for j in range(chunks):
        for copy in load(j):
            copy.start()
    load_k.start()
    load_p.start()

    barrier = pltpu.get_barrier_semaphore()
    for o in range(1, n_row):
        pl.semaphore_signal(barrier, inc=1, device_id={"row": lax.rem(me + o, n_row)}, device_id_type=MESH)
    sx_next = lax.rem(my_sx + 1, n_sx)
    sx_prev = lax.rem(my_sx + n_sx - 1, n_sx)
    pl.semaphore_signal(barrier, inc=1, device_id={"sx": sx_next}, device_id_type=MESH)
    pl.semaphore_signal(barrier, inc=1, device_id={"sx": sx_prev}, device_id_type=MESH)

    @pl.when(has_left)
    def _():
        pl.semaphore_signal(barrier, inc=1, device_id={"sy": my_sy - 1}, device_id_type=MESH)

    @pl.when(has_right)
    def _():
        pl.semaphore_signal(barrier, inc=1, device_id={"sy": my_sy + 1}, device_id_type=MESH)

    lane = lax.broadcasted_iota(jnp.int32, (SUB, LANES), 1)
    sub = lax.broadcasted_iota(jnp.int32, (SUB, LANES), 0)
    at_ends = (lane == 0) | (lane == LANES - 1)
    is_even = (lane & 1) == 0
    pair = (((lane + 1) >> 1) & (LANES // 2 - 1), lane >> 1)
    zero = jnp.zeros((SUB, LANES), jnp.float32)

    @pl.when(jnp.logical_not(has_prev))
    def _():
        for a in (u, d, h):
            a[0] = jnp.zeros((wide, LANES), jnp.float32)

    @pl.when(jnp.logical_not(has_next))
    def _():
        for a in (u, d, h):
            a[depth + 1] = jnp.zeros((wide, LANES), jnp.float32)

    @pl.when(jnp.logical_not(has_left))
    def _():
        yr[0] = jnp.zeros(yr.shape[1:], jnp.float32)
        yr2[0] = jnp.zeros(yr2.shape[1:], jnp.float32)

    @pl.when(jnp.logical_not(has_right))
    def _():
        yr[1] = jnp.zeros(yr.shape[1:], jnp.float32)
        yr2[1] = jnp.zeros(yr2.shape[1:], jnp.float32)

    def rows(xb):
        return pl.ds(SUB * xb, SUB)

    def spot(z0, xb):
        return depth * (xb % per_group) + z0

    def put(acc, v, z0, parity, xb):
        m = spot(z0, xb)
        at = (parity, xb // per_group)
        acc[at] = jnp.where(pair[parity] == m >> 1, pltpu.roll(v, m, 1), acc[at])

    def fresh():
        return {(p, g): zero for p in (0, 1) for g in range(groups)}

    def faces(acc, g):
        low = jnp.where(is_even, acc[0, g], acc[1, g])
        high = jnp.where(is_even, acc[1, g], acc[0, g])
        return low, pltpu.roll(high, 1, 1)

    load_c.wait()
    c0, c1, c2 = 0.5 * coef[0], 0.5 * coef[1], 0.5 * coef[2]

    def pack_first(j, carry):
        au, ad = [dict(c) for c in carry]
        for copy in load(j):
            copy.wait()
        for i in range(SUB):
            z0 = SUB * j + i
            for xb in range(blocks):
                v = u[z0 + 1, rows(xb), :]
                lb = lab[z0, rows(xb), :]
                dv = jnp.where(lb == 0, c0, jnp.where(lb == 1, c1, c2))
                d[z0 + 1, rows(xb), :] = dv
                put(au, v, z0, i % 2, xb)
                put(ad, dv, z0, i % 2, xb)
        return au, ad

    au, ad = lax.fori_loop(0, chunks, pack_first, (fresh(), fresh()))
    for g in range(groups):
        at = pl.ds(SUB * g, SUB)
        ys[0, 0, at, :], ys[1, 0, at, :] = faces(au, g)
        ys[0, 1, at, :], ys[1, 1, at, :] = faces(ad, g)

    def edge(ref, first, k, side):
        flat = ref.reshape(ref.shape[0] * wide, LANES)
        got = None
        for i in range(SUB):
            row = flat[pl.ds((first + SUB * k + i) * wide + (wide - 1) * side, SUB, stride=0), :]
            got = row if got is None else jnp.where(sub == i, row, got)
        return got

    for side in (0, 1):
        for k in range(chunks):
            for i, a in enumerate((u, d)):
                xs[side, i, pl.ds(SUB * k, SUB), :] = edge(a, 1, k, side)

    def remote(src, dst, s, where):
        return pltpu.make_async_remote_copy(
            src_ref=src, dst_ref=dst, send_sem=ssem.at[s], recv_sem=rsem.at[s],
            device_id=where, device_id_type=MESH,
        )

    to_next, to_prev = {"row": me + 1}, {"row": me - 1}
    to_right, to_left = {"sy": my_sy + 1}, {"sy": my_sy - 1}
    to_up, to_down = {"sx": sx_next}, {"sx": sx_prev}
    z_first = [
        (remote(u.at[last], u.at[0], 0, to_next), has_next, has_prev),
        (remote(d.at[last], d.at[0], 1, to_next), has_next, has_prev),
        (remote(u.at[1], u.at[depth + 1], 2, to_prev), has_prev, has_next),
        (remote(d.at[1], d.at[depth + 1], 3, to_prev), has_prev, has_next),
    ]
    y_first = [
        (remote(ys.at[1], yr.at[0], 4, to_right), has_right, has_left),
        (remote(ys.at[0], yr.at[1], 5, to_left), has_left, has_right),
    ]
    x_first = [
        (remote(xs.at[1], xr.at[0], 6, to_up), None, None),
        (remote(xs.at[0], xr.at[1], 7, to_down), None, None),
    ]
    z_second = [
        (remote(h.at[last], h.at[0], 8, to_next), has_next, has_prev),
        (remote(h.at[1], h.at[depth + 1], 9, to_prev), has_prev, has_next),
    ]
    y_second = [
        (remote(ys2.at[1], yr2.at[0], 10, to_right), has_right, has_left),
        (remote(ys2.at[0], yr2.at[1], 11, to_left), has_left, has_right),
    ]
    x_second = [
        (remote(xs2.at[1], xr2.at[0], 12, to_up), None, None),
        (remote(xs2.at[0], xr2.at[1], 13, to_down), None, None),
    ]

    def only(cond, act):
        if cond is None:
            act()
        else:
            pl.when(cond)(act)

    def start(copies):
        for copy, sends, _ in copies:
            only(sends, copy.start)

    def arrive(copies):
        for copy, _, receives in copies:
            only(receives, copy.wait_recv)

    def left_here(copies):
        for copy, sends, _ in copies:
            only(sends, copy.wait_send)

    waits = n_row + 1 + has_left.astype(jnp.int32) + has_right.astype(jnp.int32)
    pl.semaphore_wait(barrier, waits)
    start(y_first)
    start(z_first)
    start(x_first)

    def flux(da, db, ub, ua):
        return (da + db) * (ub - ua)

    def inner(src, dst, shift):
        def plane(z, fz, closing):
            nf, before = [], None
            for xb in range(blocks):
                a, k = src[z, rows(xb), :], d[z, rows(xb), :]
                if xb < blocks - 1:
                    at = pl.ds(SUB * xb + 1, SUB)
                    fxx = flux(k, d[z, at, :], src[z, at, :], a)
                else:
                    fxx = flux(k, pltpu.roll(k, SUB - 1, 0), pltpu.roll(a, SUB - 1, 0), a)
                    fxx = jnp.where(sub == SUB - 1, 0.0, fxx)
                turned = pltpu.roll(fxx, 1, 0)
                behind = jnp.where(sub == 0, 0.0 if before is None else before, turned)
                before = turned
                fy = flux(k, pltpu.roll(k, LANES - 1, 1), pltpu.roll(a, LANES - 1, 1), a)
                total = (fxx - behind) + (fy - pltpu.roll(fy, 1, 1))
                if not closing:
                    nz = flux(k, d[z + 1, rows(xb), :], src[z + 1, rows(xb), :], a)
                    total = total + (nz - fz[xb])
                    nf.append(nz)
                else:
                    total = total - fz[xb]
                dst[z + shift, rows(xb), :] = a + total
            return tuple(nf)

        def several(j, fz):
            for i in range(UNROLL):
                fz = plane(UNROLL * j + 1 + i, fz, False)
            return fz

        fz = lax.fori_loop(0, depth // UNROLL - 1, several, (zero,) * blocks)
        for z in range(depth - UNROLL + 1, depth + 1):
            fz = plane(z, fz, z == last)

    def x_faces(own, came):
        for side in (0, 1):
            for k in range(chunks):
                at = pl.ds(SUB * k, SUB)
                fx[side, at, :] = flux(xs[side, 1, at, :], xr[side, 1, at, :], came(side, at), own(side, at))

    def y_faces(own, came):
        even, odd = [], []
        for g in range(groups):
            at = pl.ds(SUB * g, SUB)
            dl, dr, ul, ur = ys[0, 1, at, :], ys[1, 1, at, :], own(0, at), own(1, at)
            closed = flux(dl, dr, ul, ur)
            a = flux(dl, yr[0, 1, at, :], came(0, at), ul) + closed
            b = flux(dr, yr[1, 1, at, :], came(1, at), ur) - closed
            b = pltpu.roll(b, LANES - 1, 1)
            even.append(jnp.where(is_even, a, b))
            odd.append(jnp.where(is_even, b, a))
        return even, odd

    def with_faces(v, packed, z0, parity, xb):
        r = pltpu.roll(packed[parity][xb // per_group], (LANES - spot(z0, xb)) & (LANES - 1), 1)
        v = jnp.where(at_ends, v + r, v)
        if xb == 0:
            v = jnp.where(sub == 0, v + fx[0, pl.ds(z0, SUB, stride=0), :], v)
        if xb == blocks - 1:
            v = jnp.where(sub == SUB - 1, v + fx[1, pl.ds(z0, SUB, stride=0), :], v)
        return v

    inner(u, h, 0)

    arrive(x_first)
    x_faces(lambda s, at: xs[s, 0, at, :], lambda s, at: xr[s, 0, at, :])
    arrive(y_first)
    packed = y_faces(lambda s, at: ys[s, 0, at, :], lambda s, at: yr[s, 0, at, :])

    def correct(z0, parity, acc):
        for xb in range(blocks):
            v = with_faces(h[z0 + 1, rows(xb), :], packed, z0, parity, xb)
            h[z0 + 1, rows(xb), :] = v
            put(acc, v, z0, parity, xb)

    def correct_some(j, acc):
        acc = dict(acc)
        for i in range(MARCH):
            correct(MARCH * j + 1 + i, (1 + i) % 2, acc)
        return acc

    acc = dict(lax.fori_loop(0, (depth - 2) // MARCH, correct_some, fresh()))
    arrive(z_first)
    for z0, ghost, parity in ((0, 0, 0), (depth - 1, depth + 1, 1)):
        for xb in range(blocks):
            at = rows(xb)
            fz = flux(d[z0 + 1, at, :], d[ghost, at, :], u[ghost, at, :], u[z0 + 1, at, :])
            v = with_faces(h[z0 + 1, at, :] + fz, packed, z0, parity, xb)
            h[z0 + 1, at, :] = v
            put(acc, v, z0, parity, xb)
    start(z_second)
    for g in range(groups):
        at = pl.ds(SUB * g, SUB)
        ys2[0, at, :], ys2[1, at, :] = faces(acc, g)
    start(y_second)
    for side in (0, 1):
        for k in range(chunks):
            xs2[side, pl.ds(SUB * k, SUB), :] = edge(h, 1, k, side)
    start(x_second)

    inner(h, f, -1)

    load_k.wait()
    scale = 0.5 / (depth * n_row)
    k0, k1, k2 = thick[0] * scale, thick[1] * scale, thick[2] * scale

    def opaque(v, lb):
        first, second = lb == 0, lb == 1
        half = jnp.where(first, k0, jnp.where(second, k1, k2))
        return half + half * jnp.tanh(0.5 * v), first, second

    arrive(x_second)
    x_faces(lambda s, at: xs2[s, at, :], lambda s, at: xr2[s, at, :])
    arrive(y_second)
    packed2 = y_faces(lambda s, at: ys2[s, at, :], lambda s, at: yr2[s, at, :])

    def march(z0, parity, carry):
        through, w0, w1 = [list(c) for c in carry]
        for xb in range(blocks):
            v = with_faces(f[z0, rows(xb), :], packed2, z0, parity, xb)
            f[z0, rows(xb), :] = v
            a, first, second = opaque(v, lab[z0, rows(xb), :])
            w = through[xb] * a
            through[xb] = through[xb] - w
            w0[xb] = w0[xb] + jnp.where(first, w, 0.0)
            w1[xb] = w1[xb] + jnp.where(second, w, 0.0)
        return tuple(tuple(c) for c in (through, w0, w1))

    def march_some(j, carry):
        for i in range(MARCH):
            carry = march(MARCH * j + 1 + i, (1 + i) % 2, carry)
        return carry

    one = jnp.ones((SUB, LANES), jnp.float32)
    state = ((one,) * blocks,) + ((zero,) * blocks,) * 2
    state = lax.fori_loop(0, (depth - 2) // MARCH, march_some, state)
    for i in range(3):
        for xb in range(blocks):
            mid[i, rows(xb), :] = state[i][xb]
    load_p.wait()

    arrive(z_second)
    for xb in range(blocks):
        at = rows(xb)
        ends = []
        for z0, ghost, parity in ((0, 0, 0), (depth - 1, depth + 1, 1)):
            fz = flux(d[z0 + 1, at, :], d[ghost, at, :], h[ghost, at, :], h[z0 + 1, at, :])
            v = with_faces(f[z0, at, :] + fz, packed2, z0, parity, xb)
            f[z0, at, :] = v
            ends.append(opaque(v, lab[z0, at, :]))
        (a, fa, fb), (b, ga, gb) = ends
        clear = 1.0 - a
        through = clear * mid[0, at, :]
        w = through * b
        ib[xb, 0] = jnp.where(fa, a, 0.0) + clear * mid[1, at, :] + jnp.where(ga, w, 0.0)
        ib[xb, 1] = jnp.where(fb, a, 0.0) + clear * mid[2, at, :] + jnp.where(gb, w, 0.0)
        ib[xb, 2] = through - w

    def hand(o):
        dest = lax.rem(me + o, n_row)
        return pltpu.make_async_remote_copy(
            src_ref=ib.at[dest], dst_ref=rb.at[me], send_sem=asem.at[o], recv_sem=bsem.at[me],
            device_id={"row": dest}, device_id_type=MESH,
        )

    for o in range(1, n_row):
        hand(o).start()
    rb[me] = ib[me]

    for s in range(n_row):
        @pl.when(me != s)
        def _():
            pltpu.make_async_remote_copy(
                src_ref=ib.at[s], dst_ref=rb.at[s], send_sem=asem.at[0], recv_sem=bsem.at[s],
                device_id={"row": s}, device_id_type=MESH,
            ).wait_recv()

    through, w0, w1 = one, zero, zero
    for s in range(n_row):
        w0 = w0 + through * rb[s, 0]
        w1 = w1 + through * rb[s, 1]
        through = through * rb[s, 2]
    blocked = 1.0 - through
    w2 = (blocked - w0) - w1
    for c in range(3):
        pic_ref[c] = w0 * tint[0, c] + w1 * tint[1, c] + w2 * tint[2, c]
    pic_ref[3] = blocked

    for o in range(1, n_row):
        hand(o).wait_send()
    for copies in (z_first, y_first, x_first, z_second, y_second, x_second):
        left_here(copies)


def deliver(f, pic, out, out_pic, sem):
    a = pltpu.make_async_copy(f, out, sem.at[0])
    b = pltpu.make_async_copy(pic, out_pic, sem.at[1])
    a.start()
    b.start()
    a.wait()
    b.wait()


def solution(mesh):
    sizes = (mesh.shape["sx"], mesh.shape["sy"], mesh.shape["row"])
    n_row = sizes[2]

    def per_device(thermal_state, substance_label, thermal_coefficients, optical_thickness, substance_colours):
        depth, wide, tall = thermal_state.shape
        f32 = jnp.float32
        sides = (2, SUB * (depth * wide // (SUB * LANES)), LANES)
        both = (2, 2) + sides[1:]
        anywhere = pl.BlockSpec(memory_space=pl.ANY)
        near = pl.BlockSpec(memory_space=pltpu.VMEM)
        chunks = depth // SUB
        results = (
            jax.ShapeDtypeStruct((depth, wide, tall), f32),
            jax.ShapeDtypeStruct((4, wide // n_row, tall), f32),
        )
        f, pic = pl.pallas_call(
            functools.partial(kernel, sizes),
            out_shape=results,
            in_specs=[pl.BlockSpec(memory_space=pltpu.HBM)] * 5,
            out_specs=(near, near),
            scratch_shapes=[
                pltpu.VMEM((depth + 2, wide, tall), f32),
                pltpu.VMEM((depth + 2, wide, tall), f32),
                pltpu.VMEM((depth + 2, wide, tall), f32),
                pltpu.VMEM((depth, wide, tall), jnp.int32),
                pltpu.VMEM((2, 2, depth, tall), f32),
                pltpu.VMEM((2, 2, depth, tall), f32),
                pltpu.VMEM((2, depth, tall), f32),
                pltpu.VMEM((2, depth, tall), f32),
                pltpu.VMEM((2, depth, tall), f32),
                pltpu.VMEM(both, f32),
                pltpu.VMEM(both, f32),
                pltpu.VMEM(sides, f32),
                pltpu.VMEM(sides, f32),
                pltpu.VMEM((3, wide, tall), f32),
                pltpu.VMEM((n_row, 3, wide // n_row, tall), f32),
                pltpu.VMEM((n_row, 3, wide // n_row, tall), f32),
                pltpu.SMEM((3,), f32),
                pltpu.SMEM((3,), f32),
                pltpu.SMEM((3, 3), f32),
                pltpu.SemaphoreType.DMA((2, chunks)),
                pltpu.SemaphoreType.DMA((3,)),
                pltpu.SemaphoreType.DMA((14,)),
                pltpu.SemaphoreType.DMA((14,)),
                pltpu.SemaphoreType.DMA((n_row,)),
                pltpu.SemaphoreType.DMA((n_row,)),
            ],
            compiler_params=pltpu.CompilerParams(
                collective_id=0, has_side_effects=True, vmem_limit_bytes=VMEM_LIMIT
            ),
        )(*[pltpu.with_memory_space_constraint(a, pltpu.HBM) for a in (thermal_state, substance_label, thermal_coefficients, optical_thickness, substance_colours)])
        return pl.pallas_call(
            deliver,
            out_shape=results,
            in_specs=[near, near],
            out_specs=(anywhere, anywhere),
            scratch_shapes=[pltpu.SemaphoreType.DMA((2,))],
            compiler_params=pltpu.CompilerParams(vmem_limit_bytes=VMEM_LIMIT),
        )(f, pic)

    placed = (P("row", "sx", "sy"), P("row", "sx", "sy"), P(), P(), P())
    return jax.shard_map(
        per_device,
        mesh=mesh,
        in_specs=placed,
        out_specs=(P("row", "sx", "sy"), P(None, ("sx", "row"), "sy")),
        check_vma=False,
    )
```

```python
import functools

import jax
import jax.numpy as jnp
from jax import lax
from jax.experimental import pallas as pl
from jax.experimental.pallas import tpu as pltpu
from jax.sharding import PartitionSpec as P

MESH = pl.DeviceIdType.MESH
SUB, LANES = 8, 128
FLUX, FIX, PACK, MARCH, PARTS = 4, 6, 6, 6, 4
VMEM_LIMIT = 16 << 20


def kernel(
    sizes,
    t_hbm, lab_hbm, coef_hbm, thick_hbm, tint_hbm,
    f, pic_ref,
    u, d, h, ky, fy, lab, xs, xr, xs2, xr2, xs3, xr3, fx, fx3, ys, yr, ys2, yr2, ys3, yr3, mid, ib, rb,
    coef, thick, tint, lsem, csem, zsem1, zrec1, zsem2, zrec2, ssem, rsem, asem, bsem,
):
    n_sx, n_sy, n_row = sizes
    depth, wide = t_hbm.shape[0], t_hbm.shape[1]
    blocks = wide // SUB
    per_group = LANES // depth
    groups = blocks // per_group
    chunks = depth // SUB
    last = depth
    per_part = blocks // PARTS
    me, my_sx, my_sy = lax.axis_index("row"), lax.axis_index("sx"), lax.axis_index("sy")
    has_prev, has_next = me > 0, me < n_row - 1
    has_left, has_right = my_sy > 0, my_sy < n_sy - 1

    def load(j):
        at, to = pl.ds(SUB * j, SUB), pl.ds(SUB * j + 1, SUB)
        return (
            pltpu.make_async_copy(lab_hbm.at[at], lab.at[to], lsem.at[0, j]),
            pltpu.make_async_copy(t_hbm.at[at], u.at[to], lsem.at[1, j]),
        )

    load_c = pltpu.make_async_copy(coef_hbm, coef, csem.at[0])
    load_k = pltpu.make_async_copy(thick_hbm, thick, csem.at[1])
    load_p = pltpu.make_async_copy(tint_hbm, tint, csem.at[2])
    load_c.start()
    for j in range(chunks):
        for copy in load(j):
            copy.start()
    load_k.start()
    load_p.start()

    barrier = pltpu.get_barrier_semaphore()
    for o in range(1, n_row):
        pl.semaphore_signal(barrier, inc=1, device_id={"row": lax.rem(me + o, n_row)}, device_id_type=MESH)
    sx_next = lax.rem(my_sx + 1, n_sx)
    sx_prev = lax.rem(my_sx + n_sx - 1, n_sx)
    pl.semaphore_signal(barrier, inc=1, device_id={"sx": sx_next}, device_id_type=MESH)
    pl.semaphore_signal(barrier, inc=1, device_id={"sx": sx_prev}, device_id_type=MESH)

    @pl.when(has_left)
    def _():
        pl.semaphore_signal(barrier, inc=1, device_id={"sy": my_sy - 1}, device_id_type=MESH)

    @pl.when(has_right)
    def _():
        pl.semaphore_signal(barrier, inc=1, device_id={"sy": my_sy + 1}, device_id_type=MESH)

    lane = lax.broadcasted_iota(jnp.int32, (SUB, LANES), 1)
    sub = lax.broadcasted_iota(jnp.int32, (SUB, LANES), 0)
    at_ends = (lane == 0) | (lane == LANES - 1)
    is_even = (lane & 1) == 0
    pair = (((lane + 1) >> 1) & (LANES // 2 - 1), lane >> 1)
    zero = jnp.zeros((SUB, LANES), jnp.float32)
    one = jnp.ones((SUB, LANES), jnp.float32)

    def clear(cond, refs):
        @pl.when(jnp.logical_not(cond))
        def _():
            for r in refs:
                r[...] = jnp.zeros(r.shape, r.dtype)

    clear(has_prev, (u.at[0], d.at[0], h.at[0]))
    clear(has_next, (u.at[depth + 1], d.at[depth + 1], h.at[depth + 1]))
    clear(has_left, (yr.at[0], yr2.at[0], yr3.at[0]))
    clear(has_right, (yr.at[1], yr2.at[1], yr3.at[1]))

    to_next, to_prev = {"row": me + 1}, {"row": me - 1}
    to_right, to_left = {"sy": my_sy + 1}, {"sy": my_sy - 1}
    to_up, to_down = {"sx": sx_next}, {"sx": sx_prev}

    def only(cond, act):
        if cond is None:
            act()
        else:
            pl.when(cond)(act)

    def start(copies):
        for copy, sends, _ in copies:
            only(sends, copy.start)

    def arrive(copies):
        for copy, _, receives in copies:
            only(receives, copy.wait_recv)

    def left_here(copies):
        for copy, sends, _ in copies:
            only(sends, copy.wait_send)

    def remote(src, dst, send, recv, where):
        return pltpu.make_async_remote_copy(
            src_ref=src, dst_ref=dst, send_sem=send, recv_sem=recv, device_id=where, device_id_type=MESH
        )

    def z_first(p):
        at = pl.ds(SUB * per_part * p, SUB * per_part)
        got = []
        for i, (src, dst) in enumerate(((t_hbm, u), (lab_hbm, lab))):
            got.append((remote(src.at[depth - 1, at], dst.at[0, at], zsem1.at[0, i, p], zrec1.at[0, i, p], to_next),
                        has_next, has_prev))
            got.append((remote(src.at[0, at], dst.at[depth + 1, at], zsem1.at[1, i, p], zrec1.at[1, i, p], to_prev),
                        has_prev, has_next))
        return got

    def z_second(p):
        at = pl.ds(SUB * per_part * p, SUB * per_part)
        return [
            (remote(h.at[last, at], h.at[0, at], zsem2.at[0, p], zrec2.at[0, p], to_next), has_next, has_prev),
            (remote(h.at[1, at], h.at[depth + 1, at], zsem2.at[1, p], zrec2.at[1, p], to_prev), has_prev, has_next),
        ]

    def y_copies(src, dst, s):
        return [
            (remote(src.at[1], dst.at[0], ssem.at[s], rsem.at[s], to_right), has_right, has_left),
            (remote(src.at[0], dst.at[1], ssem.at[s + 1], rsem.at[s + 1], to_left), has_left, has_right),
        ]

    def x_copies(src, dst, s):
        return [
            (remote(src.at[1], dst.at[0], ssem.at[s], rsem.at[s], to_up), None, None),
            (remote(src.at[0], dst.at[1], ssem.at[s + 1], rsem.at[s + 1], to_down), None, None),
        ]

    y_first, x_first = y_copies(ys, yr, 0), x_copies(xs, xr, 2)
    y_second, x_second = y_copies(ys2, yr2, 4), x_copies(xs2, xr2, 6)
    y_third, x_third = y_copies(ys3, yr3, 8), x_copies(xs3, xr3, 10)

    waits = n_row + 1 + has_left.astype(jnp.int32) + has_right.astype(jnp.int32)
    pl.semaphore_wait(barrier, waits)
    for p in range(PARTS):
        start(z_first(p))

    def rows(xb):
        return pl.ds(SUB * xb, SUB)

    def spot(z0, xb):
        return depth * (xb % per_group) + z0

    def put(acc, v, z0, parity, xb):
        m = spot(z0, xb)
        at = (parity, xb // per_group)
        acc[at] = jnp.where(pair[parity] == m >> 1, pltpu.roll(v, m, 1), acc[at])

    def fresh():
        return {(p, g): zero for p in (0, 1) for g in range(groups)}

    def faces(acc, g):
        low = jnp.where(is_even, acc[0, g], acc[1, g])
        high = jnp.where(is_even, acc[1, g], acc[0, g])
        return low, pltpu.roll(high, 1, 1)

    load_c.wait()
    c0, c1, c2 = 0.5 * coef[0], 0.5 * coef[1], 0.5 * coef[2]

    def conduct(lb):
        return jnp.where(lb == 0, c0, jnp.where(lb == 1, c1, c2))

    def pack_first(j, carry):
        au, ad = [dict(c) for c in carry]
        for copy in load(j):
            copy.wait()
        for i in range(SUB):
            z0 = SUB * j + i
            for xb in range(blocks):
                v = u[z0 + 1, rows(xb), :]
                dv = conduct(lab[z0 + 1, rows(xb), :])
                d[z0 + 1, rows(xb), :] = dv
                put(au, v, z0, i % 2, xb)
                put(ad, dv, z0, i % 2, xb)
        return au, ad

    au, ad = lax.fori_loop(0, chunks, pack_first, (fresh(), fresh()))
    for g in range(groups):
        at = pl.ds(SUB * g, SUB)
        ys[0, 0, at, :], ys[1, 0, at, :] = faces(au, g)
        ys[0, 1, at, :], ys[1, 1, at, :] = faces(ad, g)
    start(y_first)

    def edge(ref, first, k, side):
        flat = ref.reshape(ref.shape[0] * wide, LANES)
        got = None
        for i in range(SUB):
            row = flat[pl.ds((first + SUB * k + i) * wide + (wide - 1) * side, SUB, stride=0), :]
            got = row if got is None else jnp.where(sub == i, row, got)
        return got

    for side in (0, 1):
        for k in range(chunks):
            for i, a in enumerate((u, d)):
                xs[side, i, pl.ds(SUB * k, SUB), :] = edge(a, 1, k, side)
    start(x_first)

    def flux(da, db, ub, ua):
        return (da + db) * (ub - ua)

    def plane(src, dst, shift, z, fz, high, first_step):
        nf, before = [], None
        for xb in range(blocks):
            a, k = src[z, rows(xb), :], d[z, rows(xb), :]
            if xb < blocks - 1:
                at = pl.ds(SUB * xb + 1, SUB)
                fxx = flux(k, d[z, at, :], src[z, at, :], a)
            else:
                fxx = flux(k, pltpu.roll(k, SUB - 1, 0), pltpu.roll(a, SUB - 1, 0), a)
                fxx = jnp.where(sub == SUB - 1, 0.0, fxx)
            turned = pltpu.roll(fxx, 1, 0)
            behind = jnp.where(sub == 0, 0.0 if before is None else before, turned)
            before = turned
            if first_step:
                kk = k + pltpu.roll(k, LANES - 1, 1)
                ky[z - 1, rows(xb), :] = kk
            else:
                kk = ky[z - 1, rows(xb), :]
            gy = kk * (pltpu.roll(a, LANES - 1, 1) - a)
            fy[z - 1, rows(xb), :] = gy
            total = (fxx - behind) + gy
            if high:
                nz = flux(k, d[z + 1, rows(xb), :], src[z + 1, rows(xb), :], a)
                total = total + (nz if fz is None else nz - fz[xb])
                nf.append(nz)
            elif fz is not None:
                total = total - fz[xb]
            dst[z + shift, rows(xb), :] = a + total
        return tuple(nf)

    def between(src, z):
        return tuple(
            flux(d[z, rows(xb), :], d[z + 1, rows(xb), :], src[z + 1, rows(xb), :], src[z, rows(xb), :])
            for xb in range(blocks)
        )

    def planes(src, dst, shift, begin, count, fz, first_step):
        def several(j, fz):
            for i in range(FLUX):
                fz = plane(src, dst, shift, begin + FLUX * j + i, fz, True, first_step)
            return fz

        return lax.fori_loop(0, count // FLUX, several, fz)

    fz = plane(u, h, 0, 1, None, True, True)
    fz = planes(u, h, 0, 2, depth - FLUX, fz, True)
    for z in range(depth - FLUX + 2, last):
        fz = plane(u, h, 0, z, fz, True, True)
    plane(u, h, 0, last, fz, False, True)

    def x_faces(to, tiles, own, came):
        for side in (0, 1):
            for i, k in enumerate(tiles):
                at, place = pl.ds(SUB * k, SUB), pl.ds(SUB * i, SUB)
                to[side, place, :] = flux(
                    xs[side, 1, at, :], xr[side, 1, at, :], came(side, place), own(side, place)
                )

    def y_faces(own, came):
        even, odd = [], []
        for g in range(groups):
            at = pl.ds(SUB * g, SUB)
            dl, dr, ul, ur = ys[0, 1, at, :], ys[1, 1, at, :], own(0, at), own(1, at)
            closed = flux(dl, dr, ul, ur)
            a = flux(dl, yr[0, 1, at, :], came(0, at), ul) + closed
            b = flux(dr, yr[1, 1, at, :], came(1, at), ur) - closed
            b = pltpu.roll(b, LANES - 1, 1)
            even.append(jnp.where(is_even, a, b))
            odd.append(jnp.where(is_even, b, a))
        return even, odd

    def with_faces(v, packed, rowsx, zx, z0, parity, xb):
        r = pltpu.roll(packed[parity][xb // per_group], (LANES - spot(z0, xb)) & (LANES - 1), 1)
        v = v - pltpu.roll(fy[z0, rows(xb), :], 1, 1)
        v = jnp.where(at_ends, v + r, v)
        if xb == 0:
            v = jnp.where(sub == 0, v + rowsx[0, pl.ds(zx, SUB, stride=0), :], v)
        if xb == blocks - 1:
            v = jnp.where(sub == SUB - 1, v + rowsx[1, pl.ds(zx, SUB, stride=0), :], v)
        return v

    def sweep(count, body, carry):
        def some(j, carry):
            for i in range(count):
                carry = body(count * j + 1 + i, (1 + i) % 2, carry)
            return carry

        return lax.fori_loop(0, (depth - 2) // count, some, carry)

    arrive(x_first)
    x_faces(fx, range(chunks), lambda s, at: xs[s, 0, at, :], lambda s, at: xr[s, 0, at, :])
    arrive(y_first)
    packed = y_faces(lambda s, at: ys[s, 0, at, :], lambda s, at: yr[s, 0, at, :])

    def fix_h(z0, parity, carry):
        for xb in range(blocks):
            h[z0 + 1, rows(xb), :] = with_faces(h[z0 + 1, rows(xb), :], packed, fx, z0, z0, parity, xb)
        return carry

    def pack_h(z0, parity, acc):
        acc = dict(acc)
        for xb in range(blocks):
            put(acc, h[z0 + 1, rows(xb), :], z0, parity, xb)
        return acc

    sweep(FIX, fix_h, 0)
    acc = dict(sweep(PACK, pack_h, fresh()))

    def y_out(to, acc):
        for g in range(groups):
            at = pl.ds(SUB * g, SUB)
            to[0, at, :], to[1, at, :] = faces(acc, g)

    y_out(ys2, acc)
    start(y_second)
    for side in (0, 1):
        for k in range(chunks):
            xs2[side, pl.ds(SUB * k, SUB), :] = edge(h, 1, k, side)
    start(x_second)
    planes(h, f, -1, 3, depth - 4, between(h, 2), False)

    outer = ((0, 0, 0), (depth - 1, depth + 1, 1))
    tiles = (0, chunks - 1)

    for p in range(PARTS):
        arrive(z_first(p))
        for (z0, ghost, parity), inside in zip(outer, (has_prev, has_next)):
            for xb in range(per_part * p, per_part * (p + 1)):
                at = rows(xb)
                dg = jnp.where(inside, conduct(lab[ghost, at, :]), 0.0)
                d[ghost, at, :] = dg
                fz = flux(d[z0 + 1, at, :], dg, u[ghost, at, :], u[z0 + 1, at, :])
                h[z0 + 1, at, :] = with_faces(h[z0 + 1, at, :] + fz, packed, fx, z0, z0, parity, xb)
        start(z_second(p))

    for z0, _, parity in outer:
        acc = pack_h(z0, parity, acc)
    y_out(ys3, acc)
    start(y_third)
    for side in (0, 1):
        for i, k in enumerate(tiles):
            xs3[side, pl.ds(SUB * i, SUB), :] = edge(h, 1, k, side)
    start(x_third)

    fz = plane(h, f, -1, 1, None, True, False)
    plane(h, f, -1, 2, fz, True, False)
    fz = plane(h, f, -1, last - 1, between(h, last - 2), True, False)
    plane(h, f, -1, last, fz, False, False)

    arrive(x_second)
    x_faces(fx, range(chunks), lambda s, at: xs2[s, at, :], lambda s, at: xr2[s, at, :])
    arrive(y_second)
    packed2 = y_faces(lambda s, at: ys2[s, at, :], lambda s, at: yr2[s, at, :])

    def fix_f(z0, parity, carry):
        for xb in range(blocks):
            f[z0, rows(xb), :] = with_faces(f[z0, rows(xb), :], packed2, fx, z0, z0, parity, xb)
        return carry

    sweep(FIX, fix_f, 0)

    load_k.wait()
    scale = 0.5 / (depth * n_row)
    k0, k1, k2 = thick[0] * scale, thick[1] * scale, thick[2] * scale

    def opaque(v, lb):
        first, second = lb == 0, lb == 1
        half = jnp.where(first, k0, jnp.where(second, k1, k2))
        return half + half * jnp.tanh(0.5 * v), first, second

    def march(z0, parity, carry):
        through, w0, w1 = [list(c) for c in carry]
        for xb in range(blocks):
            a, first, second = opaque(f[z0, rows(xb), :], lab[z0 + 1, rows(xb), :])
            w = through[xb] * a
            through[xb] = through[xb] - w
            w0[xb] = w0[xb] + jnp.where(first, w, 0.0)
            w1[xb] = w1[xb] + jnp.where(second, w, 0.0)
        return tuple(tuple(c) for c in (through, w0, w1))

    state = sweep(MARCH, march, ((one,) * blocks,) + ((zero,) * blocks,) * 2)
    for i in range(3):
        for xb in range(blocks):
            mid[i, rows(xb), :] = state[i][xb]

    arrive(x_third)
    x_faces(fx3, tiles, lambda s, at: xs3[s, at, :], lambda s, at: xr3[s, at, :])
    arrive(y_third)
    packed3 = y_faces(lambda s, at: ys3[s, at, :], lambda s, at: yr3[s, at, :])
    for z0, _, parity in outer:
        for xb in range(blocks):
            f[z0, rows(xb), :] = with_faces(
                f[z0, rows(xb), :], packed3, fx3, z0 if z0 == 0 else 2 * SUB - 1, z0, parity, xb
            )
    load_p.wait()

    def hand(dest):
        return pltpu.make_async_remote_copy(
            src_ref=ib.at[dest], dst_ref=rb.at[me], send_sem=asem.at[dest], recv_sem=bsem.at[me],
            device_id={"row": dest}, device_id_type=MESH,
        )

    for p in range(PARTS):
        arrive(z_second(p))
        for xb in range(per_part * p, per_part * (p + 1)):
            at = rows(xb)
            ends = []
            for z0, ghost, parity in outer:
                fz = flux(d[z0 + 1, at, :], d[ghost, at, :], h[ghost, at, :], h[z0 + 1, at, :])
                v = f[z0, at, :] + fz
                f[z0, at, :] = v
                ends.append(opaque(v, lab[z0 + 1, at, :]))
            (a, fa, fb), (b, ga, gb) = ends
            clear_a = 1.0 - a
            through = clear_a * mid[0, at, :]
            w = through * b
            ib[xb, 0] = jnp.where(fa, a, 0.0) + clear_a * mid[1, at, :] + jnp.where(ga, w, 0.0)
            ib[xb, 1] = jnp.where(fb, a, 0.0) + clear_a * mid[2, at, :] + jnp.where(gb, w, 0.0)
            ib[xb, 2] = through - w
        for dest in range(per_part * p, per_part * (p + 1)):
            pl.when(me != dest)(hand(dest).start)
    rb[me] = ib[me]

    for s in range(n_row):
        @pl.when(me != s)
        def _():
            pltpu.make_async_remote_copy(
                src_ref=ib.at[s], dst_ref=rb.at[s], send_sem=asem.at[s], recv_sem=bsem.at[s],
                device_id={"row": s}, device_id_type=MESH,
            ).wait_recv()

    through, w0, w1 = one, zero, zero
    for s in range(n_row):
        w0 = w0 + through * rb[s, 0]
        w1 = w1 + through * rb[s, 1]
        through = through * rb[s, 2]
    blocked = 1.0 - through
    w2 = (blocked - w0) - w1
    for c in range(3):
        pic_ref[c] = w0 * tint[0, c] + w1 * tint[1, c] + w2 * tint[2, c]
    pic_ref[3] = blocked

    for dest in range(n_row):
        pl.when(me != dest)(hand(dest).wait_send)
    for p in range(PARTS):
        left_here(z_first(p))
        left_here(z_second(p))
    for copies in (y_first, x_first, y_second, x_second, y_third, x_third):
        left_here(copies)


def deliver(f, pic, out, out_pic, sem):
    a = pltpu.make_async_copy(f, out, sem.at[0])
    b = pltpu.make_async_copy(pic, out_pic, sem.at[1])
    a.start()
    b.start()
    a.wait()
    b.wait()


def solution(mesh):
    sizes = (mesh.shape["sx"], mesh.shape["sy"], mesh.shape["row"])
    n_row = sizes[2]

    def per_device(thermal_state, substance_label, thermal_coefficients, optical_thickness, substance_colours):
        depth, wide, tall = thermal_state.shape
        f32 = jnp.float32
        side = depth * wide // LANES
        near = pl.BlockSpec(memory_space=pltpu.VMEM)
        anywhere = pl.BlockSpec(memory_space=pl.ANY)
        chunks = depth // SUB
        results = (
            jax.ShapeDtypeStruct((depth, wide, tall), f32),
            jax.ShapeDtypeStruct((4, wide // n_row, tall), f32),
        )
        f, pic = pl.pallas_call(
            functools.partial(kernel, sizes),
            out_shape=results,
            in_specs=[anywhere] * 5,
            out_specs=(near, near),
            scratch_shapes=[
                pltpu.VMEM((depth + 2, wide, tall), f32),
                pltpu.VMEM((depth + 2, wide, tall), f32),
                pltpu.VMEM((depth + 2, wide, tall), f32),
                pltpu.VMEM((depth, wide, tall), f32),
                pltpu.VMEM((depth, wide, tall), f32),
                pltpu.VMEM((depth + 2, wide, tall), jnp.int32),
                pltpu.VMEM((2, 2, depth, tall), f32),
                pltpu.VMEM((2, 2, depth, tall), f32),
                pltpu.VMEM((2, depth, tall), f32),
                pltpu.VMEM((2, depth, tall), f32),
                pltpu.VMEM((2, 2 * SUB, tall), f32),
                pltpu.VMEM((2, 2 * SUB, tall), f32),
                pltpu.VMEM((2, depth + SUB, tall), f32),
                pltpu.VMEM((2, 3 * SUB, tall), f32),
                pltpu.VMEM((2, 2, side, tall), f32),
                pltpu.VMEM((2, 2, side, tall), f32),
                pltpu.VMEM((2, side, tall), f32),
                pltpu.VMEM((2, side, tall), f32),
                pltpu.VMEM((2, side, tall), f32),
                pltpu.VMEM((2, side, tall), f32),
                pltpu.VMEM((3, wide, tall), f32),
                pltpu.VMEM((n_row, 3, wide // n_row, tall), f32),
                pltpu.VMEM((n_row, 3, wide // n_row, tall), f32),
                pltpu.SMEM((3,), f32),
                pltpu.SMEM((3,), f32),
                pltpu.SMEM((3, 3), f32),
                pltpu.SemaphoreType.DMA((2, chunks)),
                pltpu.SemaphoreType.DMA((3,)),
                pltpu.SemaphoreType.DMA((2, 2, PARTS)),
                pltpu.SemaphoreType.DMA((2, 2, PARTS)),
                pltpu.SemaphoreType.DMA((2, PARTS)),
                pltpu.SemaphoreType.DMA((2, PARTS)),
                pltpu.SemaphoreType.DMA((12,)),
                pltpu.SemaphoreType.DMA((12,)),
                pltpu.SemaphoreType.DMA((n_row,)),
                pltpu.SemaphoreType.DMA((n_row,)),
            ],
            compiler_params=pltpu.CompilerParams(
                collective_id=0, has_side_effects=True, vmem_limit_bytes=VMEM_LIMIT
            ),
        )(*[
            pltpu.with_memory_space_constraint(a, pltpu.HBM)
            for a in (thermal_state, substance_label, thermal_coefficients, optical_thickness, substance_colours)
        ])
        return pl.pallas_call(
            deliver,
            out_shape=results,
            in_specs=[near, near],
            out_specs=(anywhere, anywhere),
            scratch_shapes=[pltpu.SemaphoreType.DMA((2,))],
            compiler_params=pltpu.CompilerParams(vmem_limit_bytes=VMEM_LIMIT),
        )(f, pic)

    placed = (P("row", "sx", "sy"), P("row", "sx", "sy"), P(), P(), P())
    return jax.shard_map(
        per_device,
        mesh=mesh,
        in_specs=placed,
        out_specs=(P("row", "sx", "sy"), P(None, ("sx", "row"), "sy")),
        check_vma=False,
    )
```

```python
import functools

import jax
import jax.numpy as jnp
from jax import lax
from jax.experimental import pallas as pl
from jax.experimental.pallas import tpu as pltpu
from jax.sharding import PartitionSpec as P

MESH = pl.DeviceIdType.MESH
SUB, LANES = 8, 128
FLUX, PACK, MARCH, PARTS = 4, 4, 6, 4
VMEM_LIMIT = 16 << 20


def kernel(
    sizes,
    t_hbm, lab_hbm, coef_hbm, thick_hbm, tint_hbm,
    f, pic_ref,
    u, d, h, ky, fy, lab, xs, xr, xs2, xr2, fx, ys, yr, ys2, yr2, mid, ib, rb,
    coef, thick, tint, lsem, csem, zsem1, zrec1, zsem2, zrec2, ssem, rsem, asem, bsem,
):
    n_sx, n_sy, n_row = sizes
    depth, wide = t_hbm.shape[0], t_hbm.shape[1]
    blocks = wide // SUB
    per_group = LANES // depth
    groups = blocks // per_group
    chunks = depth // SUB
    last = depth
    per_part = blocks // PARTS
    me, my_sx, my_sy = lax.axis_index("row"), lax.axis_index("sx"), lax.axis_index("sy")
    has_prev, has_next = me > 0, me < n_row - 1
    has_left, has_right = my_sy > 0, my_sy < n_sy - 1

    def load(j):
        at, to = pl.ds(SUB * j, SUB), pl.ds(SUB * j + 1, SUB)
        return (
            pltpu.make_async_copy(lab_hbm.at[at], lab.at[to], lsem.at[0, j]),
            pltpu.make_async_copy(t_hbm.at[at], u.at[to], lsem.at[1, j]),
        )

    load_c = pltpu.make_async_copy(coef_hbm, coef, csem.at[0])
    load_k = pltpu.make_async_copy(thick_hbm, thick, csem.at[1])
    load_p = pltpu.make_async_copy(tint_hbm, tint, csem.at[2])
    load_c.start()
    for j in range(chunks):
        for copy in load(j):
            copy.start()
    load_k.start()
    load_p.start()

    barrier = pltpu.get_barrier_semaphore()
    for o in range(1, n_row):
        pl.semaphore_signal(barrier, inc=1, device_id={"row": lax.rem(me + o, n_row)}, device_id_type=MESH)
    sx_next = lax.rem(my_sx + 1, n_sx)
    sx_prev = lax.rem(my_sx + n_sx - 1, n_sx)
    pl.semaphore_signal(barrier, inc=1, device_id={"sx": sx_next}, device_id_type=MESH)
    pl.semaphore_signal(barrier, inc=1, device_id={"sx": sx_prev}, device_id_type=MESH)

    @pl.when(has_left)
    def _():
        pl.semaphore_signal(barrier, inc=1, device_id={"sy": my_sy - 1}, device_id_type=MESH)

    @pl.when(has_right)
    def _():
        pl.semaphore_signal(barrier, inc=1, device_id={"sy": my_sy + 1}, device_id_type=MESH)

    lane = lax.broadcasted_iota(jnp.int32, (SUB, LANES), 1)
    sub = lax.broadcasted_iota(jnp.int32, (SUB, LANES), 0)
    at_ends = (lane == 0) | (lane == LANES - 1)
    is_even = (lane & 1) == 0
    pair = (((lane + 1) >> 1) & (LANES // 2 - 1), lane >> 1)
    zero = jnp.zeros((SUB, LANES), jnp.float32)
    one = jnp.ones((SUB, LANES), jnp.float32)

    def clear(cond, refs):
        @pl.when(jnp.logical_not(cond))
        def _():
            for r in refs:
                r[...] = jnp.zeros(r.shape, r.dtype)

    clear(has_prev, (u.at[0], d.at[0], h.at[0]))
    clear(has_next, (u.at[depth + 1], d.at[depth + 1], h.at[depth + 1]))
    clear(has_left, (yr.at[0], yr2.at[0]))
    clear(has_right, (yr.at[1], yr2.at[1]))

    to_next, to_prev = {"row": me + 1}, {"row": me - 1}
    to_right, to_left = {"sy": my_sy + 1}, {"sy": my_sy - 1}
    to_up, to_down = {"sx": sx_next}, {"sx": sx_prev}

    def only(cond, act):
        if cond is None:
            act()
        else:
            pl.when(cond)(act)

    def start(copies):
        for copy, sends, _ in copies:
            only(sends, copy.start)

    def arrive(copies):
        for copy, _, receives in copies:
            only(receives, copy.wait_recv)

    def left_here(copies):
        for copy, sends, _ in copies:
            only(sends, copy.wait_send)

    def remote(src, dst, send, recv, where):
        return pltpu.make_async_remote_copy(
            src_ref=src, dst_ref=dst, send_sem=send, recv_sem=recv, device_id=where, device_id_type=MESH
        )

    def z_first(p):
        at = pl.ds(SUB * per_part * p, SUB * per_part)
        got = []
        for i, (src, dst) in enumerate(((t_hbm, u), (lab_hbm, lab))):
            got.append((remote(src.at[depth - 1, at], dst.at[0, at], zsem1.at[0, i, p], zrec1.at[0, i, p], to_next),
                        has_next, has_prev))
            got.append((remote(src.at[0, at], dst.at[depth + 1, at], zsem1.at[1, i, p], zrec1.at[1, i, p], to_prev),
                        has_prev, has_next))
        return got

    def z_second(p):
        at = pl.ds(SUB * per_part * p, SUB * per_part)
        return [
            (remote(h.at[last, at], h.at[0, at], zsem2.at[0, p], zrec2.at[0, p], to_next), has_next, has_prev),
            (remote(h.at[1, at], h.at[depth + 1, at], zsem2.at[1, p], zrec2.at[1, p], to_prev), has_prev, has_next),
        ]

    def y_copies(src, dst, s):
        return [
            (remote(src.at[1], dst.at[0], ssem.at[s], rsem.at[s], to_right), has_right, has_left),
            (remote(src.at[0], dst.at[1], ssem.at[s + 1], rsem.at[s + 1], to_left), has_left, has_right),
        ]

    def x_copies(src, dst, s):
        return [
            (remote(src.at[1], dst.at[0], ssem.at[s], rsem.at[s], to_up), None, None),
            (remote(src.at[0], dst.at[1], ssem.at[s + 1], rsem.at[s + 1], to_down), None, None),
        ]

    y_first, x_first = y_copies(ys, yr, 0), x_copies(xs, xr, 2)
    y_second, x_second = y_copies(ys2, yr2, 4), x_copies(xs2, xr2, 6)

    def rows(xb):
        return pl.ds(SUB * xb, SUB)

    def spot(z0, xb):
        return depth * (xb % per_group) + z0

    def put(acc, v, z0, parity, xb):
        m = spot(z0, xb)
        at = (parity, xb // per_group)
        acc[at] = jnp.where(pair[parity] == m >> 1, pltpu.roll(v, m, 1), acc[at])

    def fresh():
        return {(p, g): zero for p in (0, 1) for g in range(groups)}

    def faces(acc, g):
        low = jnp.where(is_even, acc[0, g], acc[1, g])
        high = jnp.where(is_even, acc[1, g], acc[0, g])
        return low, pltpu.roll(high, 1, 1)

    load_c.wait()
    c0, c1, c2 = 0.5 * coef[0], 0.5 * coef[1], 0.5 * coef[2]

    def conduct(lb):
        return jnp.where(lb == 0, c0, jnp.where(lb == 1, c1, c2))

    def pack_first(j, carry):
        au, ad = [dict(c) for c in carry]
        for copy in load(j):
            copy.wait()
        for i in range(SUB):
            z0 = SUB * j + i
            for xb in range(blocks):
                v = u[z0 + 1, rows(xb), :]
                dv = conduct(lab[z0 + 1, rows(xb), :])
                d[z0 + 1, rows(xb), :] = dv
                put(au, v, z0, i % 2, xb)
                put(ad, dv, z0, i % 2, xb)
        return au, ad

    au, ad = lax.fori_loop(0, chunks, pack_first, (fresh(), fresh()))
    for g in range(groups):
        at = pl.ds(SUB * g, SUB)
        ys[0, 0, at, :], ys[1, 0, at, :] = faces(au, g)
        ys[0, 1, at, :], ys[1, 1, at, :] = faces(ad, g)

    def edge(ref, first, k, side):
        flat = ref.reshape(ref.shape[0] * wide, LANES)
        got = None
        for i in range(SUB):
            row = flat[pl.ds((first + SUB * k + i) * wide + (wide - 1) * side, SUB, stride=0), :]
            got = row if got is None else jnp.where(sub == i, row, got)
        return got

    for side in (0, 1):
        for k in range(chunks):
            for i, a in enumerate((u, d)):
                xs[side, i, pl.ds(SUB * k, SUB), :] = edge(a, 1, k, side)

    waits = n_row + 1 + has_left.astype(jnp.int32) + has_right.astype(jnp.int32)
    pl.semaphore_wait(barrier, waits)
    start(y_first)
    for p in range(PARTS):
        start(z_first(p))
    start(x_first)

    def flux(da, db, ub, ua):
        return (da + db) * (ub - ua)

    def plane(src, dst, shift, z, fz, high, first_step):
        nf, before = [], None
        for xb in range(blocks):
            a, k = src[z, rows(xb), :], d[z, rows(xb), :]
            if xb < blocks - 1:
                at = pl.ds(SUB * xb + 1, SUB)
                fxx = flux(k, d[z, at, :], src[z, at, :], a)
            else:
                fxx = flux(k, pltpu.roll(k, SUB - 1, 0), pltpu.roll(a, SUB - 1, 0), a)
                fxx = jnp.where(sub == SUB - 1, 0.0, fxx)
            turned = pltpu.roll(fxx, 1, 0)
            behind = jnp.where(sub == 0, 0.0 if before is None else before, turned)
            before = turned
            if first_step:
                kk = k + pltpu.roll(k, LANES - 1, 1)
                ky[z - 1, rows(xb), :] = kk
            else:
                kk = ky[z - 1, rows(xb), :]
            gy = kk * (pltpu.roll(a, LANES - 1, 1) - a)
            fy[z - 1, rows(xb), :] = gy
            total = (fxx - behind) + gy
            if high:
                nz = flux(k, d[z + 1, rows(xb), :], src[z + 1, rows(xb), :], a)
                total = total + (nz if fz is None else nz - fz[xb])
                nf.append(nz)
            elif fz is not None:
                total = total - fz[xb]
            dst[z + shift, rows(xb), :] = a + total
        return tuple(nf)

    def between(src, z):
        return tuple(
            flux(d[z, rows(xb), :], d[z + 1, rows(xb), :], src[z + 1, rows(xb), :], src[z, rows(xb), :])
            for xb in range(blocks)
        )

    def planes(src, dst, shift, begin, count, fz, first_step):
        def several(j, fz):
            for i in range(FLUX):
                fz = plane(src, dst, shift, begin + FLUX * j + i, fz, True, first_step)
            return fz

        return lax.fori_loop(0, count // FLUX, several, fz)

    fz = plane(u, h, 0, 1, None, True, True)
    fz = planes(u, h, 0, 2, depth - FLUX, fz, True)
    for z in range(depth - FLUX + 2, last):
        fz = plane(u, h, 0, z, fz, True, True)
    plane(u, h, 0, last, fz, False, True)

    def settle(dst, shift):
        def some(j, carry):
            for i in range(FLUX):
                z0 = FLUX * j + i
                for xb in range(blocks):
                    dst[z0 + shift, rows(xb), :] = dst[z0 + shift, rows(xb), :] - pltpu.roll(fy[z0, rows(xb), :], 1, 1)
            return carry

        lax.fori_loop(0, depth // FLUX, some, 0)

    def sweep(first, trips, count, body, carry):
        def some(j, carry):
            for i in range(count):
                carry = body(count * j + first + i, carry, (first + i) % 2)
            return carry

        return lax.fori_loop(0, trips, some, carry)

    settle(h, 1)

    def pack_h(z0, acc, parity, which=range(blocks)):
        acc = dict(acc)
        for xb in which:
            put(acc, h[z0 + 1, rows(xb), :], z0, parity, xb)
        return acc

    acc = dict(sweep(0, depth // PACK, PACK, pack_h, fresh()))

    def x_faces(own, came):
        for side in (0, 1):
            for k in range(chunks):
                at = pl.ds(SUB * k, SUB)
                fx[side, at, :] = flux(xs[side, 1, at, :], xr[side, 1, at, :], came(side, at), own(side, at))

    def y_faces(own, came):
        even, odd = [], []
        for g in range(groups):
            at = pl.ds(SUB * g, SUB)
            dl, dr, ul, ur = ys[0, 1, at, :], ys[1, 1, at, :], own(0, at), own(1, at)
            closed = flux(dl, dr, ul, ur)
            a = flux(dl, yr[0, 1, at, :], came(0, at), ul) + closed
            b = flux(dr, yr[1, 1, at, :], came(1, at), ur) - closed
            b = pltpu.roll(b, LANES - 1, 1)
            even.append(jnp.where(is_even, a, b))
            odd.append(jnp.where(is_even, b, a))
        return even, odd

    def with_faces(v, packed, z0, parity, xb):
        r = pltpu.roll(packed[parity][xb // per_group], (LANES - spot(z0, xb)) & (LANES - 1), 1)
        v = jnp.where(at_ends, v + r, v)
        if xb == 0:
            v = jnp.where(sub == 0, v + fx[0, pl.ds(z0, SUB, stride=0), :], v)
        if xb == blocks - 1:
            v = jnp.where(sub == SUB - 1, v + fx[1, pl.ds(z0, SUB, stride=0), :], v)
        return v

    arrive(x_first)
    x_faces(lambda s, at: xs[s, 0, at, :], lambda s, at: xr[s, 0, at, :])
    arrive(y_first)
    packed = y_faces(lambda s, at: ys[s, 0, at, :], lambda s, at: yr[s, 0, at, :])

    outer = ((0, 0, 0), (depth - 1, depth + 1, 1))
    brims = (0, blocks - 1)

    for p in range(PARTS):
        arrive(z_first(p))
        for (z0, ghost, parity), inside in zip(outer, (has_prev, has_next)):
            for xb in range(per_part * p, per_part * (p + 1)):
                at = rows(xb)
                dg = jnp.where(inside, conduct(lab[ghost, at, :]), 0.0)
                d[ghost, at, :] = dg
                fz = flux(d[z0 + 1, at, :], dg, u[ghost, at, :], u[z0 + 1, at, :])
                h[z0 + 1, at, :] = with_faces(h[z0 + 1, at, :] + fz, packed, z0, parity, xb)
        start(z_second(p))

    def fix_h(which):
        def body(z0, carry, parity):
            for xb in which:
                h[z0 + 1, rows(xb), :] = with_faces(h[z0 + 1, rows(xb), :], packed, z0, parity, xb)
            return carry

        return body

    sweep(1, 3, 10, fix_h(brims), 0)
    for p in (0, 1):
        for g in range(groups):
            acc[p, g] = acc[p, g] + packed[p][g]
    for z0, _, parity in outer:
        acc = pack_h(z0, acc, parity)
    acc = dict(sweep(1, 3, 10, functools.partial(pack_h, which=brims), acc))
    for g in range(groups):
        at = pl.ds(SUB * g, SUB)
        ys2[0, at, :], ys2[1, at, :] = faces(acc, g)
    start(y_second)
    for side in (0, 1):
        for k in range(chunks):
            xs2[side, pl.ds(SUB * k, SUB), :] = edge(h, 1, k, side)
    start(x_second)
    sweep(1, 5, 6, fix_h(range(1, blocks - 1)), 0)

    fz = plane(h, f, -1, 1, None, True, False)
    fz = planes(h, f, -1, 2, depth - FLUX, fz, False)
    for z in range(depth - FLUX + 2, last):
        fz = plane(h, f, -1, z, fz, True, False)
    plane(h, f, -1, last, fz, False, False)
    settle(f, 0)

    load_k.wait()
    scale = 0.5 / (depth * n_row)
    k0, k1, k2 = thick[0] * scale, thick[1] * scale, thick[2] * scale

    def opaque(v, lb):
        first, second = lb == 0, lb == 1
        half = jnp.where(first, k0, jnp.where(second, k1, k2))
        return half + half * jnp.tanh(0.5 * v), first, second

    arrive(x_second)
    x_faces(lambda s, at: xs2[s, at, :], lambda s, at: xr2[s, at, :])
    arrive(y_second)
    packed2 = y_faces(lambda s, at: ys2[s, at, :], lambda s, at: yr2[s, at, :])

    def march(z0, carry, parity):
        through, w0, w1 = [list(c) for c in carry]
        for xb in range(blocks):
            v = with_faces(f[z0, rows(xb), :], packed2, z0, parity, xb)
            f[z0, rows(xb), :] = v
            a, first, second = opaque(v, lab[z0 + 1, rows(xb), :])
            w = through[xb] * a
            through[xb] = through[xb] - w
            w0[xb] = w0[xb] + jnp.where(first, w, 0.0)
            w1[xb] = w1[xb] + jnp.where(second, w, 0.0)
        return tuple(tuple(c) for c in (through, w0, w1))

    state = sweep(1, (depth - 2) // MARCH, MARCH, march, ((one,) * blocks,) + ((zero,) * blocks,) * 2)
    for i in range(3):
        for xb in range(blocks):
            mid[i, rows(xb), :] = state[i][xb]
    for z0, _, parity in outer:
        for xb in range(blocks):
            f[z0, rows(xb), :] = with_faces(f[z0, rows(xb), :], packed2, z0, parity, xb)
    load_p.wait()

    def hand(dest):
        return pltpu.make_async_remote_copy(
            src_ref=ib.at[dest], dst_ref=rb.at[me], send_sem=asem.at[dest], recv_sem=bsem.at[me],
            device_id={"row": dest}, device_id_type=MESH,
        )

    for p in range(PARTS):
        arrive(z_second(p))
        for xb in range(per_part * p, per_part * (p + 1)):
            at = rows(xb)
            ends = []
            for z0, ghost, parity in outer:
                fz = flux(d[z0 + 1, at, :], d[ghost, at, :], h[ghost, at, :], h[z0 + 1, at, :])
                v = f[z0, at, :] + fz
                f[z0, at, :] = v
                ends.append(opaque(v, lab[z0 + 1, at, :]))
            (a, fa, fb), (b, ga, gb) = ends
            clear_a = 1.0 - a
            through = clear_a * mid[0, at, :]
            w = through * b
            ib[xb, 0] = jnp.where(fa, a, 0.0) + clear_a * mid[1, at, :] + jnp.where(ga, w, 0.0)
            ib[xb, 1] = jnp.where(fb, a, 0.0) + clear_a * mid[2, at, :] + jnp.where(gb, w, 0.0)
            ib[xb, 2] = through - w
        for dest in range(per_part * p, per_part * (p + 1)):
            pl.when(me != dest)(hand(dest).start)
    rb[me] = ib[me]

    for s in range(n_row):
        @pl.when(me != s)
        def _():
            pltpu.make_async_remote_copy(
                src_ref=ib.at[s], dst_ref=rb.at[s], send_sem=asem.at[s], recv_sem=bsem.at[s],
                device_id={"row": s}, device_id_type=MESH,
            ).wait_recv()

    through, w0, w1 = one, zero, zero
    for s in range(n_row):
        w0 = w0 + through * rb[s, 0]
        w1 = w1 + through * rb[s, 1]
        through = through * rb[s, 2]
    blocked = 1.0 - through
    w2 = (blocked - w0) - w1
    for c in range(3):
        pic_ref[c] = w0 * tint[0, c] + w1 * tint[1, c] + w2 * tint[2, c]
    pic_ref[3] = blocked

    for dest in range(n_row):
        pl.when(me != dest)(hand(dest).wait_send)
    for p in range(PARTS):
        left_here(z_first(p))
        left_here(z_second(p))
    for copies in (y_first, x_first, y_second, x_second):
        left_here(copies)


def deliver(f, pic, out, out_pic, sem):
    a = pltpu.make_async_copy(f, out, sem.at[0])
    b = pltpu.make_async_copy(pic, out_pic, sem.at[1])
    a.start()
    b.start()
    a.wait()
    b.wait()


def solution(mesh):
    sizes = (mesh.shape["sx"], mesh.shape["sy"], mesh.shape["row"])
    n_row = sizes[2]

    def per_device(thermal_state, substance_label, thermal_coefficients, optical_thickness, substance_colours):
        depth, wide, tall = thermal_state.shape
        f32 = jnp.float32
        side = depth * wide // LANES
        near = pl.BlockSpec(memory_space=pltpu.VMEM)
        anywhere = pl.BlockSpec(memory_space=pl.ANY)
        chunks = depth // SUB
        results = (
            jax.ShapeDtypeStruct((depth, wide, tall), f32),
            jax.ShapeDtypeStruct((4, wide // n_row, tall), f32),
        )
        f, pic = pl.pallas_call(
            functools.partial(kernel, sizes),
            out_shape=results,
            in_specs=[anywhere] * 5,
            out_specs=(near, near),
            scratch_shapes=[
                pltpu.VMEM((depth + 2, wide, tall), f32),
                pltpu.VMEM((depth + 2, wide, tall), f32),
                pltpu.VMEM((depth + 2, wide, tall), f32),
                pltpu.VMEM((depth, wide, tall), f32),
                pltpu.VMEM((depth, wide, tall), f32),
                pltpu.VMEM((depth + 2, wide, tall), jnp.int32),
                pltpu.VMEM((2, 2, depth, tall), f32),
                pltpu.VMEM((2, 2, depth, tall), f32),
                pltpu.VMEM((2, depth, tall), f32),
                pltpu.VMEM((2, depth, tall), f32),
                pltpu.VMEM((2, depth + SUB, tall), f32),
                pltpu.VMEM((2, 2, side, tall), f32),
                pltpu.VMEM((2, 2, side, tall), f32),
                pltpu.VMEM((2, side, tall), f32),
                pltpu.VMEM((2, side, tall), f32),
                pltpu.VMEM((3, wide, tall), f32),
                pltpu.VMEM((n_row, 3, wide // n_row, tall), f32),
                pltpu.VMEM((n_row, 3, wide // n_row, tall), f32),
                pltpu.SMEM((3,), f32),
                pltpu.SMEM((3,), f32),
                pltpu.SMEM((3, 3), f32),
                pltpu.SemaphoreType.DMA((2, chunks)),
                pltpu.SemaphoreType.DMA((3,)),
                pltpu.SemaphoreType.DMA((2, 2, PARTS)),
                pltpu.SemaphoreType.DMA((2, 2, PARTS)),
                pltpu.SemaphoreType.DMA((2, PARTS)),
                pltpu.SemaphoreType.DMA((2, PARTS)),
                pltpu.SemaphoreType.DMA((8,)),
                pltpu.SemaphoreType.DMA((8,)),
                pltpu.SemaphoreType.DMA((n_row,)),
                pltpu.SemaphoreType.DMA((n_row,)),
            ],
            compiler_params=pltpu.CompilerParams(
                collective_id=0, has_side_effects=True, vmem_limit_bytes=VMEM_LIMIT
            ),
        )(*[
            pltpu.with_memory_space_constraint(a, pltpu.HBM)
            for a in (thermal_state, substance_label, thermal_coefficients, optical_thickness, substance_colours)
        ])
        return pl.pallas_call(
            deliver,
            out_shape=results,
            in_specs=[near, near],
            out_specs=(anywhere, anywhere),
            scratch_shapes=[pltpu.SemaphoreType.DMA((2,))],
            compiler_params=pltpu.CompilerParams(vmem_limit_bytes=VMEM_LIMIT),
        )(f, pic)

    placed = (P("row", "sx", "sy"), P("row", "sx", "sy"), P(), P(), P())
    return jax.shard_map(
        per_device,
        mesh=mesh,
        in_specs=placed,
        out_specs=(P("row", "sx", "sy"), P(None, ("sx", "row"), "sy")),
        check_vma=False,
    )
```

```python
import functools

import jax
import jax.numpy as jnp
from jax import lax
from jax.experimental import pallas as pl
from jax.experimental.pallas import tpu as pltpu
from jax.sharding import PartitionSpec as P

MESH = pl.DeviceIdType.MESH
SUB, LANES = 8, 128
FLUX, PACK, MARCH, PARTS = 4, 4, 6, 4
VMEM_LIMIT = 16 << 20


def kernel(
    sizes,
    t_hbm, lab_hbm, coef_hbm, thick_hbm, tint_hbm,
    f, pic_ref,
    u, d, h, ky, fy, lab, xs, xr, xs2, xr2, fx, ys, yr, ys2, yr2, mid, ib, rb,
    coef, thick, tint, lsem, csem, zsem1, zrec1, zsem2, zrec2, ssem, rsem, asem, bsem, hello,
):
    n_sx, n_sy, n_row = sizes
    depth, wide = t_hbm.shape[0], t_hbm.shape[1]
    blocks = wide // SUB
    per_group = LANES // depth
    groups = blocks // per_group
    chunks = depth // SUB
    last = depth
    per_part = blocks // PARTS
    me, my_sx, my_sy = lax.axis_index("row"), lax.axis_index("sx"), lax.axis_index("sy")
    has_prev, has_next = me > 0, me < n_row - 1
    has_left, has_right = my_sy > 0, my_sy < n_sy - 1

    def load(j):
        at, to = pl.ds(SUB * j, SUB), pl.ds(SUB * j + 1, SUB)
        return (
            pltpu.make_async_copy(lab_hbm.at[at], lab.at[to], lsem.at[0, j]),
            pltpu.make_async_copy(t_hbm.at[at], u.at[to], lsem.at[1, j]),
        )

    load_c = pltpu.make_async_copy(coef_hbm, coef, csem.at[0])
    load_k = pltpu.make_async_copy(thick_hbm, thick, csem.at[1])
    load_p = pltpu.make_async_copy(tint_hbm, tint, csem.at[2])
    load_c.start()
    for j in range(chunks):
        for copy in load(j):
            copy.start()
    load_k.start()
    load_p.start()

    sx_next = lax.rem(my_sx + 1, n_sx)
    sx_prev = lax.rem(my_sx + n_sx - 1, n_sx)
    to_next, to_prev = {"row": me + 1}, {"row": me - 1}
    to_right, to_left = {"sy": my_sy + 1}, {"sy": my_sy - 1}
    to_up, to_down = {"sx": sx_next}, {"sx": sx_prev}

    def only(cond, act):
        if cond is None:
            act()
        else:
            pl.when(cond)(act)

    barrier = pltpu.get_barrier_semaphore()
    near = (
        (has_prev, to_prev), (has_next, to_next), (has_left, to_left), (has_right, to_right),
        (None, to_up), (None, to_down),
    )
    for there, where in near:
        only(there, functools.partial(pl.semaphore_signal, barrier, inc=1, device_id=where, device_id_type=MESH))

    lane = lax.broadcasted_iota(jnp.int32, (SUB, LANES), 1)
    sub = lax.broadcasted_iota(jnp.int32, (SUB, LANES), 0)
    at_ends = (lane == 0) | (lane == LANES - 1)
    is_even = (lane & 1) == 0
    pair = (((lane + 1) >> 1) & (LANES // 2 - 1), lane >> 1)
    zero = jnp.zeros((SUB, LANES), jnp.float32)
    one = jnp.ones((SUB, LANES), jnp.float32)

    def clear(cond, refs):
        @pl.when(jnp.logical_not(cond))
        def _():
            for r in refs:
                r[...] = jnp.zeros(r.shape, r.dtype)

    clear(has_prev, (u.at[0], d.at[0], h.at[0]))
    clear(has_next, (u.at[depth + 1], d.at[depth + 1], h.at[depth + 1]))
    clear(has_left, (yr.at[0], yr2.at[0]))
    clear(has_right, (yr.at[1], yr2.at[1]))

    def start(copies):
        for copy, sends, _ in copies:
            only(sends, copy.start)

    def arrive(copies):
        for copy, _, receives in copies:
            only(receives, copy.wait_recv)

    def left_here(copies):
        for copy, sends, _ in copies:
            only(sends, copy.wait_send)

    def remote(src, dst, send, recv, where):
        return pltpu.make_async_remote_copy(
            src_ref=src, dst_ref=dst, send_sem=send, recv_sem=recv, device_id=where, device_id_type=MESH
        )

    def z_first(p):
        at = pl.ds(SUB * per_part * p, SUB * per_part)
        got = []
        for i, (src, dst) in enumerate(((t_hbm, u), (lab_hbm, lab))):
            got.append((remote(src.at[depth - 1, at], dst.at[0, at], zsem1.at[0, i, p], zrec1.at[0, i, p], to_next),
                        has_next, has_prev))
            got.append((remote(src.at[0, at], dst.at[depth + 1, at], zsem1.at[1, i, p], zrec1.at[1, i, p], to_prev),
                        has_prev, has_next))
        return got

    def z_second(p):
        at = pl.ds(SUB * per_part * p, SUB * per_part)
        return [
            (remote(h.at[last, at], h.at[0, at], zsem2.at[0, p], zrec2.at[0, p], to_next), has_next, has_prev),
            (remote(h.at[1, at], h.at[depth + 1, at], zsem2.at[1, p], zrec2.at[1, p], to_prev), has_prev, has_next),
        ]

    def y_copies(src, dst, s):
        return [
            (remote(src.at[1], dst.at[0], ssem.at[s], rsem.at[s], to_right), has_right, has_left),
            (remote(src.at[0], dst.at[1], ssem.at[s + 1], rsem.at[s + 1], to_left), has_left, has_right),
        ]

    def x_copies(src, dst, s):
        return [
            (remote(src.at[1], dst.at[0], ssem.at[s], rsem.at[s], to_up), None, None),
            (remote(src.at[0], dst.at[1], ssem.at[s + 1], rsem.at[s + 1], to_down), None, None),
        ]

    y_first, x_first = y_copies(ys, yr, 0), x_copies(xs, xr, 2)
    y_second, x_second = y_copies(ys2, yr2, 4), x_copies(xs2, xr2, 6)

    pl.semaphore_wait(barrier, 2 + sum(c.astype(jnp.int32) for c in (has_prev, has_next, has_left, has_right)))
    for p in range(PARTS):
        start(z_first(p))

    def greet(i, apart, act):
        for side, there, where in ((0, me >= apart, me - apart), (1, me + apart < n_row, me + apart)):
            @pl.when(there)
            def _():
                if act == "signal":
                    pl.semaphore_signal(hello.at[i, 1 - side], inc=1, device_id={"row": where}, device_id_type=MESH)
                else:
                    pl.semaphore_wait(hello.at[i, side], 1)

    def rows(xb):
        return pl.ds(SUB * xb, SUB)

    def spot(z0, xb):
        return depth * (xb % per_group) + z0

    def put(acc, v, z0, parity, xb):
        m = spot(z0, xb)
        at = (parity, xb // per_group)
        acc[at] = jnp.where(pair[parity] == m >> 1, pltpu.roll(v, m, 1), acc[at])

    def fresh():
        return {(p, g): zero for p in (0, 1) for g in range(groups)}

    def faces(acc, g):
        low = jnp.where(is_even, acc[0, g], acc[1, g])
        high = jnp.where(is_even, acc[1, g], acc[0, g])
        return low, pltpu.roll(high, 1, 1)

    load_c.wait()
    c0, c1, c2 = 0.5 * coef[0], 0.5 * coef[1], 0.5 * coef[2]

    def conduct(lb):
        return jnp.where(lb == 0, c0, jnp.where(lb == 1, c1, c2))

    def pack_first(j, carry):
        au, ad = [dict(c) for c in carry]
        for copy in load(j):
            copy.wait()
        for i in range(SUB):
            z0 = SUB * j + i
            for xb in range(blocks):
                v = u[z0 + 1, rows(xb), :]
                dv = conduct(lab[z0 + 1, rows(xb), :])
                d[z0 + 1, rows(xb), :] = dv
                put(au, v, z0, i % 2, xb)
                put(ad, dv, z0, i % 2, xb)
        return au, ad

    au, ad = lax.fori_loop(0, chunks, pack_first, (fresh(), fresh()))
    for g in range(groups):
        at = pl.ds(SUB * g, SUB)
        ys[0, 0, at, :], ys[1, 0, at, :] = faces(au, g)
        ys[0, 1, at, :], ys[1, 1, at, :] = faces(ad, g)
    start(y_first)

    def edge(ref, first, k, side):
        flat = ref.reshape(ref.shape[0] * wide, LANES)
        got = None
        for i in range(SUB):
            row = flat[pl.ds((first + SUB * k + i) * wide + (wide - 1) * side, SUB, stride=0), :]
            got = row if got is None else jnp.where(sub == i, row, got)
        return got

    for side in (0, 1):
        for k in range(chunks):
            for i, a in enumerate((u, d)):
                xs[side, i, pl.ds(SUB * k, SUB), :] = edge(a, 1, k, side)

    start(x_first)

    def flux(da, db, ub, ua):
        return (da + db) * (ub - ua)

    def plane(src, dst, shift, z, fz, high, first_step):
        nf, before = [], None
        for xb in range(blocks):
            a, k = src[z, rows(xb), :], d[z, rows(xb), :]
            if xb < blocks - 1:
                at = pl.ds(SUB * xb + 1, SUB)
                fxx = flux(k, d[z, at, :], src[z, at, :], a)
            else:
                fxx = flux(k, pltpu.roll(k, SUB - 1, 0), pltpu.roll(a, SUB - 1, 0), a)
                fxx = jnp.where(sub == SUB - 1, 0.0, fxx)
            turned = pltpu.roll(fxx, 1, 0)
            behind = jnp.where(sub == 0, 0.0 if before is None else before, turned)
            before = turned
            if first_step:
                kk = k + pltpu.roll(k, LANES - 1, 1)
                ky[z - 1, rows(xb), :] = kk
            else:
                kk = ky[z - 1, rows(xb), :]
            gy = kk * (pltpu.roll(a, LANES - 1, 1) - a)
            fy[z - 1, rows(xb), :] = gy
            total = (fxx - behind) + gy
            if high:
                nz = flux(k, d[z + 1, rows(xb), :], src[z + 1, rows(xb), :], a)
                total = total + (nz if fz is None else nz - fz[xb])
                nf.append(nz)
            elif fz is not None:
                total = total - fz[xb]
            dst[z + shift, rows(xb), :] = a + total
        return tuple(nf)

    def between(src, z):
        return tuple(
            flux(d[z, rows(xb), :], d[z + 1, rows(xb), :], src[z + 1, rows(xb), :], src[z, rows(xb), :])
            for xb in range(blocks)
        )

    def planes(src, dst, shift, begin, count, fz, first_step):
        def several(j, fz):
            for i in range(FLUX):
                fz = plane(src, dst, shift, begin + FLUX * j + i, fz, True, first_step)
            return fz

        return lax.fori_loop(0, count // FLUX, several, fz)

    fz = plane(u, h, 0, 1, None, True, True)
    fz = planes(u, h, 0, 2, depth - FLUX, fz, True)
    for z in range(depth - FLUX + 2, last):
        fz = plane(u, h, 0, z, fz, True, True)
    plane(u, h, 0, last, fz, False, True)

    def settle(dst, shift):
        def some(j, carry):
            for i in range(FLUX):
                z0 = FLUX * j + i
                for xb in range(blocks):
                    dst[z0 + shift, rows(xb), :] = dst[z0 + shift, rows(xb), :] - pltpu.roll(fy[z0, rows(xb), :], 1, 1)
            return carry

        lax.fori_loop(0, depth // FLUX, some, 0)

    def sweep(first, trips, count, body, carry):
        def some(j, carry):
            for i in range(count):
                carry = body(count * j + first + i, carry, (first + i) % 2)
            return carry

        return lax.fori_loop(0, trips, some, carry)

    settle(h, 1)

    def pack_h(z0, acc, parity, which=range(blocks)):
        acc = dict(acc)
        for xb in which:
            put(acc, h[z0 + 1, rows(xb), :], z0, parity, xb)
        return acc

    acc = dict(sweep(0, depth // PACK, PACK, pack_h, fresh()))

    def x_faces(own, came):
        for side in (0, 1):
            for k in range(chunks):
                at = pl.ds(SUB * k, SUB)
                fx[side, at, :] = flux(xs[side, 1, at, :], xr[side, 1, at, :], came(side, at), own(side, at))

    def y_faces(own, came):
        even, odd = [], []
        for g in range(groups):
            at = pl.ds(SUB * g, SUB)
            dl, dr, ul, ur = ys[0, 1, at, :], ys[1, 1, at, :], own(0, at), own(1, at)
            closed = flux(dl, dr, ul, ur)
            a = flux(dl, yr[0, 1, at, :], came(0, at), ul) + closed
            b = flux(dr, yr[1, 1, at, :], came(1, at), ur) - closed
            b = pltpu.roll(b, LANES - 1, 1)
            even.append(jnp.where(is_even, a, b))
            odd.append(jnp.where(is_even, b, a))
        return even, odd

    def with_faces(v, packed, z0, parity, xb):
        r = pltpu.roll(packed[parity][xb // per_group], (LANES - spot(z0, xb)) & (LANES - 1), 1)
        v = jnp.where(at_ends, v + r, v)
        if xb == 0:
            v = jnp.where(sub == 0, v + fx[0, pl.ds(z0, SUB, stride=0), :], v)
        if xb == blocks - 1:
            v = jnp.where(sub == SUB - 1, v + fx[1, pl.ds(z0, SUB, stride=0), :], v)
        return v

    arrive(x_first)
    x_faces(lambda s, at: xs[s, 0, at, :], lambda s, at: xr[s, 0, at, :])
    arrive(y_first)
    packed = y_faces(lambda s, at: ys[s, 0, at, :], lambda s, at: yr[s, 0, at, :])

    outer = ((0, 0, 0), (depth - 1, depth + 1, 1))
    brims = (0, blocks - 1)

    for p in range(PARTS):
        arrive(z_first(p))
        for (z0, ghost, parity), inside in zip(outer, (has_prev, has_next)):
            for xb in range(per_part * p, per_part * (p + 1)):
                at = rows(xb)
                dg = jnp.where(inside, conduct(lab[ghost, at, :]), 0.0)
                d[ghost, at, :] = dg
                fz = flux(d[z0 + 1, at, :], dg, u[ghost, at, :], u[z0 + 1, at, :])
                h[z0 + 1, at, :] = with_faces(h[z0 + 1, at, :] + fz, packed, z0, parity, xb)
        start(z_second(p))
    greet(0, 2, "signal")

    def fix_h(which):
        def body(z0, carry, parity):
            for xb in which:
                h[z0 + 1, rows(xb), :] = with_faces(h[z0 + 1, rows(xb), :], packed, z0, parity, xb)
            return carry

        return body

    sweep(1, 3, 10, fix_h(brims), 0)
    for p in (0, 1):
        for g in range(groups):
            acc[p, g] = acc[p, g] + packed[p][g]
    for z0, _, parity in outer:
        acc = pack_h(z0, acc, parity)
    acc = dict(sweep(1, 3, 10, functools.partial(pack_h, which=brims), acc))
    for g in range(groups):
        at = pl.ds(SUB * g, SUB)
        ys2[0, at, :], ys2[1, at, :] = faces(acc, g)
    start(y_second)
    for side in (0, 1):
        for k in range(chunks):
            xs2[side, pl.ds(SUB * k, SUB), :] = edge(h, 1, k, side)
    start(x_second)
    sweep(1, 5, 6, fix_h(range(1, blocks - 1)), 0)
    greet(0, 2, "wait")
    greet(1, 4, "signal")

    fz = plane(h, f, -1, 1, None, True, False)
    fz = planes(h, f, -1, 2, depth - FLUX, fz, False)
    for z in range(depth - FLUX + 2, last):
        fz = plane(h, f, -1, z, fz, True, False)
    plane(h, f, -1, last, fz, False, False)
    settle(f, 0)

    load_k.wait()
    scale = 0.5 / (depth * n_row)
    k0, k1, k2 = thick[0] * scale, thick[1] * scale, thick[2] * scale

    def opaque(v, lb):
        first, second = lb == 0, lb == 1
        half = jnp.where(first, k0, jnp.where(second, k1, k2))
        return half + half * jnp.tanh(0.5 * v), first, second

    arrive(x_second)
    x_faces(lambda s, at: xs2[s, at, :], lambda s, at: xr2[s, at, :])
    arrive(y_second)
    packed2 = y_faces(lambda s, at: ys2[s, at, :], lambda s, at: yr2[s, at, :])

    def march(z0, carry, parity):
        through, w0, w1 = [list(c) for c in carry]
        for xb in range(blocks):
            v = with_faces(f[z0, rows(xb), :], packed2, z0, parity, xb)
            f[z0, rows(xb), :] = v
            a, first, second = opaque(v, lab[z0 + 1, rows(xb), :])
            w = through[xb] * a
            through[xb] = through[xb] - w
            w0[xb] = w0[xb] + jnp.where(first, w, 0.0)
            w1[xb] = w1[xb] + jnp.where(second, w, 0.0)
        return tuple(tuple(c) for c in (through, w0, w1))

    state = sweep(1, (depth - 2) // MARCH, MARCH, march, ((one,) * blocks,) + ((zero,) * blocks,) * 2)
    for i in range(3):
        for xb in range(blocks):
            mid[i, rows(xb), :] = state[i][xb]
    for z0, _, parity in outer:
        for xb in range(blocks):
            f[z0, rows(xb), :] = with_faces(f[z0, rows(xb), :], packed2, z0, parity, xb)
    load_p.wait()

    for p in range(PARTS):
        arrive(z_second(p))
    for xb in range(blocks):
        at = rows(xb)
        ends = []
        for z0, ghost, parity in outer:
            fz = flux(d[z0 + 1, at, :], d[ghost, at, :], h[ghost, at, :], h[z0 + 1, at, :])
            v = f[z0, at, :] + fz
            f[z0, at, :] = v
            ends.append(opaque(v, lab[z0 + 1, at, :]))
        (a, fa, fb), (b, ga, gb) = ends
        clear_a = 1.0 - a
        through = clear_a * mid[0, at, :]
        w = through * b
        ib[xb, 0] = jnp.where(fa, a, 0.0) + clear_a * mid[1, at, :] + jnp.where(ga, w, 0.0)
        ib[xb, 1] = jnp.where(fb, a, 0.0) + clear_a * mid[2, at, :] + jnp.where(gb, w, 0.0)
        ib[xb, 2] = through - w

    def hand(o):
        dest = lax.rem(me + o, n_row)
        return pltpu.make_async_remote_copy(
            src_ref=ib.at[dest], dst_ref=rb.at[me], send_sem=asem.at[o], recv_sem=bsem.at[me],
            device_id={"row": dest}, device_id_type=MESH,
        )

    greet(1, 4, "wait")
    half = n_row // 2
    order = sorted(range(1, n_row), key=lambda o: abs(o - half))
    for o in order:
        hand(o).start()
    rb[me] = ib[me]

    for s in range(n_row):
        @pl.when(me != s)
        def _():
            pltpu.make_async_remote_copy(
                src_ref=ib.at[s], dst_ref=rb.at[s], send_sem=asem.at[0], recv_sem=bsem.at[s],
                device_id={"row": s}, device_id_type=MESH,
            ).wait_recv()

    through, w0, w1 = one, zero, zero
    for s in range(n_row):
        w0 = w0 + through * rb[s, 0]
        w1 = w1 + through * rb[s, 1]
        through = through * rb[s, 2]
    blocked = 1.0 - through
    w2 = (blocked - w0) - w1
    for c in range(3):
        pic_ref[c] = w0 * tint[0, c] + w1 * tint[1, c] + w2 * tint[2, c]
    pic_ref[3] = blocked

    for o in order:
        hand(o).wait_send()
    for p in range(PARTS):
        left_here(z_first(p))
        left_here(z_second(p))
    for copies in (y_first, x_first, y_second, x_second):
        left_here(copies)


def deliver(f, pic, out, out_pic, sem):
    a = pltpu.make_async_copy(f, out, sem.at[0])
    b = pltpu.make_async_copy(pic, out_pic, sem.at[1])
    a.start()
    b.start()
    a.wait()
    b.wait()


def solution(mesh):
    sizes = (mesh.shape["sx"], mesh.shape["sy"], mesh.shape["row"])
    n_row = sizes[2]

    def per_device(thermal_state, substance_label, thermal_coefficients, optical_thickness, substance_colours):
        depth, wide, tall = thermal_state.shape
        f32 = jnp.float32
        side = depth * wide // LANES
        near = pl.BlockSpec(memory_space=pltpu.VMEM)
        anywhere = pl.BlockSpec(memory_space=pl.ANY)
        chunks = depth // SUB
        results = (
            jax.ShapeDtypeStruct((depth, wide, tall), f32),
            jax.ShapeDtypeStruct((4, wide // n_row, tall), f32),
        )
        f, pic = pl.pallas_call(
            functools.partial(kernel, sizes),
            out_shape=results,
            in_specs=[anywhere] * 5,
            out_specs=(near, near),
            scratch_shapes=[
                pltpu.VMEM((depth + 2, wide, tall), f32),
                pltpu.VMEM((depth + 2, wide, tall), f32),
                pltpu.VMEM((depth + 2, wide, tall), f32),
                pltpu.VMEM((depth, wide, tall), f32),
                pltpu.VMEM((depth, wide, tall), f32),
                pltpu.VMEM((depth + 2, wide, tall), jnp.int32),
                pltpu.VMEM((2, 2, depth, tall), f32),
                pltpu.VMEM((2, 2, depth, tall), f32),
                pltpu.VMEM((2, depth, tall), f32),
                pltpu.VMEM((2, depth, tall), f32),
                pltpu.VMEM((2, depth + SUB, tall), f32),
                pltpu.VMEM((2, 2, side, tall), f32),
                pltpu.VMEM((2, 2, side, tall), f32),
                pltpu.VMEM((2, side, tall), f32),
                pltpu.VMEM((2, side, tall), f32),
                pltpu.VMEM((3, wide, tall), f32),
                pltpu.VMEM((n_row, 3, wide // n_row, tall), f32),
                pltpu.VMEM((n_row, 3, wide // n_row, tall), f32),
                pltpu.SMEM((3,), f32),
                pltpu.SMEM((3,), f32),
                pltpu.SMEM((3, 3), f32),
                pltpu.SemaphoreType.DMA((2, chunks)),
                pltpu.SemaphoreType.DMA((3,)),
                pltpu.SemaphoreType.DMA((2, 2, PARTS)),
                pltpu.SemaphoreType.DMA((2, 2, PARTS)),
                pltpu.SemaphoreType.DMA((2, PARTS)),
                pltpu.SemaphoreType.DMA((2, PARTS)),
                pltpu.SemaphoreType.DMA((8,)),
                pltpu.SemaphoreType.DMA((8,)),
                pltpu.SemaphoreType.DMA((n_row,)),
                pltpu.SemaphoreType.DMA((n_row,)),
                pltpu.SemaphoreType.REGULAR((2, 2)),
            ],
            compiler_params=pltpu.CompilerParams(
                collective_id=0, has_side_effects=True, vmem_limit_bytes=VMEM_LIMIT
            ),
        )(*[
            pltpu.with_memory_space_constraint(a, pltpu.HBM)
            for a in (thermal_state, substance_label, thermal_coefficients, optical_thickness, substance_colours)
        ])
        return pl.pallas_call(
            deliver,
            out_shape=results,
            in_specs=[near, near],
            out_specs=(anywhere, anywhere),
            scratch_shapes=[pltpu.SemaphoreType.DMA((2,))],
            compiler_params=pltpu.CompilerParams(vmem_limit_bytes=VMEM_LIMIT),
        )(f, pic)

    placed = (P("row", "sx", "sy"), P("row", "sx", "sy"), P(), P(), P())
    return jax.shard_map(
        per_device,
        mesh=mesh,
        in_specs=placed,
        out_specs=(P("row", "sx", "sy"), P(None, ("sx", "row"), "sy")),
        check_vma=False,
    )
```

```python
import functools

import jax
import jax.numpy as jnp
from jax import lax
from jax.experimental import pallas as pl
from jax.experimental.pallas import tpu as pltpu
from jax.sharding import PartitionSpec as P

MESH = pl.DeviceIdType.MESH
SUB, LANES = 8, 128
FLUX, PACK, MARCH, PARTS = 4, 4, 6, 2
VMEM_LIMIT = 16 << 20


def kernel(
    sizes,
    t_hbm, lab_hbm, coef_hbm, thick_hbm, tint_hbm,
    f, pic_ref,
    u, d, h, ky, fy, lab, xs, xr, xs2, xr2, fx, ys, yr, ys2, yr2, mid, ib, rb,
    coef, thick, tint, lsem, csem, zsem1, zrec1, zsem2, zrec2, ssem, rsem, asem, bsem, hello, above,
):
    n_sx, n_sy, n_row = sizes
    depth, wide = t_hbm.shape[0], t_hbm.shape[1]
    blocks = wide // SUB
    per_group = LANES // depth
    groups = blocks // per_group
    chunks = depth // SUB
    last = depth
    per_part = blocks // PARTS
    me, my_sx, my_sy = lax.axis_index("row"), lax.axis_index("sx"), lax.axis_index("sy")
    has_prev, has_next = me > 0, me < n_row - 1
    has_left, has_right = my_sy > 0, my_sy < n_sy - 1

    def load(j):
        at, to = pl.ds(SUB * j, SUB), pl.ds(SUB * j + 1, SUB)
        return (
            pltpu.make_async_copy(lab_hbm.at[at], lab.at[to], lsem.at[0, j]),
            pltpu.make_async_copy(t_hbm.at[at], u.at[to], lsem.at[1, j]),
        )

    load_c = pltpu.make_async_copy(coef_hbm, coef, csem.at[0])
    load_k = pltpu.make_async_copy(thick_hbm, thick, csem.at[1])
    load_p = pltpu.make_async_copy(tint_hbm, tint, csem.at[2])
    load_c.start()
    for j in range(chunks):
        for copy in load(j):
            copy.start()
    load_k.start()
    load_p.start()

    sx_next = lax.rem(my_sx + 1, n_sx)
    sx_prev = lax.rem(my_sx + n_sx - 1, n_sx)
    to_next, to_prev = {"row": me + 1}, {"row": me - 1}
    to_right, to_left = {"sy": my_sy + 1}, {"sy": my_sy - 1}
    to_up, to_down = {"sx": sx_next}, {"sx": sx_prev}

    def only(cond, act):
        if cond is None:
            act()
        else:
            pl.when(cond)(act)

    barrier = pltpu.get_barrier_semaphore()
    near = (
        (has_prev, to_prev), (has_next, to_next), (has_right, to_right), (None, to_up), (None, to_down),
    )
    for there, where in near:
        only(there, functools.partial(pl.semaphore_signal, barrier, inc=1, device_id=where, device_id_type=MESH))

    lane = lax.broadcasted_iota(jnp.int32, (SUB, LANES), 1)
    sub = lax.broadcasted_iota(jnp.int32, (SUB, LANES), 0)
    at_ends = (lane == 0) | (lane == LANES - 1)
    is_even = (lane & 1) == 0
    pair = (((lane + 1) >> 1) & (LANES // 2 - 1), lane >> 1)
    zero = jnp.zeros((SUB, LANES), jnp.float32)
    one = jnp.ones((SUB, LANES), jnp.float32)

    def clear(cond, refs):
        @pl.when(jnp.logical_not(cond))
        def _():
            for r in refs:
                r[...] = jnp.zeros(r.shape, r.dtype)

    clear(has_prev, (u.at[0], d.at[0], h.at[0]))
    clear(has_next, (u.at[depth + 1], d.at[depth + 1], h.at[depth + 1]))
    clear(has_left, (yr.at[0], yr2.at[0]))
    clear(has_right, (yr.at[1], yr2.at[1]))

    def start(copies):
        for copy, sends, _ in copies:
            only(sends, copy.start)

    def arrive(copies):
        for copy, _, receives in copies:
            only(receives, copy.wait_recv)

    def left_here(copies):
        for copy, sends, _ in copies:
            only(sends, copy.wait_send)

    def remote(src, dst, send, recv, where):
        return pltpu.make_async_remote_copy(
            src_ref=src, dst_ref=dst, send_sem=send, recv_sem=recv, device_id=where, device_id_type=MESH
        )

    def z_first(p):
        at = pl.ds(SUB * per_part * p, SUB * per_part)
        got = []
        for i, (src, dst) in enumerate(((t_hbm, u), (lab_hbm, lab))):
            got.append((remote(src.at[depth - 1, at], dst.at[0, at], zsem1.at[0, i, p], zrec1.at[0, i, p], to_next),
                        has_next, has_prev))
            got.append((remote(src.at[0, at], dst.at[depth + 1, at], zsem1.at[1, i, p], zrec1.at[1, i, p], to_prev),
                        has_prev, has_next))
        return got

    def z_second(p):
        at = pl.ds(SUB * per_part * p, SUB * per_part)
        return [
            (remote(h.at[last, at], h.at[0, at], zsem2.at[0, p], zrec2.at[0, p], to_next), has_next, has_prev),
            (remote(h.at[1, at], h.at[depth + 1, at], zsem2.at[1, p], zrec2.at[1, p], to_prev), has_prev, has_next),
        ]

    def y_copies(src, dst, s):
        return (
            [(remote(src.at[0], dst.at[1], ssem.at[s + 1], rsem.at[s + 1], to_left), has_left, has_right)],
            [(remote(src.at[1], dst.at[0], ssem.at[s], rsem.at[s], to_right), has_right, has_left)],
        )

    def x_copies(src, dst, s):
        return [
            (remote(src.at[1], dst.at[0], ssem.at[s], rsem.at[s], to_up), None, None),
            (remote(src.at[0], dst.at[1], ssem.at[s + 1], rsem.at[s + 1], to_down), None, None),
        ]

    (y_down, y_up), x_first = y_copies(ys, yr, 0), x_copies(xs, xr, 2)
    (y_down2, y_up2), x_second = y_copies(ys2, yr2, 4), x_copies(xs2, xr2, 6)

    pl.semaphore_wait(barrier, 2 + sum(c.astype(jnp.int32) for c in (has_prev, has_next, has_left)))
    only(has_left, functools.partial(pl.semaphore_signal, above, inc=1, device_id=to_left, device_id_type=MESH))
    waits_long = has_right & (my_sy == n_sy // 2 - 1)
    waits_short = has_right & (my_sy != n_sy // 2 - 1)

    def greet(i, apart, act):
        for side, there, where in ((0, me >= apart, me - apart), (1, me + apart < n_row, me + apart)):
            @pl.when(there)
            def _():
                if act == "signal":
                    pl.semaphore_signal(hello.at[i, 1 - side], inc=1, device_id={"row": where}, device_id_type=MESH)
                else:
                    pl.semaphore_wait(hello.at[i, side], 1)

    def rows(xb):
        return pl.ds(SUB * xb, SUB)

    def spot(z0, xb):
        return depth * (xb % per_group) + z0

    def put(acc, v, z0, parity, xb):
        m = spot(z0, xb)
        at = (parity, xb // per_group)
        acc[at] = jnp.where(pair[parity] == m >> 1, pltpu.roll(v, m, 1), acc[at])

    def fresh():
        return {(p, g): zero for p in (0, 1) for g in range(groups)}

    def faces(acc, g):
        low = jnp.where(is_even, acc[0, g], acc[1, g])
        high = jnp.where(is_even, acc[1, g], acc[0, g])
        return low, pltpu.roll(high, 1, 1)

    load_c.wait()
    c0, c1, c2 = 0.5 * coef[0], 0.5 * coef[1], 0.5 * coef[2]

    def conduct(lb):
        return jnp.where(lb == 0, c0, jnp.where(lb == 1, c1, c2))

    def pack_first(j, carry):
        au, ad = [dict(c) for c in carry]
        for copy in load(j):
            copy.wait()
        for i in range(SUB):
            z0 = SUB * j + i
            for xb in range(blocks):
                v = u[z0 + 1, rows(xb), :]
                dv = conduct(lab[z0 + 1, rows(xb), :])
                d[z0 + 1, rows(xb), :] = dv
                put(au, v, z0, i % 2, xb)
                put(ad, dv, z0, i % 2, xb)
        return au, ad

    au, ad = lax.fori_loop(0, chunks, pack_first, (fresh(), fresh()))
    for g in range(groups):
        at = pl.ds(SUB * g, SUB)
        ys[0, 0, at, :], ys[1, 0, at, :] = faces(au, g)
        ys[0, 1, at, :], ys[1, 1, at, :] = faces(ad, g)
    start(y_down)

    def meet_above(cond):
        @pl.when(cond)
        def _():
            pl.semaphore_wait(above, 1)
            for copy, _, _ in y_up:
                copy.start()

    meet_above(waits_short)

    def edge(ref, first, k, side):
        flat = ref.reshape(ref.shape[0] * wide, LANES)
        got = None
        for i in range(SUB):
            row = flat[pl.ds((first + SUB * k + i) * wide + (wide - 1) * side, SUB, stride=0), :]
            got = row if got is None else jnp.where(sub == i, row, got)
        return got

    for side in (0, 1):
        for k in range(chunks):
            for i, a in enumerate((u, d)):
                xs[side, i, pl.ds(SUB * k, SUB), :] = edge(a, 1, k, side)

    start(x_first)
    for p in range(PARTS):
        start(z_first(p))

    def flux(da, db, ub, ua):
        return (da + db) * (ub - ua)

    def plane(src, dst, shift, z, fz, high, first_step):
        nf, before = [], None
        for xb in range(blocks):
            a, k = src[z, rows(xb), :], d[z, rows(xb), :]
            if xb < blocks - 1:
                at = pl.ds(SUB * xb + 1, SUB)
                fxx = flux(k, d[z, at, :], src[z, at, :], a)
            else:
                fxx = flux(k, pltpu.roll(k, SUB - 1, 0), pltpu.roll(a, SUB - 1, 0), a)
                fxx = jnp.where(sub == SUB - 1, 0.0, fxx)
            turned = pltpu.roll(fxx, 1, 0)
            behind = jnp.where(sub == 0, 0.0 if before is None else before, turned)
            before = turned
            if first_step:
                kk = k + pltpu.roll(k, LANES - 1, 1)
                ky[z - 1, rows(xb), :] = kk
            else:
                kk = ky[z - 1, rows(xb), :]
            gy = kk * (pltpu.roll(a, LANES - 1, 1) - a)
            fy[z - 1, rows(xb), :] = gy
            total = (fxx - behind) + gy
            if high:
                nz = flux(k, d[z + 1, rows(xb), :], src[z + 1, rows(xb), :], a)
                total = total + (nz if fz is None else nz - fz[xb])
                nf.append(nz)
            elif fz is not None:
                total = total - fz[xb]
            dst[z + shift, rows(xb), :] = a + total
        return tuple(nf)

    def between(src, z):
        return tuple(
            flux(d[z, rows(xb), :], d[z + 1, rows(xb), :], src[z + 1, rows(xb), :], src[z, rows(xb), :])
            for xb in range(blocks)
        )

    def planes(src, dst, shift, begin, count, fz, first_step):
        def several(j, fz):
            for i in range(FLUX):
                fz = plane(src, dst, shift, begin + FLUX * j + i, fz, True, first_step)
            return fz

        return lax.fori_loop(0, count // FLUX, several, fz)

    fz = plane(u, h, 0, 1, None, True, True)
    fz = planes(u, h, 0, 2, depth - FLUX, fz, True)
    for z in range(depth - FLUX + 2, last):
        fz = plane(u, h, 0, z, fz, True, True)
    plane(u, h, 0, last, fz, False, True)

    def settle(dst, shift):
        def some(j, carry):
            for i in range(FLUX):
                z0 = FLUX * j + i
                for xb in range(blocks):
                    dst[z0 + shift, rows(xb), :] = dst[z0 + shift, rows(xb), :] - pltpu.roll(fy[z0, rows(xb), :], 1, 1)
            return carry

        lax.fori_loop(0, depth // FLUX, some, 0)

    def sweep(first, trips, count, body, carry):
        def some(j, carry):
            for i in range(count):
                carry = body(count * j + first + i, carry, (first + i) % 2)
            return carry

        return lax.fori_loop(0, trips, some, carry)

    settle(h, 1)

    def pack_h(z0, acc, parity, which=range(blocks)):
        acc = dict(acc)
        for xb in which:
            put(acc, h[z0 + 1, rows(xb), :], z0, parity, xb)
        return acc

    acc = dict(sweep(0, depth // PACK, PACK, pack_h, fresh()))
    meet_above(waits_long)

    def x_faces(own, came):
        for side in (0, 1):
            for k in range(chunks):
                at = pl.ds(SUB * k, SUB)
                fx[side, at, :] = flux(xs[side, 1, at, :], xr[side, 1, at, :], came(side, at), own(side, at))

    def y_faces(own, came, with_high=True):
        even, odd, highs = [], [], []
        for g in range(groups):
            at = pl.ds(SUB * g, SUB)
            dl, dr, ul, ur = ys[0, 1, at, :], ys[1, 1, at, :], own(0, at), own(1, at)
            closed = flux(dl, dr, ul, ur)
            a = flux(dl, yr[0, 1, at, :], came(0, at), ul) + closed
            b = zero - closed
            if with_high:
                high = flux(dr, yr[1, 1, at, :], came(1, at), ur)
                highs.append(high)
                b = b + high
            b = pltpu.roll(b, LANES - 1, 1)
            even.append(jnp.where(is_even, a, b))
            odd.append(jnp.where(is_even, b, a))
        return (even, odd), highs

    def with_faces(v, packed, z0, parity, xb):
        r = pltpu.roll(packed[parity][xb // per_group], (LANES - spot(z0, xb)) & (LANES - 1), 1)
        v = jnp.where(at_ends, v + r, v)
        if xb == 0:
            v = jnp.where(sub == 0, v + fx[0, pl.ds(z0, SUB, stride=0), :], v)
        if xb == blocks - 1:
            v = jnp.where(sub == SUB - 1, v + fx[1, pl.ds(z0, SUB, stride=0), :], v)
        return v

    own_y, came_y = lambda s, at: ys[s, 0, at, :], lambda s, at: yr[s, 0, at, :]
    arrive(x_first)
    x_faces(lambda s, at: xs[s, 0, at, :], lambda s, at: xr[s, 0, at, :])
    arrive(y_up)
    packed, _ = y_faces(own_y, came_y, with_high=False)

    outer = ((0, 0, 0), (depth - 1, depth + 1, 1))
    brims = (0, blocks - 1)

    for p in (0, 1):
        for g in range(groups):
            acc[p, g] = acc[p, g] + packed[p][g]

    def pack_brims(z0, acc, parity):
        acc = dict(acc)
        for xb in brims:
            put(acc, with_faces(h[z0 + 1, rows(xb), :], packed, z0, parity, xb), z0, parity, xb)
        return acc

    acc = dict(sweep(1, 3, 10, pack_brims, acc))
    for p in range(PARTS):
        arrive(z_first(p))
    for (z0, ghost, parity), inside in zip(outer, (has_prev, has_next)):
        for xb in range(blocks):
            at = rows(xb)
            dg = jnp.where(inside, conduct(lab[ghost, at, :]), 0.0)
            d[ghost, at, :] = dg
            v = h[z0 + 1, at, :] + flux(d[z0 + 1, at, :], dg, u[ghost, at, :], u[z0 + 1, at, :])
            h[z0 + 1, at, :] = v
            put(acc, with_faces(v, packed, z0, parity, xb), z0, parity, xb)
    ends = [faces(acc, g) for g in range(groups)]
    for g in range(groups):
        ys2[0, pl.ds(SUB * g, SUB), :] = ends[g][0]
    start(y_down2)

    arrive(y_down)
    packed, highs = y_faces(own_y, came_y)
    for g in range(groups):
        ys2[1, pl.ds(SUB * g, SUB), :] = ends[g][1] + highs[g]
    start(y_up2)

    def fix_h(which):
        def body(z0, carry, parity):
            for xb in which:
                h[z0 + 1, rows(xb), :] = with_faces(h[z0 + 1, rows(xb), :], packed, z0, parity, xb)
            return carry

        return body

    for z0, _, parity in outer:
        fix_h(range(blocks))(z0, 0, parity)
    for p in range(PARTS):
        start(z_second(p))
    greet(0, 2, "signal")
    sweep(1, 3, 10, fix_h(brims), 0)
    for side in (0, 1):
        for k in range(chunks):
            xs2[side, pl.ds(SUB * k, SUB), :] = edge(h, 1, k, side)
    start(x_second)
    sweep(1, 5, 6, fix_h(range(1, blocks - 1)), 0)
    greet(0, 2, "wait")
    greet(1, 4, "signal")

    fz = plane(h, f, -1, 1, None, True, False)
    fz = planes(h, f, -1, 2, depth - FLUX, fz, False)
    for z in range(depth - FLUX + 2, last):
        fz = plane(h, f, -1, z, fz, True, False)
    plane(h, f, -1, last, fz, False, False)
    settle(f, 0)

    load_k.wait()
    scale = 0.5 / (depth * n_row)
    k0, k1, k2 = thick[0] * scale, thick[1] * scale, thick[2] * scale

    def opaque(v, lb):
        first, second = lb == 0, lb == 1
        half = jnp.where(first, k0, jnp.where(second, k1, k2))
        return half + half * jnp.tanh(0.5 * v), first, second

    arrive(x_second)
    x_faces(lambda s, at: xs2[s, at, :], lambda s, at: xr2[s, at, :])
    arrive(y_up2)
    arrive(y_down2)
    packed2, _ = y_faces(lambda s, at: ys2[s, at, :], lambda s, at: yr2[s, at, :])

    def march(z0, carry, parity):
        through, w0, w1 = [list(c) for c in carry]
        for xb in range(blocks):
            v = with_faces(f[z0, rows(xb), :], packed2, z0, parity, xb)
            f[z0, rows(xb), :] = v
            a, first, second = opaque(v, lab[z0 + 1, rows(xb), :])
            w = through[xb] * a
            through[xb] = through[xb] - w
            w0[xb] = w0[xb] + jnp.where(first, w, 0.0)
            w1[xb] = w1[xb] + jnp.where(second, w, 0.0)
        return tuple(tuple(c) for c in (through, w0, w1))

    state = sweep(1, (depth - 2) // MARCH, MARCH, march, ((one,) * blocks,) + ((zero,) * blocks,) * 2)
    for i in range(3):
        for xb in range(blocks):
            mid[i, rows(xb), :] = state[i][xb]
    for z0, _, parity in outer:
        for xb in range(blocks):
            f[z0, rows(xb), :] = with_faces(f[z0, rows(xb), :], packed2, z0, parity, xb)
    load_p.wait()

    for p in range(PARTS):
        arrive(z_second(p))
    for xb in range(blocks):
        at = rows(xb)
        ends = []
        for z0, ghost, parity in outer:
            fz = flux(d[z0 + 1, at, :], d[ghost, at, :], h[ghost, at, :], h[z0 + 1, at, :])
            v = f[z0, at, :] + fz
            f[z0, at, :] = v
            ends.append(opaque(v, lab[z0 + 1, at, :]))
        (a, fa, fb), (b, ga, gb) = ends
        clear_a = 1.0 - a
        through = clear_a * mid[0, at, :]
        w = through * b
        ib[xb, 0] = jnp.where(fa, a, 0.0) + clear_a * mid[1, at, :] + jnp.where(ga, w, 0.0)
        ib[xb, 1] = jnp.where(fb, a, 0.0) + clear_a * mid[2, at, :] + jnp.where(gb, w, 0.0)
        ib[xb, 2] = through - w

    def hand(o):
        dest = lax.rem(me + o, n_row)
        return pltpu.make_async_remote_copy(
            src_ref=ib.at[dest], dst_ref=rb.at[me], send_sem=asem.at[o], recv_sem=bsem.at[me],
            device_id={"row": dest}, device_id_type=MESH,
        )

    greet(1, 4, "wait")
    half = n_row // 2
    order = sorted(range(1, n_row), key=lambda o: abs(o - half))
    for o in order:
        hand(o).start()
    rb[me] = ib[me]

    for s in range(n_row):
        @pl.when(me != s)
        def _():
            pltpu.make_async_remote_copy(
                src_ref=ib.at[s], dst_ref=rb.at[s], send_sem=asem.at[0], recv_sem=bsem.at[s],
                device_id={"row": s}, device_id_type=MESH,
            ).wait_recv()

    through, w0, w1 = one, zero, zero
    for s in range(n_row):
        w0 = w0 + through * rb[s, 0]
        w1 = w1 + through * rb[s, 1]
        through = through * rb[s, 2]
    blocked = 1.0 - through
    w2 = (blocked - w0) - w1
    for c in range(3):
        pic_ref[c] = w0 * tint[0, c] + w1 * tint[1, c] + w2 * tint[2, c]
    pic_ref[3] = blocked

    for o in order:
        hand(o).wait_send()
    for p in range(PARTS):
        left_here(z_first(p))
        left_here(z_second(p))
    for copies in (y_down, y_up, x_first, y_down2, y_up2, x_second):
        left_here(copies)


def deliver(f, pic, out, out_pic, sem):
    a = pltpu.make_async_copy(f, out, sem.at[0])
    b = pltpu.make_async_copy(pic, out_pic, sem.at[1])
    a.start()
    b.start()
    a.wait()
    b.wait()


def solution(mesh):
    sizes = (mesh.shape["sx"], mesh.shape["sy"], mesh.shape["row"])
    n_row = sizes[2]

    def per_device(thermal_state, substance_label, thermal_coefficients, optical_thickness, substance_colours):
        depth, wide, tall = thermal_state.shape
        f32 = jnp.float32
        side = depth * wide // LANES
        near = pl.BlockSpec(memory_space=pltpu.VMEM)
        anywhere = pl.BlockSpec(memory_space=pl.ANY)
        chunks = depth // SUB
        results = (
            jax.ShapeDtypeStruct((depth, wide, tall), f32),
            jax.ShapeDtypeStruct((4, wide // n_row, tall), f32),
        )
        f, pic = pl.pallas_call(
            functools.partial(kernel, sizes),
            out_shape=results,
            in_specs=[anywhere] * 5,
            out_specs=(near, near),
            scratch_shapes=[
                pltpu.VMEM((depth + 2, wide, tall), f32),
                pltpu.VMEM((depth + 2, wide, tall), f32),
                pltpu.VMEM((depth + 2, wide, tall), f32),
                pltpu.VMEM((depth, wide, tall), f32),
                pltpu.VMEM((depth, wide, tall), f32),
                pltpu.VMEM((depth + 2, wide, tall), jnp.int32),
                pltpu.VMEM((2, 2, depth, tall), f32),
                pltpu.VMEM((2, 2, depth, tall), f32),
                pltpu.VMEM((2, depth, tall), f32),
                pltpu.VMEM((2, depth, tall), f32),
                pltpu.VMEM((2, depth + SUB, tall), f32),
                pltpu.VMEM((2, 2, side, tall), f32),
                pltpu.VMEM((2, 2, side, tall), f32),
                pltpu.VMEM((2, side, tall), f32),
                pltpu.VMEM((2, side, tall), f32),
                pltpu.VMEM((3, wide, tall), f32),
                pltpu.VMEM((n_row, 3, wide // n_row, tall), f32),
                pltpu.VMEM((n_row, 3, wide // n_row, tall), f32),
                pltpu.SMEM((3,), f32),
                pltpu.SMEM((3,), f32),
                pltpu.SMEM((3, 3), f32),
                pltpu.SemaphoreType.DMA((2, chunks)),
                pltpu.SemaphoreType.DMA((3,)),
                pltpu.SemaphoreType.DMA((2, 2, PARTS)),
                pltpu.SemaphoreType.DMA((2, 2, PARTS)),
                pltpu.SemaphoreType.DMA((2, PARTS)),
                pltpu.SemaphoreType.DMA((2, PARTS)),
                pltpu.SemaphoreType.DMA((8,)),
                pltpu.SemaphoreType.DMA((8,)),
                pltpu.SemaphoreType.DMA((n_row,)),
                pltpu.SemaphoreType.DMA((n_row,)),
                pltpu.SemaphoreType.REGULAR((2, 2)),
                pltpu.SemaphoreType.REGULAR,
            ],
            compiler_params=pltpu.CompilerParams(
                collective_id=0, has_side_effects=True, vmem_limit_bytes=VMEM_LIMIT
            ),
        )(*[
            pltpu.with_memory_space_constraint(a, pltpu.HBM)
            for a in (thermal_state, substance_label, thermal_coefficients, optical_thickness, substance_colours)
        ])
        return pl.pallas_call(
            deliver,
            out_shape=results,
            in_specs=[near, near],
            out_specs=(anywhere, anywhere),
            scratch_shapes=[pltpu.SemaphoreType.DMA((2,))],
            compiler_params=pltpu.CompilerParams(vmem_limit_bytes=VMEM_LIMIT),
        )(f, pic)

    placed = (P("row", "sx", "sy"), P("row", "sx", "sy"), P(), P(), P())
    return jax.shard_map(
        per_device,
        mesh=mesh,
        in_specs=placed,
        out_specs=(P("row", "sx", "sy"), P(None, ("sx", "row"), "sy")),
        check_vma=False,
    )
```

```python
import functools

import jax
import jax.numpy as jnp
from jax import lax
from jax.experimental import pallas as pl
from jax.experimental.pallas import tpu as pltpu
from jax.sharding import PartitionSpec as P

MESH = pl.DeviceIdType.MESH
SUB, LANES = 8, 128
FLUX, PACK, MARCH, PARTS = 4, 4, 4, 1
VMEM_LIMIT = 16 << 20


def kernel(
    sizes,
    t_hbm, lab_hbm, coef_hbm, thick_hbm, tint_hbm,
    f, pic_ref,
    u, d, h, ky, fy, lab, xs, xr, xs2, xr2, fx, ys, yr, ys2, yr2, turn, ib, rb,
    coef, thick, tint, lsem, csem, zsem1, zrec1, zsem2, zrec2, ssem, rsem, asem, bsem, hello, above,
):
    n_sx, n_sy, n_row = sizes
    depth, wide = t_hbm.shape[0], t_hbm.shape[1]
    blocks = wide // SUB
    per_group = LANES // depth
    groups = blocks // per_group
    chunks = depth // SUB
    last = depth
    per_part = blocks // PARTS
    me, my_sx, my_sy = lax.axis_index("row"), lax.axis_index("sx"), lax.axis_index("sy")
    has_prev, has_next = me > 0, me < n_row - 1
    has_left, has_right = my_sy > 0, my_sy < n_sy - 1

    def load(j):
        at, to = pl.ds(SUB * j, SUB), pl.ds(SUB * j + 1, SUB)
        return (
            pltpu.make_async_copy(lab_hbm.at[at], lab.at[to], lsem.at[0, j]),
            pltpu.make_async_copy(t_hbm.at[at], u.at[to], lsem.at[1, j]),
        )

    load_c = pltpu.make_async_copy(coef_hbm, coef, csem.at[0])
    load_k = pltpu.make_async_copy(thick_hbm, thick, csem.at[1])
    load_p = pltpu.make_async_copy(tint_hbm, tint, csem.at[2])
    load_c.start()
    for j in range(chunks):
        for copy in load(j):
            copy.start()
    load_k.start()
    load_p.start()

    sx_next = lax.rem(my_sx + 1, n_sx)
    sx_prev = lax.rem(my_sx + n_sx - 1, n_sx)
    to_next, to_prev = {"row": me + 1}, {"row": me - 1}
    to_right, to_left = {"sy": my_sy + 1}, {"sy": my_sy - 1}
    to_up, to_down = {"sx": sx_next}, {"sx": sx_prev}

    def only(cond, act):
        if cond is None:
            act()
        else:
            pl.when(cond)(act)

    barrier = pltpu.get_barrier_semaphore()
    near = (
        (has_prev, to_prev), (has_next, to_next), (has_right, to_right), (None, to_up), (None, to_down),
    )
    for there, where in near:
        only(there, functools.partial(pl.semaphore_signal, barrier, inc=1, device_id=where, device_id_type=MESH))

    lane = lax.broadcasted_iota(jnp.int32, (SUB, LANES), 1)
    sub = lax.broadcasted_iota(jnp.int32, (SUB, LANES), 0)
    at_ends = (lane == 0) | (lane == LANES - 1)
    is_even = (lane & 1) == 0
    pair = (((lane + 1) >> 1) & (LANES // 2 - 1), lane >> 1)
    zero = jnp.zeros((SUB, LANES), jnp.float32)
    one = jnp.ones((SUB, LANES), jnp.float32)

    def clear(cond, refs):
        @pl.when(jnp.logical_not(cond))
        def _():
            for r in refs:
                r[...] = jnp.zeros(r.shape, r.dtype)

    clear(has_prev, (u.at[0], d.at[0], h.at[0]))
    clear(has_next, (u.at[depth + 1], d.at[depth + 1], h.at[depth + 1]))
    clear(has_left, (yr.at[0], yr2.at[0]))
    clear(has_right, (yr.at[1], yr2.at[1]))

    def start(copies):
        for copy, sends, _ in copies:
            only(sends, copy.start)

    def arrive(copies):
        for copy, _, receives in copies:
            only(receives, copy.wait_recv)

    def left_here(copies):
        for copy, sends, _ in copies:
            only(sends, copy.wait_send)

    def remote(src, dst, send, recv, where):
        return pltpu.make_async_remote_copy(
            src_ref=src, dst_ref=dst, send_sem=send, recv_sem=recv, device_id=where, device_id_type=MESH
        )

    def z_first(p):
        at = pl.ds(SUB * per_part * p, SUB * per_part)
        got = []
        for i, (src, dst) in enumerate(((t_hbm, u), (lab_hbm, lab))):
            got.append((remote(src.at[depth - 1, at], dst.at[0, at], zsem1.at[0, i, p], zrec1.at[0, i, p], to_next),
                        has_next, has_prev))
            got.append((remote(src.at[0, at], dst.at[depth + 1, at], zsem1.at[1, i, p], zrec1.at[1, i, p], to_prev),
                        has_prev, has_next))
        return got

    def z_second(p):
        at = pl.ds(SUB * per_part * p, SUB * per_part)
        return [
            (remote(h.at[last, at], h.at[0, at], zsem2.at[0, p], zrec2.at[0, p], to_next), has_next, has_prev),
            (remote(h.at[1, at], h.at[depth + 1, at], zsem2.at[1, p], zrec2.at[1, p], to_prev), has_prev, has_next),
        ]

    def y_copies(src, dst, s):
        return (
            [(remote(src.at[0], dst.at[1], ssem.at[s + 1], rsem.at[s + 1], to_left), has_left, has_right)],
            [(remote(src.at[1], dst.at[0], ssem.at[s], rsem.at[s], to_right), has_right, has_left)],
        )

    def x_copies(src, dst, s):
        return [
            (remote(src.at[1], dst.at[0], ssem.at[s], rsem.at[s], to_up), None, None),
            (remote(src.at[0], dst.at[1], ssem.at[s + 1], rsem.at[s + 1], to_down), None, None),
        ]

    (y_down, y_up), x_first = y_copies(ys, yr, 0), x_copies(xs, xr, 2)
    (y_down2, y_up2), x_second = y_copies(ys2, yr2, 4), x_copies(xs2, xr2, 6)

    waits_long = has_right & (my_sy == n_sy // 2 - 1)
    waits_short = has_right & (my_sy != n_sy // 2 - 1)

    def greet(i, apart, act):
        for side, there, where in ((0, me >= apart, me - apart), (1, me + apart < n_row, me + apart)):
            @pl.when(there)
            def _():
                if act == "signal":
                    pl.semaphore_signal(hello.at[i, 1 - side], inc=1, device_id={"row": where}, device_id_type=MESH)
                else:
                    pl.semaphore_wait(hello.at[i, side], 1)

    def rows(xb):
        return pl.ds(SUB * xb, SUB)

    def spot(z0, xb):
        return depth * (xb % per_group) + z0

    def put(acc, v, z0, parity, xb):
        m = spot(z0, xb)
        at = (parity, xb // per_group)
        acc[at] = jnp.where(pair[parity] == m >> 1, pltpu.roll(v, m, 1), acc[at])

    def fresh():
        return {(p, g): zero for p in (0, 1) for g in range(groups)}

    def faces(acc, g):
        low = jnp.where(is_even, acc[0, g], acc[1, g])
        high = jnp.where(is_even, acc[1, g], acc[0, g])
        return low, pltpu.roll(high, 1, 1)

    load_c.wait()
    c0, c1, c2 = 0.5 * coef[0], 0.5 * coef[1], 0.5 * coef[2]

    def conduct(lb):
        return jnp.where(lb == 0, c0, jnp.where(lb == 1, c1, c2))

    def pack_first(j, carry):
        au, ad = [dict(c) for c in carry]
        for copy in load(j):
            copy.wait()
        for i in range(SUB):
            z0 = SUB * j + i
            for xb in range(blocks):
                v = u[z0 + 1, rows(xb), :]
                dv = conduct(lab[z0 + 1, rows(xb), :])
                d[z0 + 1, rows(xb), :] = dv
                put(au, v, z0, i % 2, xb)
                put(ad, dv, z0, i % 2, xb)
        return au, ad

    au, ad = lax.fori_loop(0, chunks, pack_first, (fresh(), fresh()))
    for g in range(groups):
        at = pl.ds(SUB * g, SUB)
        ys[0, 0, at, :], ys[1, 0, at, :] = faces(au, g)
        ys[0, 1, at, :], ys[1, 1, at, :] = faces(ad, g)
    pl.semaphore_wait(barrier, 2 + sum(c.astype(jnp.int32) for c in (has_prev, has_next, has_left)))
    only(has_left, functools.partial(pl.semaphore_signal, above, inc=1, device_id=to_left, device_id_type=MESH))
    start(y_down)

    def meet_above(cond):
        @pl.when(cond)
        def _():
            pl.semaphore_wait(above, 1)
            for copy, _, _ in y_up:
                copy.start()

    meet_above(waits_short)

    def edge(ref, first, k, side):
        flat = ref.reshape(ref.shape[0] * wide, LANES)
        got = None
        for i in range(SUB):
            row = flat[pl.ds((first + SUB * k + i) * wide + (wide - 1) * side, SUB, stride=0), :]
            got = row if got is None else jnp.where(sub == i, row, got)
        return got

    for side in (0, 1):
        for k in range(chunks):
            for i, a in enumerate((u, d)):
                xs[side, i, pl.ds(SUB * k, SUB), :] = edge(a, 1, k, side)

    start(x_first)
    for p in range(PARTS):
        start(z_first(p))

    def flux(da, db, ub, ua):
        return (da + db) * (ub - ua)

    def plane(src, dst, shift, z, fz, high, first_step):
        nf, before = [], None
        for xb in range(blocks):
            a, k = src[z, rows(xb), :], d[z, rows(xb), :]
            if xb < blocks - 1:
                at = pl.ds(SUB * xb + 1, SUB)
                fxx = flux(k, d[z, at, :], src[z, at, :], a)
            else:
                fxx = flux(k, pltpu.roll(k, SUB - 1, 0), pltpu.roll(a, SUB - 1, 0), a)
                fxx = jnp.where(sub == SUB - 1, 0.0, fxx)
            turned = pltpu.roll(fxx, 1, 0)
            behind = jnp.where(sub == 0, 0.0 if before is None else before, turned)
            before = turned
            if first_step:
                kk = k + pltpu.roll(k, LANES - 1, 1)
                ky[z - 1, rows(xb), :] = kk
            else:
                kk = ky[z - 1, rows(xb), :]
            gy = kk * (pltpu.roll(a, LANES - 1, 1) - a)
            fy[z - 1, rows(xb), :] = gy
            total = (fxx - behind) + gy
            if high:
                nz = flux(k, d[z + 1, rows(xb), :], src[z + 1, rows(xb), :], a)
                total = total + (nz if fz is None else nz - fz[xb])
                nf.append(nz)
            elif fz is not None:
                total = total - fz[xb]
            dst[z + shift, rows(xb), :] = a + total
        return tuple(nf)

    def between(src, z):
        return tuple(
            flux(d[z, rows(xb), :], d[z + 1, rows(xb), :], src[z + 1, rows(xb), :], src[z, rows(xb), :])
            for xb in range(blocks)
        )

    def planes(src, dst, shift, begin, count, fz, first_step):
        def several(j, fz):
            for i in range(FLUX):
                fz = plane(src, dst, shift, begin + FLUX * j + i, fz, True, first_step)
            return fz

        return lax.fori_loop(0, count // FLUX, several, fz)

    fz = plane(u, h, 0, 1, None, True, True)
    fz = planes(u, h, 0, 2, depth - FLUX, fz, True)
    for z in range(depth - FLUX + 2, last):
        fz = plane(u, h, 0, z, fz, True, True)
    plane(u, h, 0, last, fz, False, True)

    def settle(dst, shift):
        def some(j, carry):
            for i in range(FLUX):
                z0 = FLUX * j + i
                for xb in range(blocks):
                    dst[z0 + shift, rows(xb), :] = dst[z0 + shift, rows(xb), :] - pltpu.roll(fy[z0, rows(xb), :], 1, 1)
            return carry

        lax.fori_loop(0, depth // FLUX, some, 0)

    def sweep(first, trips, count, body, carry):
        def some(j, carry):
            for i in range(count):
                carry = body(count * j + first + i, carry, (first + i) % 2)
            return carry

        return lax.fori_loop(0, trips, some, carry)

    settle(h, 1)

    def pack_h(z0, acc, parity, which=range(blocks)):
        acc = dict(acc)
        for xb in which:
            put(acc, h[z0 + 1, rows(xb), :], z0, parity, xb)
        return acc

    acc = dict(sweep(0, depth // PACK, PACK, pack_h, fresh()))
    meet_above(waits_long)

    def x_faces(own, came):
        for side in (0, 1):
            for k in range(chunks):
                at = pl.ds(SUB * k, SUB)
                fx[side, at, :] = flux(xs[side, 1, at, :], xr[side, 1, at, :], came(side, at), own(side, at))

    def y_faces(own, came, with_high=True):
        even, odd, highs = [], [], []
        for g in range(groups):
            at = pl.ds(SUB * g, SUB)
            dl, dr, ul, ur = ys[0, 1, at, :], ys[1, 1, at, :], own(0, at), own(1, at)
            closed = flux(dl, dr, ul, ur)
            a = flux(dl, yr[0, 1, at, :], came(0, at), ul) + closed
            b = zero - closed
            if with_high:
                high = flux(dr, yr[1, 1, at, :], came(1, at), ur)
                highs.append(high)
                b = b + high
            b = pltpu.roll(b, LANES - 1, 1)
            even.append(jnp.where(is_even, a, b))
            odd.append(jnp.where(is_even, b, a))
        return (even, odd), highs

    def with_faces(v, packed, z0, parity, xb):
        r = pltpu.roll(packed[parity][xb // per_group], (LANES - spot(z0, xb)) & (LANES - 1), 1)
        v = jnp.where(at_ends, v + r, v)
        if xb == 0:
            v = jnp.where(sub == 0, v + fx[0, pl.ds(z0, SUB, stride=0), :], v)
        if xb == blocks - 1:
            v = jnp.where(sub == SUB - 1, v + fx[1, pl.ds(z0, SUB, stride=0), :], v)
        return v

    own_y, came_y = lambda s, at: ys[s, 0, at, :], lambda s, at: yr[s, 0, at, :]
    arrive(x_first)
    x_faces(lambda s, at: xs[s, 0, at, :], lambda s, at: xr[s, 0, at, :])
    arrive(y_up)
    packed, _ = y_faces(own_y, came_y, with_high=False)

    outer = ((0, 0, 0), (depth - 1, depth + 1, 1))
    brims = (0, blocks - 1)

    for p in (0, 1):
        for g in range(groups):
            acc[p, g] = acc[p, g] + packed[p][g]

    def pack_brims(z0, acc, parity):
        acc = dict(acc)
        for xb in brims:
            put(acc, with_faces(h[z0 + 1, rows(xb), :], packed, z0, parity, xb), z0, parity, xb)
        return acc

    acc = dict(sweep(1, 3, 10, pack_brims, acc))
    for p in range(PARTS):
        arrive(z_first(p))
    for (z0, ghost, parity), inside in zip(outer, (has_prev, has_next)):
        for xb in range(blocks):
            at = rows(xb)
            dg = jnp.where(inside, conduct(lab[ghost, at, :]), 0.0)
            d[ghost, at, :] = dg
            v = h[z0 + 1, at, :] + flux(d[z0 + 1, at, :], dg, u[ghost, at, :], u[z0 + 1, at, :])
            h[z0 + 1, at, :] = v
            put(acc, with_faces(v, packed, z0, parity, xb), z0, parity, xb)
    ends = [faces(acc, g) for g in range(groups)]
    for g in range(groups):
        ys2[0, pl.ds(SUB * g, SUB), :] = ends[g][0]
    start(y_down2)

    arrive(y_down)
    packed, highs = y_faces(own_y, came_y)
    for g in range(groups):
        ys2[1, pl.ds(SUB * g, SUB), :] = ends[g][1] + highs[g]
    start(y_up2)

    def fix_h(which):
        def body(z0, carry, parity):
            for xb in which:
                h[z0 + 1, rows(xb), :] = with_faces(h[z0 + 1, rows(xb), :], packed, z0, parity, xb)
            return carry

        return body

    for z0, _, parity in outer:
        fix_h(range(blocks))(z0, 0, parity)
    for p in range(PARTS):
        start(z_second(p))
    greet(0, 2, "signal")
    sweep(1, 3, 10, fix_h(brims), 0)
    for side in (0, 1):
        for k in range(chunks):
            xs2[side, pl.ds(SUB * k, SUB), :] = edge(h, 1, k, side)
    start(x_second)
    sweep(1, 5, 6, fix_h(range(1, blocks - 1)), 0)
    greet(0, 2, "wait")
    greet(1, 4, "signal")

    fz = plane(h, f, -1, 1, None, True, False)
    fz = planes(h, f, -1, 2, depth - FLUX, fz, False)
    for z in range(depth - FLUX + 2, last):
        fz = plane(h, f, -1, z, fz, True, False)
    plane(h, f, -1, last, fz, False, False)
    settle(f, 0)

    load_k.wait()
    scale = 0.5 / (depth * n_row)
    k0, k1, k2 = thick[0] * scale, thick[1] * scale, thick[2] * scale

    def opaque(v, lb):
        first, second = lb == 0, lb == 1
        half = jnp.where(first, k0, jnp.where(second, k1, k2))
        return half + half * jnp.tanh(0.5 * v), first, second

    arrive(x_second)
    x_faces(lambda s, at: xs2[s, at, :], lambda s, at: xr2[s, at, :])

    def brims_f(z0, carry, parity):
        for xb, side, at_row in ((0, 0, 0), (blocks - 1, 1, SUB - 1)):
            v = f[z0, rows(xb), :]
            f[z0, rows(xb), :] = jnp.where(sub == at_row, v + fx[side, pl.ds(z0, SUB, stride=0), :], v)
        return carry

    sweep(0, depth // SUB, SUB, brims_f, 0)
    for p in range(PARTS):
        arrive(z_second(p))
    arrive(y_up2)
    arrive(y_down2)
    packed2, _ = y_faces(lambda s, at: ys2[s, at, :], lambda s, at: yr2[s, at, :])
    for p in (0, 1):
        for g in range(groups):
            turn[p, pl.ds(SUB * g, SUB), :] = packed2[p][g]
    load_p.wait()

    def hand(o):
        dest = lax.rem(me + o, n_row)
        return pltpu.make_async_remote_copy(
            src_ref=ib.at[dest], dst_ref=rb.at[me], send_sem=asem.at[o], recv_sem=bsem.at[me],
            device_id={"row": dest}, device_id_type=MESH,
        )

    def march(dests):
        places = []
        for dest in dests:
            at = pl.ds(pl.multiple_of(dest * SUB, SUB), SUB)
            group = pl.ds(pl.multiple_of(dest // per_group * SUB, SUB), SUB)
            sides = [turn[parity, group, :] for parity in (0, 1)]
            places.append((at, sides, LANES - lax.rem(dest, per_group) * depth))

        def warm(chunk):
            got = {}
            for z0 in chunk:
                for i, (at, sides, m) in enumerate(places):
                    v = f[z0, at, :]
                    for edge_z, ghost in ((0, 0), (depth - 1, depth + 1)):
                        if z0 == edge_z:
                            v = v + flux(d[z0 + 1, at, :], d[ghost, at, :], h[ghost, at, :], h[z0 + 1, at, :])
                    got[z0, i] = jnp.where(at_ends, v + pltpu.roll(sides[z0 % 2], (m - z0) & (LANES - 1), 1), v)
            return got

        states = [(None, zero, zero)] * len(dests)
        steps = [range(k, k + MARCH) for k in range(0, depth, MARCH)]
        ahead = warm(steps[0])
        for k, chunk in enumerate(steps):
            now, ahead = ahead, warm(steps[k + 1]) if k + 1 < len(steps) else None
            for (z0, i), v in now.items():
                f[z0, places[i][0], :] = v
            for (z0, i), v in now.items():
                through, w0, w1 = states[i]
                w, first, second = opaque(v, lab[z0 + 1, places[i][0], :])
                if through is None:
                    through = 1.0 - w
                else:
                    w = through * w
                    through = through - w
                w0 = w0 + jnp.where(first, w, 0.0)
                w1 = w1 + jnp.where(second, w, 0.0)
                states[i] = (through, w0, w1)
        for dest, (through, w0, w1) in zip(dests, states):
            ib[dest, 0] = w0
            ib[dest, 1] = w1
            ib[dest, 2] = through

    greet(1, 4, "wait")
    half = n_row // 2
    order = [half + 1, half - 1, half] + [o for k in range(1, half - 1) for o in (n_row - k, k)] + [0]
    for k in range(0, n_row, 2):
        march([lax.rem(me + o, n_row) for o in order[k : k + 2]])
        for o in order[k : k + 2]:
            if o:
                hand(o).start()
    rb[me] = ib[me]

    for s in range(n_row):
        @pl.when(me != s)
        def _():
            pltpu.make_async_remote_copy(
                src_ref=ib.at[s], dst_ref=rb.at[s], send_sem=asem.at[0], recv_sem=bsem.at[s],
                device_id={"row": s}, device_id_type=MESH,
            ).wait_recv()

    through, w0, w1 = one, zero, zero
    for s in range(n_row):
        w0 = w0 + through * rb[s, 0]
        w1 = w1 + through * rb[s, 1]
        through = through * rb[s, 2]
    blocked = 1.0 - through
    w2 = (blocked - w0) - w1
    for c in range(3):
        pic_ref[c] = w0 * tint[0, c] + w1 * tint[1, c] + w2 * tint[2, c]
    pic_ref[3] = blocked

    for o in range(1, n_row):
        hand(o).wait_send()
    for p in range(PARTS):
        left_here(z_first(p))
        left_here(z_second(p))
    for copies in (y_down, y_up, x_first, y_down2, y_up2, x_second):
        left_here(copies)


def deliver(f, pic, out, out_pic, sem):
    a = pltpu.make_async_copy(f, out, sem.at[0])
    b = pltpu.make_async_copy(pic, out_pic, sem.at[1])
    a.start()
    b.start()
    a.wait()
    b.wait()


def solution(mesh):
    sizes = (mesh.shape["sx"], mesh.shape["sy"], mesh.shape["row"])
    n_row = sizes[2]

    def per_device(thermal_state, substance_label, thermal_coefficients, optical_thickness, substance_colours):
        depth, wide, tall = thermal_state.shape
        f32 = jnp.float32
        side = depth * wide // LANES
        near = pl.BlockSpec(memory_space=pltpu.VMEM)
        anywhere = pl.BlockSpec(memory_space=pl.ANY)
        chunks = depth // SUB
        results = (
            jax.ShapeDtypeStruct((depth, wide, tall), f32),
            jax.ShapeDtypeStruct((4, wide // n_row, tall), f32),
        )
        f, pic = pl.pallas_call(
            functools.partial(kernel, sizes),
            out_shape=results,
            in_specs=[anywhere] * 5,
            out_specs=(near, near),
            scratch_shapes=[
                pltpu.VMEM((depth + 2, wide, tall), f32),
                pltpu.VMEM((depth + 2, wide, tall), f32),
                pltpu.VMEM((depth + 2, wide, tall), f32),
                pltpu.VMEM((depth, wide, tall), f32),
                pltpu.VMEM((depth, wide, tall), f32),
                pltpu.VMEM((depth + 2, wide, tall), jnp.int32),
                pltpu.VMEM((2, 2, depth, tall), f32),
                pltpu.VMEM((2, 2, depth, tall), f32),
                pltpu.VMEM((2, depth, tall), f32),
                pltpu.VMEM((2, depth, tall), f32),
                pltpu.VMEM((2, depth + SUB, tall), f32),
                pltpu.VMEM((2, 2, side, tall), f32),
                pltpu.VMEM((2, 2, side, tall), f32),
                pltpu.VMEM((2, side, tall), f32),
                pltpu.VMEM((2, side, tall), f32),
                pltpu.VMEM((2, side, tall), f32),
                pltpu.VMEM((n_row, 3, wide // n_row, tall), f32),
                pltpu.VMEM((n_row, 3, wide // n_row, tall), f32),
                pltpu.SMEM((3,), f32),
                pltpu.SMEM((3,), f32),
                pltpu.SMEM((3, 3), f32),
                pltpu.SemaphoreType.DMA((2, chunks)),
                pltpu.SemaphoreType.DMA((3,)),
                pltpu.SemaphoreType.DMA((2, 2, PARTS)),
                pltpu.SemaphoreType.DMA((2, 2, PARTS)),
                pltpu.SemaphoreType.DMA((2, PARTS)),
                pltpu.SemaphoreType.DMA((2, PARTS)),
                pltpu.SemaphoreType.DMA((8,)),
                pltpu.SemaphoreType.DMA((8,)),
                pltpu.SemaphoreType.DMA((n_row,)),
                pltpu.SemaphoreType.DMA((n_row,)),
                pltpu.SemaphoreType.REGULAR((2, 2)),
                pltpu.SemaphoreType.REGULAR,
            ],
            compiler_params=pltpu.CompilerParams(
                collective_id=0, has_side_effects=True, vmem_limit_bytes=VMEM_LIMIT
            ),
        )(*[
            pltpu.with_memory_space_constraint(a, pltpu.HBM)
            for a in (thermal_state, substance_label, thermal_coefficients, optical_thickness, substance_colours)
        ])
        return pl.pallas_call(
            deliver,
            out_shape=results,
            in_specs=[near, near],
            out_specs=(anywhere, anywhere),
            scratch_shapes=[pltpu.SemaphoreType.DMA((2,))],
            compiler_params=pltpu.CompilerParams(vmem_limit_bytes=VMEM_LIMIT),
        )(f, pic)

    placed = (P("row", "sx", "sy"), P("row", "sx", "sy"), P(), P(), P())
    return jax.shard_map(
        per_device,
        mesh=mesh,
        in_specs=placed,
        out_specs=(P("row", "sx", "sy"), P(None, ("sx", "row"), "sy")),
        check_vma=False,
    )
```

```python
import functools

import jax
import jax.numpy as jnp
from jax import lax
from jax.experimental import pallas as pl
from jax.experimental.pallas import tpu as pltpu
from jax.sharding import PartitionSpec as P

MESH = pl.DeviceIdType.MESH
SUB, LANES = 8, 128
FLUX, PACK, MARCH, PARTS = 4, 4, 4, 1
VMEM_LIMIT = 16 << 20


def kernel(
    sizes,
    t_hbm, lab_hbm, coef_hbm, thick_hbm, tint_hbm,
    f, pic_ref,
    u, d, h, ky, fy, lab, xs, xr, xs2, xr2, fx, ys, yr, ys2, yr2, turn, ib, rb,
    coef, thick, tint, lsem, csem, zsem1, zrec1, zsem2, zrec2, ssem, rsem, asem, bsem, hello, above,
):
    n_sx, n_sy, n_row = sizes
    depth, wide = t_hbm.shape[0], t_hbm.shape[1]
    blocks = wide // SUB
    per_group = LANES // depth
    groups = blocks // per_group
    chunks = depth // SUB
    last = depth
    per_part = blocks // PARTS
    me, my_sx, my_sy = lax.axis_index("row"), lax.axis_index("sx"), lax.axis_index("sy")
    has_prev, has_next = me > 0, me < n_row - 1
    has_left, has_right = my_sy > 0, my_sy < n_sy - 1

    def load(j):
        at, to = pl.ds(SUB * j, SUB), pl.ds(SUB * j + 1, SUB)
        return (
            pltpu.make_async_copy(lab_hbm.at[at], lab.at[to], lsem.at[0, j]),
            pltpu.make_async_copy(t_hbm.at[at], u.at[to], lsem.at[1, j]),
        )

    load_c = pltpu.make_async_copy(coef_hbm, coef, csem.at[0])
    load_k = pltpu.make_async_copy(thick_hbm, thick, csem.at[1])
    load_p = pltpu.make_async_copy(tint_hbm, tint, csem.at[2])
    load_c.start()
    for j in range(chunks):
        for copy in load(j):
            copy.start()
    load_k.start()
    load_p.start()

    sx_next = lax.rem(my_sx + 1, n_sx)
    sx_prev = lax.rem(my_sx + n_sx - 1, n_sx)
    to_next, to_prev = {"row": me + 1}, {"row": me - 1}
    to_right, to_left = {"sy": my_sy + 1}, {"sy": my_sy - 1}
    to_up, to_down = {"sx": sx_next}, {"sx": sx_prev}

    def only(cond, act):
        if cond is None:
            act()
        else:
            pl.when(cond)(act)

    barrier = pltpu.get_barrier_semaphore()
    near = (
        (has_prev, to_prev), (has_next, to_next), (has_right, to_right), (None, to_up), (None, to_down),
    )
    for there, where in near:
        only(there, functools.partial(pl.semaphore_signal, barrier, inc=1, device_id=where, device_id_type=MESH))

    lane = lax.broadcasted_iota(jnp.int32, (SUB, LANES), 1)
    sub = lax.broadcasted_iota(jnp.int32, (SUB, LANES), 0)
    at_ends = (lane == 0) | (lane == LANES - 1)
    is_even = (lane & 1) == 0
    pair = (((lane + 1) >> 1) & (LANES // 2 - 1), lane >> 1)
    zero = jnp.zeros((SUB, LANES), jnp.float32)
    one = jnp.ones((SUB, LANES), jnp.float32)

    def clear(cond, refs):
        @pl.when(jnp.logical_not(cond))
        def _():
            for r in refs:
                r[...] = jnp.zeros(r.shape, r.dtype)

    clear(has_prev, (u.at[0], d.at[0], h.at[0]))
    clear(has_next, (u.at[depth + 1], d.at[depth + 1], h.at[depth + 1]))
    clear(has_left, (yr.at[0], yr2.at[0]))
    clear(has_right, (yr.at[1], yr2.at[1]))

    def start(copies):
        for copy, sends, _ in copies:
            only(sends, copy.start)

    def arrive(copies):
        for copy, _, receives in copies:
            only(receives, copy.wait_recv)

    def left_here(copies):
        for copy, sends, _ in copies:
            only(sends, copy.wait_send)

    def remote(src, dst, send, recv, where):
        return pltpu.make_async_remote_copy(
            src_ref=src, dst_ref=dst, send_sem=send, recv_sem=recv, device_id=where, device_id_type=MESH
        )

    def z_first(p):
        at = pl.ds(SUB * per_part * p, SUB * per_part)
        got = []
        for i, (src, dst) in enumerate(((lab_hbm, lab), (t_hbm, u))):
            got.append((remote(src.at[depth - 1, at], dst.at[0, at], zsem1.at[0, i, p], zrec1.at[0, i, p], to_next),
                        has_next, has_prev))
            got.append((remote(src.at[0, at], dst.at[depth + 1, at], zsem1.at[1, i, p], zrec1.at[1, i, p], to_prev),
                        has_prev, has_next))
        return got

    def z_second(p):
        at = pl.ds(SUB * per_part * p, SUB * per_part)
        return [
            (remote(h.at[last, at], h.at[0, at], zsem2.at[0, p], zrec2.at[0, p], to_next), has_next, has_prev),
            (remote(h.at[1, at], h.at[depth + 1, at], zsem2.at[1, p], zrec2.at[1, p], to_prev), has_prev, has_next),
        ]

    def y_copies(src, dst, s):
        return (
            [(remote(src.at[0], dst.at[1], ssem.at[s + 1], rsem.at[s + 1], to_left), has_left, has_right)],
            [(remote(src.at[1], dst.at[0], ssem.at[s], rsem.at[s], to_right), has_right, has_left)],
        )

    def x_copies(src, dst, s):
        return [
            (remote(src.at[1], dst.at[0], ssem.at[s], rsem.at[s], to_up), None, None),
            (remote(src.at[0], dst.at[1], ssem.at[s + 1], rsem.at[s + 1], to_down), None, None),
        ]

    (y_down, y_up), x_first = y_copies(ys, yr, 0), x_copies(xs, xr, 2)
    (y_down2, y_up2), x_second = y_copies(ys2, yr2, 4), x_copies(xs2, xr2, 6)

    def enter():
        pl.semaphore_wait(barrier, 2 + sum(c.astype(jnp.int32) for c in (has_prev, has_next, has_left)))
        only(has_left, functools.partial(pl.semaphore_signal, above, inc=1, device_id=to_left, device_id_type=MESH))

    pl.when(my_sy == n_sy // 2)(enter)
    waits_long = has_right & (my_sy == n_sy // 2 - 1)
    waits_short = has_right & (my_sy != n_sy // 2 - 1)

    def greet(i, apart, act):
        for side, there, where in ((0, me >= apart, me - apart), (1, me + apart < n_row, me + apart)):
            @pl.when(there)
            def _():
                if act == "signal":
                    pl.semaphore_signal(hello.at[i, 1 - side], inc=1, device_id={"row": where}, device_id_type=MESH)
                else:
                    pl.semaphore_wait(hello.at[i, side], 1)

    def rows(xb):
        return pl.ds(SUB * xb, SUB)

    def spot(z0, xb):
        return depth * (xb % per_group) + z0

    def put(acc, v, z0, parity, xb):
        m = spot(z0, xb)
        at = (parity, xb // per_group)
        acc[at] = jnp.where(pair[parity] == m >> 1, pltpu.roll(v, m, 1), acc[at])

    def fresh():
        return {(p, g): zero for p in (0, 1) for g in range(groups)}

    def faces(acc, g):
        low = jnp.where(is_even, acc[0, g], acc[1, g])
        high = jnp.where(is_even, acc[1, g], acc[0, g])
        return low, pltpu.roll(high, 1, 1)

    load_c.wait()
    c0, c1, c2 = 0.5 * coef[0], 0.5 * coef[1], 0.5 * coef[2]

    def conduct(lb):
        return jnp.where(lb == 0, c0, jnp.where(lb == 1, c1, c2))

    def pack_first(j, carry):
        au, ad = [dict(c) for c in carry]
        for copy in load(j):
            copy.wait()
        for i in range(SUB):
            z0 = SUB * j + i
            for xb in range(blocks):
                v = u[z0 + 1, rows(xb), :]
                dv = conduct(lab[z0 + 1, rows(xb), :])
                d[z0 + 1, rows(xb), :] = dv
                put(au, v, z0, i % 2, xb)
                put(ad, dv, z0, i % 2, xb)
        return au, ad

    au, ad = lax.fori_loop(0, chunks, pack_first, (fresh(), fresh()))
    for g in range(groups):
        at = pl.ds(SUB * g, SUB)
        ys[0, 0, at, :], ys[1, 0, at, :] = faces(au, g)
        ys[0, 1, at, :], ys[1, 1, at, :] = faces(ad, g)
    pl.when(my_sy != n_sy // 2)(enter)
    start(y_down)

    def meet_above(cond):
        @pl.when(cond)
        def _():
            pl.semaphore_wait(above, 1)
            for copy, _, _ in y_up:
                copy.start()

    meet_above(waits_short)

    def edge(ref, first, k, side):
        flat = ref.reshape(ref.shape[0] * wide, LANES)
        got = None
        for i in range(SUB):
            row = flat[pl.ds((first + SUB * k + i) * wide + (wide - 1) * side, SUB, stride=0), :]
            got = row if got is None else jnp.where(sub == i, row, got)
        return got

    for side in (0, 1):
        for k in range(chunks):
            for i, a in enumerate((u, d)):
                xs[side, i, pl.ds(SUB * k, SUB), :] = edge(a, 1, k, side)

    start(x_first)
    for p in range(PARTS):
        start(z_first(p))

    def flux(da, db, ub, ua):
        return (da + db) * (ub - ua)

    def plane(src, dst, shift, z, fz, high, first_step):
        nf, before = [], None
        for xb in range(blocks):
            a, k = src[z, rows(xb), :], d[z, rows(xb), :]
            if xb < blocks - 1:
                at = pl.ds(SUB * xb + 1, SUB)
                fxx = flux(k, d[z, at, :], src[z, at, :], a)
            else:
                fxx = flux(k, pltpu.roll(k, SUB - 1, 0), pltpu.roll(a, SUB - 1, 0), a)
                fxx = jnp.where(sub == SUB - 1, 0.0, fxx)
            turned = pltpu.roll(fxx, 1, 0)
            behind = jnp.where(sub == 0, 0.0 if before is None else before, turned)
            before = turned
            if first_step:
                kk = k + pltpu.roll(k, LANES - 1, 1)
                ky[z - 1, rows(xb), :] = kk
            else:
                kk = ky[z - 1, rows(xb), :]
            gy = kk * (pltpu.roll(a, LANES - 1, 1) - a)
            fy[z - 1, rows(xb), :] = gy
            total = (fxx - behind) + gy
            if high:
                nz = flux(k, d[z + 1, rows(xb), :], src[z + 1, rows(xb), :], a)
                total = total + (nz if fz is None else nz - fz[xb])
                nf.append(nz)
            elif fz is not None:
                total = total - fz[xb]
            dst[z + shift, rows(xb), :] = a + total
        return tuple(nf)

    def between(src, z):
        return tuple(
            flux(d[z, rows(xb), :], d[z + 1, rows(xb), :], src[z + 1, rows(xb), :], src[z, rows(xb), :])
            for xb in range(blocks)
        )

    def planes(src, dst, shift, begin, count, fz, first_step):
        def several(j, fz):
            for i in range(FLUX):
                fz = plane(src, dst, shift, begin + FLUX * j + i, fz, True, first_step)
            return fz

        return lax.fori_loop(0, count // FLUX, several, fz)

    fz = plane(u, h, 0, 1, None, True, True)
    fz = planes(u, h, 0, 2, depth - FLUX, fz, True)
    for z in range(depth - FLUX + 2, last):
        fz = plane(u, h, 0, z, fz, True, True)
    plane(u, h, 0, last, fz, False, True)

    def settle(dst, shift):
        def some(j, carry):
            for i in range(FLUX):
                z0 = FLUX * j + i
                for xb in range(blocks):
                    dst[z0 + shift, rows(xb), :] = dst[z0 + shift, rows(xb), :] - pltpu.roll(fy[z0, rows(xb), :], 1, 1)
            return carry

        lax.fori_loop(0, depth // FLUX, some, 0)

    def sweep(first, trips, count, body, carry):
        def some(j, carry):
            for i in range(count):
                carry = body(count * j + first + i, carry, (first + i) % 2)
            return carry

        return lax.fori_loop(0, trips, some, carry)

    settle(h, 1)

    def pack_h(z0, acc, parity, which=range(blocks)):
        acc = dict(acc)
        for xb in which:
            put(acc, h[z0 + 1, rows(xb), :], z0, parity, xb)
        return acc

    acc = dict(sweep(0, depth // PACK, PACK, pack_h, fresh()))
    meet_above(waits_long)

    def x_faces(own, came):
        for side in (0, 1):
            for k in range(chunks):
                at = pl.ds(SUB * k, SUB)
                fx[side, at, :] = flux(xs[side, 1, at, :], xr[side, 1, at, :], came(side, at), own(side, at))

    def y_faces(own, came, with_high=True):
        even, odd, highs = [], [], []
        for g in range(groups):
            at = pl.ds(SUB * g, SUB)
            dl, dr, ul, ur = ys[0, 1, at, :], ys[1, 1, at, :], own(0, at), own(1, at)
            closed = flux(dl, dr, ul, ur)
            a = flux(dl, yr[0, 1, at, :], came(0, at), ul) + closed
            b = zero - closed
            if with_high:
                high = flux(dr, yr[1, 1, at, :], came(1, at), ur)
                highs.append(high)
                b = b + high
            b = pltpu.roll(b, LANES - 1, 1)
            even.append(jnp.where(is_even, a, b))
            odd.append(jnp.where(is_even, b, a))
        return (even, odd), highs

    def with_faces(v, packed, z0, parity, xb):
        r = pltpu.roll(packed[parity][xb // per_group], (LANES - spot(z0, xb)) & (LANES - 1), 1)
        v = jnp.where(at_ends, v + r, v)
        if xb == 0:
            v = jnp.where(sub == 0, v + fx[0, pl.ds(z0, SUB, stride=0), :], v)
        if xb == blocks - 1:
            v = jnp.where(sub == SUB - 1, v + fx[1, pl.ds(z0, SUB, stride=0), :], v)
        return v

    own_y, came_y = lambda s, at: ys[s, 0, at, :], lambda s, at: yr[s, 0, at, :]
    arrive(x_first)
    x_faces(lambda s, at: xs[s, 0, at, :], lambda s, at: xr[s, 0, at, :])
    arrive(y_up)
    packed, _ = y_faces(own_y, came_y, with_high=False)

    outer = ((0, 0, 0), (depth - 1, depth + 1, 1))
    brims = (0, blocks - 1)

    for p in (0, 1):
        for g in range(groups):
            acc[p, g] = acc[p, g] + packed[p][g]

    def pack_brims(z0, acc, parity):
        acc = dict(acc)
        for xb in brims:
            put(acc, with_faces(h[z0 + 1, rows(xb), :], packed, z0, parity, xb), z0, parity, xb)
        return acc

    acc = dict(sweep(1, 3, 10, pack_brims, acc))
    for p in range(PARTS):
        arrive(z_first(p))
    for (z0, ghost, parity), inside in zip(outer, (has_prev, has_next)):
        for xb in range(blocks):
            at = rows(xb)
            dg = jnp.where(inside, conduct(lab[ghost, at, :]), 0.0)
            d[ghost, at, :] = dg
            v = h[z0 + 1, at, :] + flux(d[z0 + 1, at, :], dg, u[ghost, at, :], u[z0 + 1, at, :])
            h[z0 + 1, at, :] = v
            put(acc, with_faces(v, packed, z0, parity, xb), z0, parity, xb)
    ends = [faces(acc, g) for g in range(groups)]
    for g in range(groups):
        ys2[0, pl.ds(SUB * g, SUB), :] = ends[g][0]
    start(y_down2)

    arrive(y_down)
    packed, highs = y_faces(own_y, came_y)
    for g in range(groups):
        ys2[1, pl.ds(SUB * g, SUB), :] = ends[g][1] + highs[g]
    start(y_up2)

    def fix_h(which):
        def body(z0, carry, parity):
            for xb in which:
                h[z0 + 1, rows(xb), :] = with_faces(h[z0 + 1, rows(xb), :], packed, z0, parity, xb)
            return carry

        return body

    for z0, _, parity in outer:
        fix_h(range(blocks))(z0, 0, parity)
    for p in range(PARTS):
        start(z_second(p))
    greet(0, 2, "signal")
    sweep(1, 3, 10, fix_h(brims), 0)
    for side in (0, 1):
        for k in range(chunks):
            xs2[side, pl.ds(SUB * k, SUB), :] = edge(h, 1, k, side)
    start(x_second)
    sweep(1, 5, 6, fix_h(range(1, blocks - 1)), 0)
    greet(0, 2, "wait")
    greet(1, 4, "signal")

    fz = plane(h, f, -1, 1, None, True, False)
    fz = planes(h, f, -1, 2, depth - FLUX, fz, False)
    for z in range(depth - FLUX + 2, last):
        fz = plane(h, f, -1, z, fz, True, False)
    plane(h, f, -1, last, fz, False, False)
    settle(f, 0)

    load_k.wait()
    scale = 0.5 / (depth * n_row)
    k0, k1, k2 = thick[0] * scale, thick[1] * scale, thick[2] * scale

    def opaque(v, lb):
        first, second = lb == 0, lb == 1
        half = jnp.where(first, k0, jnp.where(second, k1, k2))
        return half + half * jnp.tanh(0.5 * v), first, second

    arrive(x_second)
    x_faces(lambda s, at: xs2[s, at, :], lambda s, at: xr2[s, at, :])

    def brims_f(z0, carry, parity):
        for xb, side, at_row in ((0, 0, 0), (blocks - 1, 1, SUB - 1)):
            v = f[z0, rows(xb), :]
            f[z0, rows(xb), :] = jnp.where(sub == at_row, v + fx[side, pl.ds(z0, SUB, stride=0), :], v)
        return carry

    sweep(0, depth // SUB, SUB, brims_f, 0)
    for p in range(PARTS):
        arrive(z_second(p))
    arrive(y_up2)
    arrive(y_down2)
    packed2, _ = y_faces(lambda s, at: ys2[s, at, :], lambda s, at: yr2[s, at, :])
    for p in (0, 1):
        for g in range(groups):
            turn[p, pl.ds(SUB * g, SUB), :] = packed2[p][g]
    load_p.wait()

    def hand(o):
        dest = lax.rem(me + o, n_row)
        return pltpu.make_async_remote_copy(
            src_ref=ib.at[dest], dst_ref=rb.at[me], send_sem=asem.at[o], recv_sem=bsem.at[me],
            device_id={"row": dest}, device_id_type=MESH,
        )

    def march(dests):
        places = []
        for dest in dests:
            at = pl.ds(pl.multiple_of(dest * SUB, SUB), SUB)
            group = pl.ds(pl.multiple_of(dest // per_group * SUB, SUB), SUB)
            sides = [turn[parity, group, :] for parity in (0, 1)]
            places.append((at, sides, LANES - lax.rem(dest, per_group) * depth))

        def warm(chunk):
            got = {}
            for z0 in chunk:
                for i, (at, sides, m) in enumerate(places):
                    v = f[z0, at, :]
                    for edge_z, ghost in ((0, 0), (depth - 1, depth + 1)):
                        if z0 == edge_z:
                            v = v + flux(d[z0 + 1, at, :], d[ghost, at, :], h[ghost, at, :], h[z0 + 1, at, :])
                    got[z0, i] = jnp.where(at_ends, v + pltpu.roll(sides[z0 % 2], (m - z0) & (LANES - 1), 1), v)
            return got

        states = [(None, zero, zero)] * len(dests)
        steps = [range(k, k + MARCH) for k in range(0, depth, MARCH)]
        ahead = warm(steps[0])
        for k, chunk in enumerate(steps):
            now, ahead = ahead, warm(steps[k + 1]) if k + 1 < len(steps) else None
            for (z0, i), v in now.items():
                f[z0, places[i][0], :] = v
            for (z0, i), v in now.items():
                through, w0, w1 = states[i]
                w, first, second = opaque(v, lab[z0 + 1, places[i][0], :])
                if through is None:
                    through = 1.0 - w
                else:
                    w = through * w
                    through = through - w
                w0 = w0 + jnp.where(first, w, 0.0)
                w1 = w1 + jnp.where(second, w, 0.0)
                states[i] = (through, w0, w1)
        for dest, (through, w0, w1) in zip(dests, states):
            ib[dest, 0] = w0
            ib[dest, 1] = w1
            ib[dest, 2] = through

    greet(1, 4, "wait")
    half = n_row // 2
    order = [half + 1, half - 1, half] + [o for k in range(1, half - 1) for o in (n_row - k, k)] + [0]
    for k in range(0, n_row, 2):
        march([lax.rem(me + o, n_row) for o in order[k : k + 2]])
        for o in order[k : k + 2]:
            if o:
                hand(o).start()
    rb[me] = ib[me]

    for s in range(n_row):
        @pl.when(me != s)
        def _():
            pltpu.make_async_remote_copy(
                src_ref=ib.at[s], dst_ref=rb.at[s], send_sem=asem.at[0], recv_sem=bsem.at[s],
                device_id={"row": s}, device_id_type=MESH,
            ).wait_recv()

    through, w0, w1 = one, zero, zero
    for s in range(n_row):
        w0 = w0 + through * rb[s, 0]
        w1 = w1 + through * rb[s, 1]
        through = through * rb[s, 2]
    blocked = 1.0 - through
    w2 = (blocked - w0) - w1
    for c in range(3):
        pic_ref[c] = w0 * tint[0, c] + w1 * tint[1, c] + w2 * tint[2, c]
    pic_ref[3] = blocked

    for o in range(1, n_row):
        hand(o).wait_send()
    for p in range(PARTS):
        left_here(z_first(p))
        left_here(z_second(p))
    for copies in (y_down, y_up, x_first, y_down2, y_up2, x_second):
        left_here(copies)


def deliver(f, pic, out, out_pic, sem):
    a = pltpu.make_async_copy(f, out, sem.at[0])
    b = pltpu.make_async_copy(pic, out_pic, sem.at[1])
    a.start()
    b.start()
    a.wait()
    b.wait()


def solution(mesh):
    sizes = (mesh.shape["sx"], mesh.shape["sy"], mesh.shape["row"])
    n_row = sizes[2]

    def per_device(thermal_state, substance_label, thermal_coefficients, optical_thickness, substance_colours):
        depth, wide, tall = thermal_state.shape
        f32 = jnp.float32
        side = depth * wide // LANES
        near = pl.BlockSpec(memory_space=pltpu.VMEM)
        anywhere = pl.BlockSpec(memory_space=pl.ANY)
        chunks = depth // SUB
        results = (
            jax.ShapeDtypeStruct((depth, wide, tall), f32),
            jax.ShapeDtypeStruct((4, wide // n_row, tall), f32),
        )
        f, pic = pl.pallas_call(
            functools.partial(kernel, sizes),
            out_shape=results,
            in_specs=[anywhere] * 5,
            out_specs=(near, near),
            scratch_shapes=[
                pltpu.VMEM((depth + 2, wide, tall), f32),
                pltpu.VMEM((depth + 2, wide, tall), f32),
                pltpu.VMEM((depth + 2, wide, tall), f32),
                pltpu.VMEM((depth, wide, tall), f32),
                pltpu.VMEM((depth, wide, tall), f32),
                pltpu.VMEM((depth + 2, wide, tall), jnp.int32),
                pltpu.VMEM((2, 2, depth, tall), f32),
                pltpu.VMEM((2, 2, depth, tall), f32),
                pltpu.VMEM((2, depth, tall), f32),
                pltpu.VMEM((2, depth, tall), f32),
                pltpu.VMEM((2, depth + SUB, tall), f32),
                pltpu.VMEM((2, 2, side, tall), f32),
                pltpu.VMEM((2, 2, side, tall), f32),
                pltpu.VMEM((2, side, tall), f32),
                pltpu.VMEM((2, side, tall), f32),
                pltpu.VMEM((2, side, tall), f32),
                pltpu.VMEM((n_row, 3, wide // n_row, tall), f32),
                pltpu.VMEM((n_row, 3, wide // n_row, tall), f32),
                pltpu.SMEM((3,), f32),
                pltpu.SMEM((3,), f32),
                pltpu.SMEM((3, 3), f32),
                pltpu.SemaphoreType.DMA((2, chunks)),
                pltpu.SemaphoreType.DMA((3,)),
                pltpu.SemaphoreType.DMA((2, 2, PARTS)),
                pltpu.SemaphoreType.DMA((2, 2, PARTS)),
                pltpu.SemaphoreType.DMA((2, PARTS)),
                pltpu.SemaphoreType.DMA((2, PARTS)),
                pltpu.SemaphoreType.DMA((8,)),
                pltpu.SemaphoreType.DMA((8,)),
                pltpu.SemaphoreType.DMA((n_row,)),
                pltpu.SemaphoreType.DMA((n_row,)),
                pltpu.SemaphoreType.REGULAR((2, 2)),
                pltpu.SemaphoreType.REGULAR,
            ],
            compiler_params=pltpu.CompilerParams(
                collective_id=0, has_side_effects=True, vmem_limit_bytes=VMEM_LIMIT
            ),
        )(*[
            pltpu.with_memory_space_constraint(a, pltpu.HBM)
            for a in (thermal_state, substance_label, thermal_coefficients, optical_thickness, substance_colours)
        ])
        return pl.pallas_call(
            deliver,
            out_shape=results,
            in_specs=[near, near],
            out_specs=(anywhere, anywhere),
            scratch_shapes=[pltpu.SemaphoreType.DMA((2,))],
            compiler_params=pltpu.CompilerParams(vmem_limit_bytes=VMEM_LIMIT),
        )(f, pic)

    placed = (P("row", "sx", "sy"), P("row", "sx", "sy"), P(), P(), P())
    return jax.shard_map(
        per_device,
        mesh=mesh,
        in_specs=placed,
        out_specs=(P("row", "sx", "sy"), P(None, ("sx", "row"), "sy")),
        check_vma=False,
    )
```

```python
import functools

import jax
import jax.numpy as jnp
from jax import lax
from jax.experimental import pallas as pl
from jax.experimental.pallas import tpu as pltpu
from jax.sharding import PartitionSpec as P

MESH = pl.DeviceIdType.MESH
SUB, LANES = 8, 128
FLUX, PACK, MARCH, PARTS = 4, 4, 4, 1
VMEM_LIMIT = 16 << 20


def kernel(
    sizes,
    t_hbm, lab_hbm, coef_hbm, thick_hbm, tint_hbm,
    f, pic_ref,
    u, d, h, ky, fy, lab, xs, xr, xs2, xr2, fx, ys, yr, ys2, yr2, turn, ib, rb,
    coef, thick, tint, lsem, csem, zsem1, zrec1, zsem2, zrec2, ssem, rsem, asem, bsem, hello, above,
):
    n_sx, n_sy, n_row = sizes
    depth, wide = t_hbm.shape[0], t_hbm.shape[1]
    blocks = wide // SUB
    per_group = LANES // depth
    groups = blocks // per_group
    chunks = depth // SUB
    last = depth
    per_part = blocks // PARTS
    me, my_sx, my_sy = lax.axis_index("row"), lax.axis_index("sx"), lax.axis_index("sy")
    has_prev, has_next = me > 0, me < n_row - 1
    has_left, has_right = my_sy > 0, my_sy < n_sy - 1

    def load(j):
        at, to = pl.ds(SUB * j, SUB), pl.ds(SUB * j + 1, SUB)
        return (
            pltpu.make_async_copy(lab_hbm.at[at], lab.at[to], lsem.at[0, j]),
            pltpu.make_async_copy(t_hbm.at[at], u.at[to], lsem.at[1, j]),
        )

    load_c = pltpu.make_async_copy(coef_hbm, coef, csem.at[0])
    load_k = pltpu.make_async_copy(thick_hbm, thick, csem.at[1])
    load_p = pltpu.make_async_copy(tint_hbm, tint, csem.at[2])
    load_c.start()
    for j in range(chunks):
        for copy in load(j):
            copy.start()
    load_k.start()
    load_p.start()

    sx_next = lax.rem(my_sx + 1, n_sx)
    sx_prev = lax.rem(my_sx + n_sx - 1, n_sx)
    to_next, to_prev = {"row": me + 1}, {"row": me - 1}
    to_right, to_left = {"sy": my_sy + 1}, {"sy": my_sy - 1}
    to_up, to_down = {"sx": sx_next}, {"sx": sx_prev}

    def only(cond, act):
        if cond is None:
            act()
        else:
            pl.when(cond)(act)

    barrier = pltpu.get_barrier_semaphore()
    near = (
        (has_prev, to_prev), (has_next, to_next), (has_right, to_right), (None, to_up), (None, to_down),
    )
    for there, where in near:
        only(there, functools.partial(pl.semaphore_signal, barrier, inc=1, device_id=where, device_id_type=MESH))

    lane = lax.broadcasted_iota(jnp.int32, (SUB, LANES), 1)
    sub = lax.broadcasted_iota(jnp.int32, (SUB, LANES), 0)
    at_ends = (lane == 0) | (lane == LANES - 1)
    is_even = (lane & 1) == 0
    pair = (((lane + 1) >> 1) & (LANES // 2 - 1), lane >> 1)
    zero = jnp.zeros((SUB, LANES), jnp.float32)
    one = jnp.ones((SUB, LANES), jnp.float32)

    def clear(cond, refs):
        @pl.when(jnp.logical_not(cond))
        def _():
            for r in refs:
                r[...] = jnp.zeros(r.shape, r.dtype)

    clear(has_prev, (u.at[0], d.at[0], h.at[0]))
    clear(has_next, (u.at[depth + 1], d.at[depth + 1], h.at[depth + 1]))
    clear(has_left, (yr.at[0], yr2.at[0]))
    clear(has_right, (yr.at[1], yr2.at[1]))

    def start(copies):
        for copy, sends, _ in copies:
            only(sends, copy.start)

    def arrive(copies):
        for copy, _, receives in copies:
            only(receives, copy.wait_recv)

    def left_here(copies):
        for copy, sends, _ in copies:
            only(sends, copy.wait_send)

    def remote(src, dst, send, recv, where):
        return pltpu.make_async_remote_copy(
            src_ref=src, dst_ref=dst, send_sem=send, recv_sem=recv, device_id=where, device_id_type=MESH
        )

    def z_first(p):
        at = pl.ds(SUB * per_part * p, SUB * per_part)
        got = []
        for i, (src, dst) in enumerate(((lab_hbm, lab), (t_hbm, u))):
            got.append((remote(src.at[depth - 1, at], dst.at[0, at], zsem1.at[0, i, p], zrec1.at[0, i, p], to_next),
                        has_next, has_prev))
            got.append((remote(src.at[0, at], dst.at[depth + 1, at], zsem1.at[1, i, p], zrec1.at[1, i, p], to_prev),
                        has_prev, has_next))
        return got

    def z_second(p):
        at = pl.ds(SUB * per_part * p, SUB * per_part)
        return [
            (remote(h.at[last, at], h.at[0, at], zsem2.at[0, p], zrec2.at[0, p], to_next), has_next, has_prev),
            (remote(h.at[1, at], h.at[depth + 1, at], zsem2.at[1, p], zrec2.at[1, p], to_prev), has_prev, has_next),
        ]

    def y_copies(src, dst, s):
        return (
            [(remote(src.at[0], dst.at[1], ssem.at[s + 1], rsem.at[s + 1], to_left), has_left, has_right)],
            [(remote(src.at[1], dst.at[0], ssem.at[s], rsem.at[s], to_right), has_right, has_left)],
        )

    def x_copies(src, dst, s):
        return [
            (remote(src.at[1], dst.at[0], ssem.at[s], rsem.at[s], to_up), None, None),
            (remote(src.at[0], dst.at[1], ssem.at[s + 1], rsem.at[s + 1], to_down), None, None),
        ]

    (y_down, y_up), x_first = y_copies(ys, yr, 0), x_copies(xs, xr, 2)
    (y_down2, y_up2), x_second = y_copies(ys2, yr2, 4), x_copies(xs2, xr2, 6)

    def enter():
        pl.semaphore_wait(barrier, 2 + sum(c.astype(jnp.int32) for c in (has_prev, has_next, has_left)))
        only(has_left, functools.partial(pl.semaphore_signal, above, inc=1, device_id=to_left, device_id_type=MESH))

    pl.when(my_sy == n_sy // 2)(enter)
    waits_long = has_right & (my_sy == n_sy // 2 - 1)
    waits_short = has_right & (my_sy != n_sy // 2 - 1)

    def greet(i, apart, act):
        for side, there, where in ((0, me >= apart, me - apart), (1, me + apart < n_row, me + apart)):
            @pl.when(there)
            def _():
                if act == "signal":
                    pl.semaphore_signal(hello.at[i, 1 - side], inc=1, device_id={"row": where}, device_id_type=MESH)
                else:
                    pl.semaphore_wait(hello.at[i, side], 1)

    def rows(xb):
        return pl.ds(SUB * xb, SUB)

    def spot(z0, xb):
        return depth * (xb % per_group) + z0

    def put(acc, v, z0, parity, xb):
        m = spot(z0, xb)
        at = (parity, xb // per_group)
        acc[at] = jnp.where(pair[parity] == m >> 1, pltpu.roll(v, m, 1), acc[at])

    def fresh():
        return {(p, g): zero for p in (0, 1) for g in range(groups)}

    def faces(acc, g):
        low = jnp.where(is_even, acc[0, g], acc[1, g])
        high = jnp.where(is_even, acc[1, g], acc[0, g])
        return low, pltpu.roll(high, 1, 1)

    load_c.wait()
    c0, c1, c2 = 0.5 * coef[0], 0.5 * coef[1], 0.5 * coef[2]

    def conduct(lb):
        return jnp.where(lb == 0, c0, jnp.where(lb == 1, c1, c2))

    def pack_first(j, carry):
        au, ad = [dict(c) for c in carry]
        for copy in load(j):
            copy.wait()
        for i in range(SUB):
            z0 = SUB * j + i
            for xb in range(blocks):
                v = u[z0 + 1, rows(xb), :]
                dv = conduct(lab[z0 + 1, rows(xb), :])
                d[z0 + 1, rows(xb), :] = dv
                put(au, v, z0, i % 2, xb)
                put(ad, dv, z0, i % 2, xb)
        return au, ad

    au, ad = lax.fori_loop(0, chunks, pack_first, (fresh(), fresh()))
    for g in range(groups):
        at = pl.ds(SUB * g, SUB)
        ys[0, 0, at, :], ys[1, 0, at, :] = faces(au, g)
        ys[0, 1, at, :], ys[1, 1, at, :] = faces(ad, g)
    pl.when(my_sy != n_sy // 2)(enter)
    start(y_down)

    def meet_above(cond):
        @pl.when(cond)
        def _():
            pl.semaphore_wait(above, 1)
            for copy, _, _ in y_up:
                copy.start()

    meet_above(waits_short)

    def edge(ref, first, k, side):
        flat = ref.reshape(ref.shape[0] * wide, LANES)
        got = None
        for i in range(SUB):
            row = flat[pl.ds((first + SUB * k + i) * wide + (wide - 1) * side, SUB, stride=0), :]
            got = row if got is None else jnp.where(sub == i, row, got)
        return got

    for side in (0, 1):
        for k in range(chunks):
            for i, a in enumerate((u, d)):
                xs[side, i, pl.ds(SUB * k, SUB), :] = edge(a, 1, k, side)

    start(x_first)
    for p in range(PARTS):
        start(z_first(p))

    def flux(da, db, ub, ua):
        return (da + db) * (ub - ua)

    def plane(src, dst, shift, z, fz, high, first_step):
        nf, before = [], None
        for xb in range(blocks):
            a, k = src[z, rows(xb), :], d[z, rows(xb), :]
            if xb < blocks - 1:
                at = pl.ds(SUB * xb + 1, SUB)
                fxx = flux(k, d[z, at, :], src[z, at, :], a)
            else:
                fxx = flux(k, pltpu.roll(k, SUB - 1, 0), pltpu.roll(a, SUB - 1, 0), a)
                fxx = jnp.where(sub == SUB - 1, 0.0, fxx)
            turned = pltpu.roll(fxx, 1, 0)
            behind = jnp.where(sub == 0, 0.0 if before is None else before, turned)
            before = turned
            if first_step:
                kk = k + pltpu.roll(k, LANES - 1, 1)
                ky[z - 1, rows(xb), :] = kk
            else:
                kk = ky[z - 1, rows(xb), :]
            gy = kk * (pltpu.roll(a, LANES - 1, 1) - a)
            fy[z - 1, rows(xb), :] = gy
            total = (fxx - behind) + gy
            if high:
                nz = flux(k, d[z + 1, rows(xb), :], src[z + 1, rows(xb), :], a)
                total = total + (nz if fz is None else nz - fz[xb])
                nf.append(nz)
            elif fz is not None:
                total = total - fz[xb]
            dst[z + shift, rows(xb), :] = a + total
        return tuple(nf)

    def between(src, z):
        return tuple(
            flux(d[z, rows(xb), :], d[z + 1, rows(xb), :], src[z + 1, rows(xb), :], src[z, rows(xb), :])
            for xb in range(blocks)
        )

    def planes(src, dst, shift, begin, count, fz, first_step):
        def several(j, fz):
            for i in range(FLUX):
                fz = plane(src, dst, shift, begin + FLUX * j + i, fz, True, first_step)
            return fz

        return lax.fori_loop(0, count // FLUX, several, fz)

    fz = plane(u, h, 0, 1, None, True, True)
    fz = planes(u, h, 0, 2, depth - FLUX, fz, True)
    for z in range(depth - FLUX + 2, last):
        fz = plane(u, h, 0, z, fz, True, True)
    plane(u, h, 0, last, fz, False, True)

    def settle(dst, shift):
        def some(j, carry):
            for i in range(FLUX):
                z0 = FLUX * j + i
                for xb in range(blocks):
                    dst[z0 + shift, rows(xb), :] = dst[z0 + shift, rows(xb), :] - pltpu.roll(fy[z0, rows(xb), :], 1, 1)
            return carry

        lax.fori_loop(0, depth // FLUX, some, 0)

    def sweep(first, trips, count, body, carry):
        def some(j, carry):
            for i in range(count):
                carry = body(count * j + first + i, carry, (first + i) % 2)
            return carry

        return lax.fori_loop(0, trips, some, carry)

    settle(h, 1)

    def pack_h(z0, acc, parity, which=range(blocks)):
        acc = dict(acc)
        for xb in which:
            put(acc, h[z0 + 1, rows(xb), :], z0, parity, xb)
        return acc

    acc = dict(sweep(0, depth // PACK, PACK, pack_h, fresh()))
    meet_above(waits_long)

    def x_faces(own, came):
        for side in (0, 1):
            for k in range(chunks):
                at = pl.ds(SUB * k, SUB)
                fx[side, at, :] = flux(xs[side, 1, at, :], xr[side, 1, at, :], came(side, at), own(side, at))

    def y_faces(own, came, with_high=True):
        even, odd, highs = [], [], []
        for g in range(groups):
            at = pl.ds(SUB * g, SUB)
            dl, dr, ul, ur = ys[0, 1, at, :], ys[1, 1, at, :], own(0, at), own(1, at)
            closed = flux(dl, dr, ul, ur)
            a = flux(dl, yr[0, 1, at, :], came(0, at), ul) + closed
            b = zero - closed
            if with_high:
                high = flux(dr, yr[1, 1, at, :], came(1, at), ur)
                highs.append(high)
                b = b + high
            b = pltpu.roll(b, LANES - 1, 1)
            even.append(jnp.where(is_even, a, b))
            odd.append(jnp.where(is_even, b, a))
        return (even, odd), highs

    def with_faces(v, packed, z0, parity, xb):
        r = pltpu.roll(packed[parity][xb // per_group], (LANES - spot(z0, xb)) & (LANES - 1), 1)
        v = jnp.where(at_ends, v + r, v)
        if xb == 0:
            v = jnp.where(sub == 0, v + fx[0, pl.ds(z0, SUB, stride=0), :], v)
        if xb == blocks - 1:
            v = jnp.where(sub == SUB - 1, v + fx[1, pl.ds(z0, SUB, stride=0), :], v)
        return v

    own_y, came_y = lambda s, at: ys[s, 0, at, :], lambda s, at: yr[s, 0, at, :]
    arrive(x_first)
    x_faces(lambda s, at: xs[s, 0, at, :], lambda s, at: xr[s, 0, at, :])
    arrive(y_up)
    packed, _ = y_faces(own_y, came_y, with_high=False)

    outer = ((0, 0, 0), (depth - 1, depth + 1, 1))
    brims = (0, blocks - 1)

    for p in (0, 1):
        for g in range(groups):
            acc[p, g] = acc[p, g] + packed[p][g]

    def pack_brims(z0, acc, parity):
        acc = dict(acc)
        for xb in brims:
            put(acc, with_faces(h[z0 + 1, rows(xb), :], packed, z0, parity, xb), z0, parity, xb)
        return acc

    acc = dict(sweep(1, 3, 10, pack_brims, acc))
    for p in range(PARTS):
        arrive(z_first(p))
    for (z0, ghost, parity), inside in zip(outer, (has_prev, has_next)):
        for xb in range(blocks):
            at = rows(xb)
            dg = jnp.where(inside, conduct(lab[ghost, at, :]), 0.0)
            d[ghost, at, :] = dg
            v = h[z0 + 1, at, :] + flux(d[z0 + 1, at, :], dg, u[ghost, at, :], u[z0 + 1, at, :])
            h[z0 + 1, at, :] = v
            put(acc, with_faces(v, packed, z0, parity, xb), z0, parity, xb)
    ends = [faces(acc, g) for g in range(groups)]
    for g in range(groups):
        ys2[0, pl.ds(SUB * g, SUB), :] = ends[g][0]
    start(y_down2)

    arrive(y_down)
    packed, highs = y_faces(own_y, came_y)
    for g in range(groups):
        ys2[1, pl.ds(SUB * g, SUB), :] = ends[g][1] + highs[g]
    start(y_up2)

    def fix_h(which):
        def body(z0, carry, parity):
            for xb in which:
                h[z0 + 1, rows(xb), :] = with_faces(h[z0 + 1, rows(xb), :], packed, z0, parity, xb)
            return carry

        return body

    for z0, _, parity in outer:
        fix_h(range(blocks))(z0, 0, parity)
    for p in range(PARTS):
        start(z_second(p))
    greet(0, 2, "signal")
    sweep(1, 3, 10, fix_h(brims), 0)
    for side in (0, 1):
        for k in range(chunks):
            xs2[side, pl.ds(SUB * k, SUB), :] = edge(h, 1, k, side)
    start(x_second)
    sweep(1, 5, 6, fix_h(range(1, blocks - 1)), 0)
    greet(0, 2, "wait")
    greet(1, 4, "signal")

    fz = plane(h, f, -1, 1, None, True, False)
    fz = planes(h, f, -1, 2, depth - FLUX, fz, False)
    for z in range(depth - FLUX + 2, last):
        fz = plane(h, f, -1, z, fz, True, False)
    plane(h, f, -1, last, fz, False, False)
    settle(f, 0)

    load_k.wait()
    scale = 0.5 / (depth * n_row)
    k0, k1, k2 = thick[0] * scale, thick[1] * scale, thick[2] * scale

    def opaque(v, lb):
        first, second = lb == 0, lb == 1
        half = jnp.where(first, k0, jnp.where(second, k1, k2))
        return half + half * jnp.tanh(0.5 * v), first, second

    arrive(x_second)
    x_faces(lambda s, at: xs2[s, at, :], lambda s, at: xr2[s, at, :])

    def brims_f(z0, carry, parity):
        for xb, side, at_row in ((0, 0, 0), (blocks - 1, 1, SUB - 1)):
            v = f[z0, rows(xb), :]
            f[z0, rows(xb), :] = jnp.where(sub == at_row, v + fx[side, pl.ds(z0, SUB, stride=0), :], v)
        return carry

    sweep(0, depth // SUB, SUB, brims_f, 0)
    for p in range(PARTS):
        arrive(z_second(p))
    arrive(y_up2)
    arrive(y_down2)
    packed2, _ = y_faces(lambda s, at: ys2[s, at, :], lambda s, at: yr2[s, at, :])
    for p in (0, 1):
        for g in range(groups):
            turn[p, pl.ds(SUB * g, SUB), :] = packed2[p][g]
    load_p.wait()

    def hand(o):
        dest = lax.rem(me + o, n_row)
        return pltpu.make_async_remote_copy(
            src_ref=ib.at[dest], dst_ref=rb.at[me], send_sem=asem.at[o], recv_sem=bsem.at[me],
            device_id={"row": dest}, device_id_type=MESH,
        )

    def march(dests):
        places = []
        for dest in dests:
            at = pl.ds(pl.multiple_of(dest * SUB, SUB), SUB)
            group = pl.ds(pl.multiple_of(dest // per_group * SUB, SUB), SUB)
            sides = [turn[parity, group, :] for parity in (0, 1)]
            places.append((at, sides, LANES - lax.rem(dest, per_group) * depth))

        def warm(chunk):
            got = {}
            for z0 in chunk:
                for i, (at, sides, m) in enumerate(places):
                    v = f[z0, at, :]
                    for edge_z, ghost in ((0, 0), (depth - 1, depth + 1)):
                        if z0 == edge_z:
                            v = v + flux(d[z0 + 1, at, :], d[ghost, at, :], h[ghost, at, :], h[z0 + 1, at, :])
                    got[z0, i] = jnp.where(at_ends, v + pltpu.roll(sides[z0 % 2], (m - z0) & (LANES - 1), 1), v)
            return got

        states = [(None, zero, zero)] * len(dests)
        steps = [range(k, k + MARCH) for k in range(0, depth, MARCH)]
        ahead = warm(steps[0])
        for k, chunk in enumerate(steps):
            now, ahead = ahead, warm(steps[k + 1]) if k + 1 < len(steps) else None
            for (z0, i), v in now.items():
                f[z0, places[i][0], :] = v
            for (z0, i), v in now.items():
                through, w0, w1 = states[i]
                w, first, second = opaque(v, lab[z0 + 1, places[i][0], :])
                if through is None:
                    through = 1.0 - w
                else:
                    w = through * w
                    through = through - w
                w0 = w0 + jnp.where(first, w, 0.0)
                w1 = w1 + jnp.where(second, w, 0.0)
                states[i] = (through, w0, w1)
        for dest, (through, w0, w1) in zip(dests, states):
            ib[dest, 0] = w0
            ib[dest, 1] = w1
            ib[dest, 2] = through

    greet(1, 4, "wait")
    half = n_row // 2
    order = [half + 1, half - 1, half] + [o for k in range(1, half - 1) for o in (n_row - k, k)] + [0]
    for k in range(0, n_row, 2):
        march([lax.rem(me + o, n_row) for o in order[k : k + 2]])
        for o in order[k : k + 2]:
            if o:
                hand(o).start()
    rb[me] = ib[me]

    for s in range(n_row):
        @pl.when(me != s)
        def _():
            pltpu.make_async_remote_copy(
                src_ref=ib.at[s], dst_ref=rb.at[s], send_sem=asem.at[0], recv_sem=bsem.at[s],
                device_id={"row": s}, device_id_type=MESH,
            ).wait_recv()

    through, w0, w1 = one, zero, zero
    for s in range(n_row):
        w0 = w0 + through * rb[s, 0]
        w1 = w1 + through * rb[s, 1]
        through = through * rb[s, 2]
    blocked = 1.0 - through
    w2 = (blocked - w0) - w1
    for c in range(3):
        pic_ref[c] = w0 * tint[0, c] + w1 * tint[1, c] + w2 * tint[2, c]
    pic_ref[3] = blocked

    for o in range(1, n_row):
        hand(o).wait_send()
    for p in range(PARTS):
        left_here(z_first(p))
        left_here(z_second(p))
    for copies in (y_down, y_up, x_first, y_down2, y_up2, x_second):
        left_here(copies)


def deliver(f, pic, out, out_pic, sem):
    half = f.shape[0] // 2
    copies = [
        pltpu.make_async_copy(f.at[pl.ds(half * i, half)], out.at[pl.ds(half * i, half)], sem.at[i]) for i in (0, 1)
    ]
    last = pltpu.make_async_copy(pic, out_pic, sem.at[2])
    copies[0].start(priority=0)
    copies[1].start(priority=1)
    last.start(priority=1)
    for copy in copies + [last]:
        copy.wait()


def solution(mesh):
    sizes = (mesh.shape["sx"], mesh.shape["sy"], mesh.shape["row"])
    n_row = sizes[2]

    def per_device(thermal_state, substance_label, thermal_coefficients, optical_thickness, substance_colours):
        depth, wide, tall = thermal_state.shape
        f32 = jnp.float32
        side = depth * wide // LANES
        near = pl.BlockSpec(memory_space=pltpu.VMEM)
        anywhere = pl.BlockSpec(memory_space=pl.ANY)
        chunks = depth // SUB
        results = (
            jax.ShapeDtypeStruct((depth, wide, tall), f32),
            jax.ShapeDtypeStruct((4, wide // n_row, tall), f32),
        )
        f, pic = pl.pallas_call(
            functools.partial(kernel, sizes),
            out_shape=results,
            in_specs=[anywhere] * 5,
            out_specs=(near, near),
            scratch_shapes=[
                pltpu.VMEM((depth + 2, wide, tall), f32),
                pltpu.VMEM((depth + 2, wide, tall), f32),
                pltpu.VMEM((depth + 2, wide, tall), f32),
                pltpu.VMEM((depth, wide, tall), f32),
                pltpu.VMEM((depth, wide, tall), f32),
                pltpu.VMEM((depth + 2, wide, tall), jnp.int32),
                pltpu.VMEM((2, 2, depth, tall), f32),
                pltpu.VMEM((2, 2, depth, tall), f32),
                pltpu.VMEM((2, depth, tall), f32),
                pltpu.VMEM((2, depth, tall), f32),
                pltpu.VMEM((2, depth + SUB, tall), f32),
                pltpu.VMEM((2, 2, side, tall), f32),
                pltpu.VMEM((2, 2, side, tall), f32),
                pltpu.VMEM((2, side, tall), f32),
                pltpu.VMEM((2, side, tall), f32),
                pltpu.VMEM((2, side, tall), f32),
                pltpu.VMEM((n_row, 3, wide // n_row, tall), f32),
                pltpu.VMEM((n_row, 3, wide // n_row, tall), f32),
                pltpu.SMEM((3,), f32),
                pltpu.SMEM((3,), f32),
                pltpu.SMEM((3, 3), f32),
                pltpu.SemaphoreType.DMA((2, chunks)),
                pltpu.SemaphoreType.DMA((3,)),
                pltpu.SemaphoreType.DMA((2, 2, PARTS)),
                pltpu.SemaphoreType.DMA((2, 2, PARTS)),
                pltpu.SemaphoreType.DMA((2, PARTS)),
                pltpu.SemaphoreType.DMA((2, PARTS)),
                pltpu.SemaphoreType.DMA((8,)),
                pltpu.SemaphoreType.DMA((8,)),
                pltpu.SemaphoreType.DMA((n_row,)),
                pltpu.SemaphoreType.DMA((n_row,)),
                pltpu.SemaphoreType.REGULAR((2, 2)),
                pltpu.SemaphoreType.REGULAR,
            ],
            compiler_params=pltpu.CompilerParams(
                collective_id=0, has_side_effects=True, vmem_limit_bytes=VMEM_LIMIT
            ),
        )(*[
            pltpu.with_memory_space_constraint(a, pltpu.HBM)
            for a in (thermal_state, substance_label, thermal_coefficients, optical_thickness, substance_colours)
        ])
        return pl.pallas_call(
            deliver,
            out_shape=results,
            in_specs=[near, near],
            out_specs=(anywhere, anywhere),
            scratch_shapes=[pltpu.SemaphoreType.DMA((3,))],
            compiler_params=pltpu.CompilerParams(vmem_limit_bytes=VMEM_LIMIT),
        )(f, pic)

    placed = (P("row", "sx", "sy"), P("row", "sx", "sy"), P(), P(), P())
    return jax.shard_map(
        per_device,
        mesh=mesh,
        in_specs=placed,
        out_specs=(P("row", "sx", "sy"), P(None, ("sx", "row"), "sy")),
        check_vma=False,
    )
```

```python
import functools

import jax
import jax.numpy as jnp
from jax import lax
from jax.experimental import pallas as pl
from jax.experimental.pallas import tpu as pltpu
from jax.sharding import PartitionSpec as P

MESH = pl.DeviceIdType.MESH
SUB, LANES = 8, 128
FLUX, PACK, MARCH, PARTS = 4, 4, 4, 1
VMEM_LIMIT = 16 << 20


def kernel(
    sizes,
    t_hbm, lab_hbm, coef_hbm, thick_hbm, tint_hbm,
    f, pic_ref,
    u, d, h, ky, fy, lab, xs, xr, xs2, xr2, fx, ys, yr, ys2, yr2, turn, ib, rb,
    coef, thick, tint, lsem, csem, zsem1, zrec1, zsem2, zrec2, ssem, rsem, asem, bsem, hello, above,
):
    n_sx, n_sy, n_row = sizes
    depth, wide = t_hbm.shape[0], t_hbm.shape[1]
    blocks = wide // SUB
    per_group = LANES // depth
    groups = blocks // per_group
    chunks = depth // SUB
    last = depth
    per_part = blocks // PARTS
    me, my_sx, my_sy = lax.axis_index("row"), lax.axis_index("sx"), lax.axis_index("sy")
    has_prev, has_next = me > 0, me < n_row - 1
    has_left, has_right = my_sy > 0, my_sy < n_sy - 1

    def load(j):
        at, to = pl.ds(SUB * j, SUB), pl.ds(SUB * j + 1, SUB)
        return (
            pltpu.make_async_copy(lab_hbm.at[at], lab.at[to], lsem.at[0, j]),
            pltpu.make_async_copy(t_hbm.at[at], u.at[to], lsem.at[1, j]),
        )

    load_c = pltpu.make_async_copy(coef_hbm, coef, csem.at[0])
    load_k = pltpu.make_async_copy(thick_hbm, thick, csem.at[1])
    load_p = pltpu.make_async_copy(tint_hbm, tint, csem.at[2])
    sx_next = lax.rem(my_sx + 1, n_sx)
    sx_prev = lax.rem(my_sx + n_sx - 1, n_sx)
    to_next, to_prev = {"row": me + 1}, {"row": me - 1}
    to_right, to_left = {"sy": my_sy + 1}, {"sy": my_sy - 1}
    to_up, to_down = {"sx": sx_next}, {"sx": sx_prev}

    def only(cond, act):
        if cond is None:
            act()
        else:
            pl.when(cond)(act)

    barrier = pltpu.get_barrier_semaphore()
    near = (
        (has_prev, to_prev), (has_next, to_next), (has_right, to_right), (None, to_up), (None, to_down),
    )
    for there, where in near:
        only(there, functools.partial(pl.semaphore_signal, barrier, inc=1, device_id=where, device_id_type=MESH))

    load_c.start()
    for j in range(chunks):
        for copy in load(j):
            copy.start()
    load_k.start()
    load_p.start()

    lane = lax.broadcasted_iota(jnp.int32, (SUB, LANES), 1)
    sub = lax.broadcasted_iota(jnp.int32, (SUB, LANES), 0)
    at_ends = (lane == 0) | (lane == LANES - 1)
    is_even = (lane & 1) == 0
    pair = (((lane + 1) >> 1) & (LANES // 2 - 1), lane >> 1)
    zero = jnp.zeros((SUB, LANES), jnp.float32)
    one = jnp.ones((SUB, LANES), jnp.float32)

    def clear(cond, refs):
        @pl.when(jnp.logical_not(cond))
        def _():
            for r in refs:
                r[...] = jnp.zeros(r.shape, r.dtype)

    clear(has_prev, (u.at[0], d.at[0], h.at[0]))
    clear(has_next, (u.at[depth + 1], d.at[depth + 1], h.at[depth + 1]))
    clear(has_left, (yr.at[0], yr2.at[0]))
    clear(has_right, (yr.at[1], yr2.at[1]))

    def start(copies):
        for copy, sends, _ in copies:
            only(sends, copy.start)

    def arrive(copies):
        for copy, _, receives in copies:
            only(receives, copy.wait_recv)

    def left_here(copies):
        for copy, sends, _ in copies:
            only(sends, copy.wait_send)

    def remote(src, dst, send, recv, where):
        return pltpu.make_async_remote_copy(
            src_ref=src, dst_ref=dst, send_sem=send, recv_sem=recv, device_id=where, device_id_type=MESH
        )

    def z_first(p):
        at = pl.ds(SUB * per_part * p, SUB * per_part)
        got = []
        for i, (src, dst) in enumerate(((lab_hbm, lab), (t_hbm, u))):
            got.append((remote(src.at[depth - 1, at], dst.at[0, at], zsem1.at[0, i, p], zrec1.at[0, i, p], to_next),
                        has_next, has_prev))
            got.append((remote(src.at[0, at], dst.at[depth + 1, at], zsem1.at[1, i, p], zrec1.at[1, i, p], to_prev),
                        has_prev, has_next))
        return got

    def z_second(p):
        at = pl.ds(SUB * per_part * p, SUB * per_part)
        return [
            (remote(h.at[last, at], h.at[0, at], zsem2.at[0, p], zrec2.at[0, p], to_next), has_next, has_prev),
            (remote(h.at[1, at], h.at[depth + 1, at], zsem2.at[1, p], zrec2.at[1, p], to_prev), has_prev, has_next),
        ]

    def y_copies(src, dst, s):
        return (
            [(remote(src.at[0], dst.at[1], ssem.at[s + 1], rsem.at[s + 1], to_left), has_left, has_right)],
            [(remote(src.at[1], dst.at[0], ssem.at[s], rsem.at[s], to_right), has_right, has_left)],
        )

    def x_copies(src, dst, s):
        return [
            (remote(src.at[1], dst.at[0], ssem.at[s], rsem.at[s], to_up), None, None),
            (remote(src.at[0], dst.at[1], ssem.at[s + 1], rsem.at[s + 1], to_down), None, None),
        ]

    (y_down, y_up), x_first = y_copies(ys, yr, 0), x_copies(xs, xr, 2)
    (y_down2, y_up2), x_second = y_copies(ys2, yr2, 4), x_copies(xs2, xr2, 6)

    def enter():
        pl.semaphore_wait(barrier, 2 + sum(c.astype(jnp.int32) for c in (has_prev, has_next, has_left)))
        only(has_left, functools.partial(pl.semaphore_signal, above, inc=1, device_id=to_left, device_id_type=MESH))

    pl.when(my_sy == n_sy // 2)(enter)
    waits_long = has_right & (my_sy == n_sy // 2 - 1)
    waits_short = has_right & (my_sy != n_sy // 2 - 1)

    def greet(i, apart, act):
        for side, there, where in ((0, me >= apart, me - apart), (1, me + apart < n_row, me + apart)):
            @pl.when(there)
            def _():
                if act == "signal":
                    pl.semaphore_signal(hello.at[i, 1 - side], inc=1, device_id={"row": where}, device_id_type=MESH)
                else:
                    pl.semaphore_wait(hello.at[i, side], 1)

    def rows(xb):
        return pl.ds(SUB * xb, SUB)

    def spot(z0, xb):
        return depth * (xb % per_group) + z0

    def put(acc, v, z0, parity, xb):
        m = spot(z0, xb)
        at = (parity, xb // per_group)
        acc[at] = jnp.where(pair[parity] == m >> 1, pltpu.roll(v, m, 1), acc[at])

    def fresh():
        return {(p, g): zero for p in (0, 1) for g in range(groups)}

    def faces(acc, g):
        low = jnp.where(is_even, acc[0, g], acc[1, g])
        high = jnp.where(is_even, acc[1, g], acc[0, g])
        return low, pltpu.roll(high, 1, 1)

    load_c.wait()
    c0, c1, c2 = 0.5 * coef[0], 0.5 * coef[1], 0.5 * coef[2]

    def conduct(lb):
        return jnp.where(lb == 0, c0, jnp.where(lb == 1, c1, c2))

    def pack_first(j, carry):
        au, ad = [dict(c) for c in carry]
        for copy in load(j):
            copy.wait()
        for i in range(SUB):
            z0 = SUB * j + i
            for xb in range(blocks):
                v = u[z0 + 1, rows(xb), :]
                dv = conduct(lab[z0 + 1, rows(xb), :])
                d[z0 + 1, rows(xb), :] = dv
                put(au, v, z0, i % 2, xb)
                put(ad, dv, z0, i % 2, xb)
        return au, ad

    au, ad = lax.fori_loop(0, chunks, pack_first, (fresh(), fresh()))
    for g in range(groups):
        at = pl.ds(SUB * g, SUB)
        ys[0, 0, at, :], ys[1, 0, at, :] = faces(au, g)
        ys[0, 1, at, :], ys[1, 1, at, :] = faces(ad, g)
    pl.when(my_sy != n_sy // 2)(enter)
    start(y_down)

    def meet_above(cond):
        @pl.when(cond)
        def _():
            pl.semaphore_wait(above, 1)
            for copy, _, _ in y_up:
                copy.start()

    meet_above(waits_short)

    def edge(ref, first, k, side):
        flat = ref.reshape(ref.shape[0] * wide, LANES)
        got = None
        for i in range(SUB):
            row = flat[pl.ds((first + SUB * k + i) * wide + (wide - 1) * side, SUB, stride=0), :]
            got = row if got is None else jnp.where(sub == i, row, got)
        return got

    for side in (0, 1):
        for k in range(chunks):
            for i, a in enumerate((u, d)):
                xs[side, i, pl.ds(SUB * k, SUB), :] = edge(a, 1, k, side)

    start(x_first)
    for p in range(PARTS):
        start(z_first(p))

    def flux(da, db, ub, ua):
        return (da + db) * (ub - ua)

    def plane(src, dst, shift, z, fz, high, first_step):
        nf, before = [], None
        for xb in range(blocks):
            a, k = src[z, rows(xb), :], d[z, rows(xb), :]
            if xb < blocks - 1:
                at = pl.ds(SUB * xb + 1, SUB)
                fxx = flux(k, d[z, at, :], src[z, at, :], a)
            else:
                fxx = flux(k, pltpu.roll(k, SUB - 1, 0), pltpu.roll(a, SUB - 1, 0), a)
                fxx = jnp.where(sub == SUB - 1, 0.0, fxx)
            turned = pltpu.roll(fxx, 1, 0)
            behind = jnp.where(sub == 0, 0.0 if before is None else before, turned)
            before = turned
            if first_step:
                kk = k + pltpu.roll(k, LANES - 1, 1)
                ky[z - 1, rows(xb), :] = kk
            else:
                kk = ky[z - 1, rows(xb), :]
            gy = kk * (pltpu.roll(a, LANES - 1, 1) - a)
            fy[z - 1, rows(xb), :] = gy
            total = (fxx - behind) + gy
            if high:
                nz = flux(k, d[z + 1, rows(xb), :], src[z + 1, rows(xb), :], a)
                total = total + (nz if fz is None else nz - fz[xb])
                nf.append(nz)
            elif fz is not None:
                total = total - fz[xb]
            dst[z + shift, rows(xb), :] = a + total
        return tuple(nf)

    def between(src, z):
        return tuple(
            flux(d[z, rows(xb), :], d[z + 1, rows(xb), :], src[z + 1, rows(xb), :], src[z, rows(xb), :])
            for xb in range(blocks)
        )

    def planes(src, dst, shift, begin, count, fz, first_step):
        def several(j, fz):
            for i in range(FLUX):
                fz = plane(src, dst, shift, begin + FLUX * j + i, fz, True, first_step)
            return fz

        return lax.fori_loop(0, count // FLUX, several, fz)

    fz = plane(u, h, 0, 1, None, True, True)
    fz = planes(u, h, 0, 2, depth - FLUX, fz, True)
    for z in range(depth - FLUX + 2, last):
        fz = plane(u, h, 0, z, fz, True, True)
    plane(u, h, 0, last, fz, False, True)

    def settle(dst, shift):
        def some(j, carry):
            for i in range(FLUX):
                z0 = FLUX * j + i
                for xb in range(blocks):
                    dst[z0 + shift, rows(xb), :] = dst[z0 + shift, rows(xb), :] - pltpu.roll(fy[z0, rows(xb), :], 1, 1)
            return carry

        lax.fori_loop(0, depth // FLUX, some, 0)

    def sweep(first, trips, count, body, carry):
        def some(j, carry):
            for i in range(count):
                carry = body(count * j + first + i, carry, (first + i) % 2)
            return carry

        return lax.fori_loop(0, trips, some, carry)

    settle(h, 1)

    def pack_h(z0, acc, parity, which=range(blocks)):
        acc = dict(acc)
        for xb in which:
            put(acc, h[z0 + 1, rows(xb), :], z0, parity, xb)
        return acc

    acc = dict(sweep(0, depth // PACK, PACK, pack_h, fresh()))
    meet_above(waits_long)

    def x_faces(own, came):
        for side in (0, 1):
            for k in range(chunks):
                at = pl.ds(SUB * k, SUB)
                fx[side, at, :] = flux(xs[side, 1, at, :], xr[side, 1, at, :], came(side, at), own(side, at))

    def y_faces(own, came, with_high=True):
        even, odd, highs = [], [], []
        for g in range(groups):
            at = pl.ds(SUB * g, SUB)
            dl, dr, ul, ur = ys[0, 1, at, :], ys[1, 1, at, :], own(0, at), own(1, at)
            closed = flux(dl, dr, ul, ur)
            a = flux(dl, yr[0, 1, at, :], came(0, at), ul) + closed
            b = zero - closed
            if with_high:
                high = flux(dr, yr[1, 1, at, :], came(1, at), ur)
                highs.append(high)
                b = b + high
            b = pltpu.roll(b, LANES - 1, 1)
            even.append(jnp.where(is_even, a, b))
            odd.append(jnp.where(is_even, b, a))
        return (even, odd), highs

    def with_faces(v, packed, z0, parity, xb):
        r = pltpu.roll(packed[parity][xb // per_group], (LANES - spot(z0, xb)) & (LANES - 1), 1)
        v = jnp.where(at_ends, v + r, v)
        if xb == 0:
            v = jnp.where(sub == 0, v + fx[0, pl.ds(z0, SUB, stride=0), :], v)
        if xb == blocks - 1:
            v = jnp.where(sub == SUB - 1, v + fx[1, pl.ds(z0, SUB, stride=0), :], v)
        return v

    own_y, came_y = lambda s, at: ys[s, 0, at, :], lambda s, at: yr[s, 0, at, :]
    arrive(x_first)
    x_faces(lambda s, at: xs[s, 0, at, :], lambda s, at: xr[s, 0, at, :])
    arrive(y_up)
    packed, _ = y_faces(own_y, came_y, with_high=False)

    outer = ((0, 0, 0), (depth - 1, depth + 1, 1))
    brims = (0, blocks - 1)

    for p in (0, 1):
        for g in range(groups):
            acc[p, g] = acc[p, g] + packed[p][g]

    def pack_brims(z0, acc, parity):
        acc = dict(acc)
        for xb in brims:
            put(acc, with_faces(h[z0 + 1, rows(xb), :], packed, z0, parity, xb), z0, parity, xb)
        return acc

    acc = dict(sweep(1, 3, 10, pack_brims, acc))
    for p in range(PARTS):
        arrive(z_first(p))
    for (z0, ghost, parity), inside in zip(outer, (has_prev, has_next)):
        for xb in range(blocks):
            at = rows(xb)
            dg = jnp.where(inside, conduct(lab[ghost, at, :]), 0.0)
            d[ghost, at, :] = dg
            v = h[z0 + 1, at, :] + flux(d[z0 + 1, at, :], dg, u[ghost, at, :], u[z0 + 1, at, :])
            h[z0 + 1, at, :] = v
            put(acc, with_faces(v, packed, z0, parity, xb), z0, parity, xb)
    ends = [faces(acc, g) for g in range(groups)]
    for g in range(groups):
        ys2[0, pl.ds(SUB * g, SUB), :] = ends[g][0]
    start(y_down2)

    arrive(y_down)
    packed, highs = y_faces(own_y, came_y)
    for g in range(groups):
        ys2[1, pl.ds(SUB * g, SUB), :] = ends[g][1] + highs[g]
    start(y_up2)

    def fix_h(which):
        def body(z0, carry, parity):
            for xb in which:
                h[z0 + 1, rows(xb), :] = with_faces(h[z0 + 1, rows(xb), :], packed, z0, parity, xb)
            return carry

        return body

    for z0, _, parity in outer:
        fix_h(range(blocks))(z0, 0, parity)
    for p in range(PARTS):
        start(z_second(p))
    greet(0, 2, "signal")
    sweep(1, 3, 10, fix_h(brims), 0)
    for side in (0, 1):
        for k in range(chunks):
            xs2[side, pl.ds(SUB * k, SUB), :] = edge(h, 1, k, side)
    start(x_second)
    sweep(1, 5, 6, fix_h(range(1, blocks - 1)), 0)
    greet(0, 2, "wait")
    greet(1, 4, "signal")

    fz = plane(h, f, -1, 1, None, True, False)
    fz = planes(h, f, -1, 2, depth - FLUX, fz, False)
    for z in range(depth - FLUX + 2, last):
        fz = plane(h, f, -1, z, fz, True, False)
    plane(h, f, -1, last, fz, False, False)
    settle(f, 0)

    load_k.wait()
    scale = 0.5 / (depth * n_row)
    k0, k1, k2 = thick[0] * scale, thick[1] * scale, thick[2] * scale

    def opaque(v, lb):
        first, second = lb == 0, lb == 1
        half = jnp.where(first, k0, jnp.where(second, k1, k2))
        return half + half * jnp.tanh(0.5 * v), first, second

    arrive(x_second)
    x_faces(lambda s, at: xs2[s, at, :], lambda s, at: xr2[s, at, :])

    def brims_f(z0, carry, parity):
        for xb, side, at_row in ((0, 0, 0), (blocks - 1, 1, SUB - 1)):
            v = f[z0, rows(xb), :]
            f[z0, rows(xb), :] = jnp.where(sub == at_row, v + fx[side, pl.ds(z0, SUB, stride=0), :], v)
        return carry

    sweep(0, depth // SUB, SUB, brims_f, 0)
    for p in range(PARTS):
        arrive(z_second(p))
    arrive(y_up2)
    arrive(y_down2)
    packed2, _ = y_faces(lambda s, at: ys2[s, at, :], lambda s, at: yr2[s, at, :])
    for p in (0, 1):
        for g in range(groups):
            turn[p, pl.ds(SUB * g, SUB), :] = packed2[p][g]
    load_p.wait()

    def hand(o):
        dest = lax.rem(me + o, n_row)
        return pltpu.make_async_remote_copy(
            src_ref=ib.at[dest], dst_ref=rb.at[me], send_sem=asem.at[o], recv_sem=bsem.at[me],
            device_id={"row": dest}, device_id_type=MESH,
        )

    def march(dests):
        places = []
        for dest in dests:
            at = pl.ds(pl.multiple_of(dest * SUB, SUB), SUB)
            group = pl.ds(pl.multiple_of(dest // per_group * SUB, SUB), SUB)
            sides = [turn[parity, group, :] for parity in (0, 1)]
            places.append((at, sides, LANES - lax.rem(dest, per_group) * depth))

        def warm(chunk):
            got = {}
            for z0 in chunk:
                for i, (at, sides, m) in enumerate(places):
                    v = f[z0, at, :]
                    for edge_z, ghost in ((0, 0), (depth - 1, depth + 1)):
                        if z0 == edge_z:
                            v = v + flux(d[z0 + 1, at, :], d[ghost, at, :], h[ghost, at, :], h[z0 + 1, at, :])
                    got[z0, i] = jnp.where(at_ends, v + pltpu.roll(sides[z0 % 2], (m - z0) & (LANES - 1), 1), v)
            return got

        states = [(None, zero, zero)] * len(dests)
        steps = [range(k, k + MARCH) for k in range(0, depth, MARCH)]
        ahead = warm(steps[0])
        for k, chunk in enumerate(steps):
            now, ahead = ahead, warm(steps[k + 1]) if k + 1 < len(steps) else None
            for (z0, i), v in now.items():
                f[z0, places[i][0], :] = v
            for (z0, i), v in now.items():
                through, w0, w1 = states[i]
                w, first, second = opaque(v, lab[z0 + 1, places[i][0], :])
                if through is None:
                    through = 1.0 - w
                else:
                    w = through * w
                    through = through - w
                w0 = w0 + jnp.where(first, w, 0.0)
                w1 = w1 + jnp.where(second, w, 0.0)
                states[i] = (through, w0, w1)
        for dest, (through, w0, w1) in zip(dests, states):
            ib[dest, 0] = w0
            ib[dest, 1] = w1
            ib[dest, 2] = through

    greet(1, 4, "wait")
    half = n_row // 2
    order = [half + 1, half - 1, half] + [o for k in range(1, half - 1) for o in (n_row - k, k)] + [0]
    for k in range(0, n_row, 2):
        march([lax.rem(me + o, n_row) for o in order[k : k + 2]])
        for o in order[k : k + 2]:
            if o:
                hand(o).start()
    rb[me] = ib[me]

    through, w0, w1 = one, zero, zero
    for s in range(n_row):
        @pl.when(me != s)
        def _():
            pltpu.make_async_remote_copy(
                src_ref=ib.at[s], dst_ref=rb.at[s], send_sem=asem.at[0], recv_sem=bsem.at[s],
                device_id={"row": s}, device_id_type=MESH,
            ).wait_recv()

        w0 = w0 + through * rb[s, 0]
        w1 = w1 + through * rb[s, 1]
        through = through * rb[s, 2]
    blocked = 1.0 - through
    w2 = (blocked - w0) - w1
    for c in range(3):
        pic_ref[c] = w0 * tint[0, c] + w1 * tint[1, c] + w2 * tint[2, c]
    pic_ref[3] = blocked

    for o in range(1, n_row):
        hand(o).wait_send()
    for p in range(PARTS):
        left_here(z_first(p))
        left_here(z_second(p))
    for copies in (y_down, y_up, x_first, y_down2, y_up2, x_second):
        left_here(copies)


def deliver(f, pic, out, out_pic, sem):
    a = pltpu.make_async_copy(f, out, sem.at[0])
    b = pltpu.make_async_copy(pic, out_pic, sem.at[1])
    a.start()
    b.start()
    a.wait()
    b.wait()


def solution(mesh):
    sizes = (mesh.shape["sx"], mesh.shape["sy"], mesh.shape["row"])
    n_row = sizes[2]

    def per_device(thermal_state, substance_label, thermal_coefficients, optical_thickness, substance_colours):
        depth, wide, tall = thermal_state.shape
        f32 = jnp.float32
        side = depth * wide // LANES
        near = pl.BlockSpec(memory_space=pltpu.VMEM)
        anywhere = pl.BlockSpec(memory_space=pl.ANY)
        chunks = depth // SUB
        results = (
            jax.ShapeDtypeStruct((depth, wide, tall), f32),
            jax.ShapeDtypeStruct((4, wide // n_row, tall), f32),
        )
        f, pic = pl.pallas_call(
            functools.partial(kernel, sizes),
            out_shape=results,
            in_specs=[anywhere] * 5,
            out_specs=(near, near),
            scratch_shapes=[
                pltpu.VMEM((depth + 2, wide, tall), f32),
                pltpu.VMEM((depth + 2, wide, tall), f32),
                pltpu.VMEM((depth + 2, wide, tall), f32),
                pltpu.VMEM((depth, wide, tall), f32),
                pltpu.VMEM((depth, wide, tall), f32),
                pltpu.VMEM((depth + 2, wide, tall), jnp.int32),
                pltpu.VMEM((2, 2, depth, tall), f32),
                pltpu.VMEM((2, 2, depth, tall), f32),
                pltpu.VMEM((2, depth, tall), f32),
                pltpu.VMEM((2, depth, tall), f32),
                pltpu.VMEM((2, depth + SUB, tall), f32),
                pltpu.VMEM((2, 2, side, tall), f32),
                pltpu.VMEM((2, 2, side, tall), f32),
                pltpu.VMEM((2, side, tall), f32),
                pltpu.VMEM((2, side, tall), f32),
                pltpu.VMEM((2, side, tall), f32),
                pltpu.VMEM((n_row, 3, wide // n_row, tall), f32),
                pltpu.VMEM((n_row, 3, wide // n_row, tall), f32),
                pltpu.SMEM((3,), f32),
                pltpu.SMEM((3,), f32),
                pltpu.SMEM((3, 3), f32),
                pltpu.SemaphoreType.DMA((2, chunks)),
                pltpu.SemaphoreType.DMA((3,)),
                pltpu.SemaphoreType.DMA((2, 2, PARTS)),
                pltpu.SemaphoreType.DMA((2, 2, PARTS)),
                pltpu.SemaphoreType.DMA((2, PARTS)),
                pltpu.SemaphoreType.DMA((2, PARTS)),
                pltpu.SemaphoreType.DMA((8,)),
                pltpu.SemaphoreType.DMA((8,)),
                pltpu.SemaphoreType.DMA((n_row,)),
                pltpu.SemaphoreType.DMA((n_row,)),
                pltpu.SemaphoreType.REGULAR((2, 2)),
                pltpu.SemaphoreType.REGULAR,
            ],
            compiler_params=pltpu.CompilerParams(
                collective_id=0, has_side_effects=True, vmem_limit_bytes=VMEM_LIMIT
            ),
        )(*[
            pltpu.with_memory_space_constraint(a, pltpu.HBM)
            for a in (thermal_state, substance_label, thermal_coefficients, optical_thickness, substance_colours)
        ])
        return pl.pallas_call(
            deliver,
            out_shape=results,
            in_specs=[near, near],
            out_specs=(anywhere, anywhere),
            scratch_shapes=[pltpu.SemaphoreType.DMA((2,))],
            compiler_params=pltpu.CompilerParams(vmem_limit_bytes=VMEM_LIMIT),
        )(f, pic)

    placed = (P("row", "sx", "sy"), P("row", "sx", "sy"), P(), P(), P())
    return jax.shard_map(
        per_device,
        mesh=mesh,
        in_specs=placed,
        out_specs=(P("row", "sx", "sy"), P(None, ("sx", "row"), "sy")),
        check_vma=False,
    )
```
